128 devices in a mesh: ens: 4 (over z_hi, core), elem: 32 (over y, z_lo, x).
Axes of the slice: x: 4, y: 4, z: 4 (z_hi: 2, z_lo: 2; z = z_hi * 2 + z_lo), core: 2. Of those that a mesh axis runs over, the one named last changes fastest.
Arguments:
- scalars: float32 [8, 512, 4096], P('ens', None, 'elem'), parts along dimension 0, may hold values from -6 to 6
- transport: float32 [3, 512, 4096], P(None, None, 'elem'), may hold values from -6 to 6
- mass: float32 [512, 4096], P(None, 'elem'), may hold values from 0.5 to 2
- element_order: int32 [32, 128], P('elem'), may hold values from 0 to 127, each once within a row
Outputs:
- advected: float32 [8, 512, 4096], P('ens', None, 'elem'), parts along dimension 0
The draws below stay inside these ranges and needn't reach their ends.
There are 4 independent parts, one for each index of `ens`. The reference program is written for one: setup_inputs(seed, part) draws one part's arguments, and reference() takes and returns one part's arrays. A program takes and returns all parts, laid end to end along the dimension named above; an argument that names none is the same for every part. Nothing has to cross between parts.
Inputs may be any that keep to these rules, and one draw needn't show every extreme that they name: `element_order`: each row is a permutation of the device's slots.
All inputs are finite; a program needn't handle non-finite values.
Results may differ from the reference program's by a relative error of at most 0.0001.
Values sent between devices are 32-bit elements; how exact they have to be, the bound alone decides.
No kernel may reach another device: no remote copies, remote signals or barrier semaphores. Data moves between devices by JAX's collectives and lax.ppermute only.
A program may use at most 64 MiB of HBM per device.

```python
import math
import jax
import jax.numpy as jnp
import numpy as np
from jax import lax

ORDER = 7
NODES = 512
MEMB = 2
SUBSTEPS = 2
EX = 1
EY = 8
EZ = 16
E_DEV = 128
ELEMS = 4096
N_ELEM = 32


def block_levels(own_key, shape, cuts, smallest, largest):
    level, own = 1.0, jax.random.fold_in(own_key, 6)
    for dim, blocks in cuts:
        heights = jnp.exp(jax.random.uniform(jax.random.fold_in(own, dim), (blocks,), jnp.float32, smallest / len(cuts), largest / len(cuts)))
        level = level * jnp.repeat(heights, shape[dim] // blocks).reshape([-1 if axis == dim else 1 for axis in range(len(shape))])
    return level


def bell_draw(own_key, shape, deviation, most, split=(), held_as=jnp.bfloat16):
    result = deviation * jax.random.normal(own_key, shape, jnp.float32)
    if split:
        result = result * block_levels(own_key, shape, split, -0.22, 0.18)
    return jnp.clip(result, -most, most).astype(held_as)


def setup_inputs(seed: int = 0, part: int = 0) -> dict:
    key_list = jax.random.split(jax.random.key(seed), 5)
    part_keys = jax.random.split(jax.random.fold_in(key_list[4], part), 5)
    scalars = bell_draw(part_keys[0], (MEMB, NODES, ELEMS), 1.0, 6.0, ((2, 32),), jnp.float32)
    transport = bell_draw(key_list[1], (3, NODES, ELEMS), 1.0, 6.0, ((2, 32),), jnp.float32)
    mass = jnp.clip(jnp.exp(math.log(2.0) - 1.3862944 * jax.random.uniform(key_list[2], (NODES, ELEMS), jnp.float32) ** block_levels(key_list[2], (NODES, ELEMS), ((1, 32),), -0.2, 0.2)), 0.5, 2.0)
    element_order = jax.vmap(lambda own: jax.random.permutation(own, E_DEV))(jax.random.split(key_list[3], N_ELEM)).reshape((N_ELEM, E_DEV)).astype(jnp.int32)
    return {"scalars": scalars, "transport": transport, "mass": mass, "element_order": element_order}


time_step = 0.015


def legendre_table(points, degree):
    table = np.zeros((points.shape[0], degree + 1))
    table[:, 0] = 1.0
    table[:, 1] = points
    for level in range(2, degree + 1):
        table[:, level] = ((2 * level - 1) * points * table[:, level - 1] - (level - 1) * table[:, level - 2]) / level
    return table


def gll_derivative(degree):
    extent = degree + 1
    points = np.cos(np.pi * np.arange(extent) / degree)
    for sweep in range(60):
        table = legendre_table(points, degree)
        points = points - (points * table[:, degree] - table[:, degree - 1]) / (extent * table[:, degree])
    points = points[::-1].copy()
    values = legendre_table(points, degree)[:, degree]
    matrix = np.zeros((extent, extent))
    for target in range(extent):
        for source in range(extent):
            if target != source:
                matrix[target, source] = values[target] / (values[source] * (points[target] - points[source]))
    matrix[0, 0] = -degree * (degree + 1) / 4.0
    matrix[extent - 1, extent - 1] = degree * (degree + 1) / 4.0
    return matrix


def assemble(field):
    last = ORDER
    upper = field[..., last, :, :, :, :, :] + jnp.roll(field[..., 0, :, :, :, :, :], -1, axis=-3)
    field = field.at[..., last, :, :, :, :, :].set(upper).at[..., 0, :, :, :, :, :].set(jnp.roll(upper, 1, axis=-3))
    upper = field[..., last, :, :, :, :] + jnp.roll(field[..., 0, :, :, :, :], -1, axis=-2)
    field = field.at[..., last, :, :, :, :].set(upper).at[..., 0, :, :, :, :].set(jnp.roll(upper, 1, axis=-2))
    upper = field[..., last, :, :, :] + jnp.roll(field[..., 0, :, :, :], -1, axis=-1)
    field = field.at[..., last, :, :, :].set(upper).at[..., 0, :, :, :].set(jnp.roll(upper, 1, axis=-1))
    return field


def reference(scalars, transport, mass, element_order):
    extent = ORDER + 1
    derivative = jnp.asarray(gll_derivative(ORDER), jnp.float32)
    highest = lax.Precision.HIGHEST
    position = (jnp.arange(N_ELEM, dtype=jnp.int32)[:, None] * E_DEV + element_order.astype(jnp.int32)).reshape(-1)

    def to_brick(values):
        placed = jnp.zeros_like(values).at[..., position].set(values)
        return placed.reshape(values.shape[:-2] + (extent, extent, extent, EX * N_ELEM, EY, EZ))

    field = to_brick(scalars)
    velocity = to_brick(transport)
    weights = to_brick(mass)
    summed = assemble(jnp.concatenate([weights[None] * field, weights[None]], axis=0))
    total_mass = summed[MEMB]
    field = summed[:MEMB] / total_mass

    def tendency(values):
        grad_r = jnp.einsum('ai,...ijkxyz->...ajkxyz', derivative, values, precision=highest)
        grad_s = jnp.einsum('bj,...ijkxyz->...ibkxyz', derivative, values, precision=highest)
        grad_t = jnp.einsum('ck,...ijkxyz->...ijcxyz', derivative, values, precision=highest)
        weighted = velocity[0] * grad_r + velocity[1] * grad_s + velocity[2] * grad_t
        return -assemble(weighted) / total_mass

    for substep in range(SUBSTEPS):
        first_k = tendency(field)
        second_k = tendency(field + 0.5 * time_step * first_k)
        third_k = tendency(field + 0.5 * time_step * second_k)
        fourth_k = tendency(field + time_step * third_k)
        field = field + (time_step / 6.0) * (first_k + 2.0 * second_k + 2.0 * third_k + fourth_k)
    flat = field.reshape(MEMB, NODES, ELEMS)
    return flat[..., position]
```

```python
import jax
import jax.numpy as jnp
import numpy as np
from jax import lax
from jax.experimental import pallas as pl
from jax.experimental.pallas import tpu as pltpu
from jax.sharding import PartitionSpec as P

ORDER = 7
EXT = ORDER + 1
SUBSTEPS = 2
STAGES = 4
EY = 8
EZ = 16
LANES = EY * EZ
SUB = 8

time_step = 0.015


def legendre_table(points, degree):
    table = np.zeros((points.shape[0], degree + 1))
    table[:, 0] = 1.0
    table[:, 1] = points
    for level in range(2, degree + 1):
        table[:, level] = (
            (2 * level - 1) * points * table[:, level - 1] - (level - 1) * table[:, level - 2]
        ) / level
    return table


def gll_derivative(degree):
    extent = degree + 1
    points = np.cos(np.pi * np.arange(extent) / degree)
    for sweep in range(60):
        table = legendre_table(points, degree)
        points = points - (points * table[:, degree] - table[:, degree - 1]) / (
            extent * table[:, degree]
        )
    points = points[::-1].copy()
    values = legendre_table(points, degree)[:, degree]
    matrix = np.zeros((extent, extent))
    for target in range(extent):
        for source in range(extent):
            if target != source:
                matrix[target, source] = values[target] / (
                    values[source] * (points[target] - points[source])
                )
    matrix[0, 0] = -degree * (degree + 1) / 4.0
    matrix[extent - 1, extent - 1] = degree * (degree + 1) / 4.0
    return matrix


DM = gll_derivative(ORDER)
SUM_PART = [[(DM[j, a] + DM[j, 7 - a]) / 2 for a in range(4)] for j in range(4)]
DIF_PART = [[(DM[j, a] - DM[j, 7 - a]) / 2 for a in range(4)] for j in range(4)]
ROT = np.array([[DM[k, (k - r) % 8] for k in range(8)] for r in range(8)], np.float32)


def combine(coefs, items):
    total = None
    for c, x in zip(coefs, items):
        term = x * np.float32(c)
        total = term if total is None else total + term
    return total


def along_second(plane):
    even = [plane[a] + plane[7 - a] for a in range(4)]
    odd = [plane[a] - plane[7 - a] for a in range(4)]
    out = [None] * 8
    for j in range(4):
        e = combine(SUM_PART[j], even)
        o = combine(DIF_PART[j], odd)
        out[j] = o + e
        out[7 - j] = o - e
    return out


def along_third(x, rot):
    total = x * rot[0]
    for r in range(1, 8):
        total = total + pltpu.roll(x, r, 0) * rot[r]
    return total


def gather_lanes(x, idx):
    return jnp.take_along_axis(x, idx, axis=1, mode="promise_in_bounds")


def third_tables():
    lane = lax.broadcasted_iota(jnp.int32, (SUB, LANES), 1)
    k = lax.broadcasted_iota(jnp.int32, (SUB, LANES), 0)
    z = lane % EZ
    back = jnp.where(z == 0, lane + (EZ - 1), lane - 1)
    ahead = jnp.where(z == EZ - 1, lane - (EZ - 1), lane + 1)
    return jnp.where(k == 0, back, ahead), k == 0, k == ORDER


def plane_sum(plane, tables):
    idx, first, last = tables
    up = plane[7] + pltpu.roll(plane[0], LANES - EZ, 1)
    plane = [pltpu.roll(up, EZ, 1)] + list(plane[1:7]) + [up]
    out = []
    for v in plane:
        x = jnp.where(first, pltpu.roll(v, 1, 0), jnp.where(last, pltpu.roll(v, 7, 0), 0.0))
        out.append(v + gather_lanes(x, idx))
    return out


def brick_index(order_ref):
    order = jnp.broadcast_to(order_ref[...], (LANES, LANES))
    pos = lax.broadcasted_iota(jnp.int32, (LANES, LANES), 0)
    hot = jnp.where(order == pos, 1.0, 0.0).astype(jnp.bfloat16)
    slot = lax.broadcasted_iota(jnp.int32, (SUB, LANES), 1).astype(jnp.float32).astype(jnp.bfloat16)
    found = lax.dot_general(
        slot, hot, (((1,), (1,)), ((), ())), preferred_element_type=jnp.float32
    )
    return found.astype(jnp.int32)


def source_plane(parity, i):
    return jnp.where(parity == 1, ORDER - i, i)


def project_faces(order_ref, scal_ref, mass_ref, od_ref, ev_ref):
    parity = lax.axis_index("elem") % 2
    idx = brick_index(order_ref)
    tables = third_tables()
    for face, out in ((0, od_ref), (ORDER, ev_ref)):
        src = source_plane(parity, face)
        weight = [gather_lanes(mass_ref[src, j], idx) for j in range(8)]
        for j, v in enumerate(plane_sum(weight, tables)):
            out[2, j] = v
        for m in range(2):
            plane = [gather_lanes(scal_ref[m, src, j], idx) * weight[j] for j in range(8)]
            for j, v in enumerate(plane_sum(plane, tables)):
                out[m, j] = v


def prepare(order_ref, scal_ref, mass_ref, tr_ref, gi_ref, q_ref, ri_ref, ti_ref, tf_ref):
    parity = lax.axis_index("elem") % 2
    idx = brick_index(order_ref)
    tables = third_tables()
    sign = jnp.where(parity == 1, time_step, -time_step).astype(jnp.float32)

    for face in range(2):
        src = source_plane(parity, face * ORDER)
        for j in range(8):
            tf_ref[face, 0, j] = gather_lanes(tr_ref[0, src, j], idx) * sign
            tf_ref[face, 1, j] = gather_lanes(tr_ref[1, src, j], idx) * np.float32(-time_step)
            tf_ref[face, 2, j] = gather_lanes(tr_ref[2, src, j], idx) * np.float32(-time_step)

    def body(i, carry):
        src = source_plane(parity, i + 1)
        for j in range(8):
            ti_ref[i, 0, j] = gather_lanes(tr_ref[0, src, j], idx) * sign
            ti_ref[i, 1, j] = gather_lanes(tr_ref[1, src, j], idx) * np.float32(-time_step)
            ti_ref[i, 2, j] = gather_lanes(tr_ref[2, src, j], idx) * np.float32(-time_step)
        weight = [gather_lanes(mass_ref[src, j], idx) for j in range(8)]
        inverse = [1.0 / v for v in plane_sum(weight, tables)]
        for j in range(8):
            ri_ref[i, j] = inverse[j]
        for m in range(2):
            plane = [gather_lanes(scal_ref[m, src, j], idx) * weight[j] for j in range(8)]
            plane = plane_sum(plane, tables)
            for j in range(8):
                gi_ref[m, i, j] = plane[j] * inverse[j]
        return carry

    lax.fori_loop(0, 6, body, 0)
    face_partials(gi_ref, q_ref)


def face_partials(gi_ref, q_ref):
    for face in range(2):
        coefs = DM[face * ORDER, 1:7]
        for m in range(2):
            for j in range(8):
                q_ref[face, m, j] = combine(coefs, [gi_ref[m, i, j] for i in range(6)])


def face_terms(p, q_ref, tf_ref, rot, tables, outs):
    for face in range(2):
        out = outs[face]
        for m in range(2):
            mine = p[face][m]
            second = along_second(mine)
            plane = []
            for j in range(8):
                first = (
                    q_ref[face, m, j]
                    + p[0][m][j] * np.float32(DM[face * ORDER, 0])
                    + p[1][m][j] * np.float32(DM[face * ORDER, ORDER])
                )
                third = along_third(mine[j], rot)
                plane.append(
                    tf_ref[face, 0, j] * first
                    + tf_ref[face, 1, j] * second[j]
                    + tf_ref[face, 2, j] * third
                )
            for j, v in enumerate(plane_sum(plane, tables)):
                out[m, j] = v


def start_faces(od_ref, ev_ref, rod_ref, rev_ref, q_ref, tf_ref, rot_ref,
                p_ref, rf_ref, sod_ref, sev_ref):
    rot = [rot_ref[r] for r in range(8)]
    tables = third_tables()
    p = []
    for face, (own, got) in enumerate(((od_ref, rod_ref), (ev_ref, rev_ref))):
        inverse = [1.0 / (own[2, j] + got[2, j]) for j in range(8)]
        for j in range(8):
            rf_ref[face, j] = inverse[j]
        p.append([[(own[m, j] + got[m, j]) * inverse[j] for j in range(8)] for m in range(2)])
        for m in range(2):
            for j in range(8):
                p_ref[face, m, j] = p[face][m][j]
    face_terms(p, q_ref, tf_ref, rot, tables, (sod_ref, sev_ref))


def make_stage_faces(scale, total):
    def stage_faces(od_ref, ev_ref, rod_ref, rev_ref, rf_ref, accf_ref, q_ref, tf_ref, rot_ref,
                    p_ref, sod_ref, sev_ref):
        rot = [rot_ref[r] for r in range(8)]
        tables = third_tables()
        p = []
        for face, (own, got) in enumerate(((od_ref, rod_ref), (ev_ref, rev_ref))):
            rows = []
            for m in range(2):
                row = [
                    (own[m, j] + got[m, j]) * (rf_ref[face, j] * np.float32(scale))
                    for j in range(8)
                ]
                if total:
                    row = [row[j] + accf_ref[face, m, j] for j in range(8)]
                rows.append(row)
                for j in range(8):
                    p_ref[face, m, j] = row[j]
            p.append(rows)
        face_terms(p, q_ref, tf_ref, rot, tables, (sod_ref, sev_ref))

    return stage_faces


def make_stage_inner(scale, opening, closing):
    def stage_inner(p_ref, gi_ref, acci_ref, accf_ref, ri_ref, ti_ref, rot_ref, d_ref,
                    gn_ref, q_ref, an_ref, afn_ref):
        rot = [rot_ref[r] for r in range(8)]
        tables = third_tables()

        def body(i, carry):
            row = [d_ref[i + 1, a] for a in range(8)]
            for m in range(2):
                mine = [gi_ref[m, i, j] for j in range(8)]
                second = along_second(mine)
                plane = []
                for j in range(8):
                    first = p_ref[0, m, j] * row[0] + p_ref[1, m, j] * row[7]
                    for a in range(6):
                        first = first + gi_ref[m, a, j] * row[a + 1]
                    third = along_third(mine[j], rot)
                    plane.append(
                        ti_ref[i, 0, j] * first
                        + ti_ref[i, 1, j] * second[j]
                        + ti_ref[i, 2, j] * third
                    )
                plane = plane_sum(plane, tables)
                for j in range(8):
                    value = plane[j] * (ri_ref[i, j] * np.float32(scale))
                    total = (mine[j] if opening else acci_ref[m, i, j]) + value
                    gn_ref[m, i, j] = total if closing else value
                    if not closing:
                        an_ref[m, i, j] = total
            return carry

        lax.fori_loop(0, 6, body, 0)
        face_partials(gn_ref, q_ref)
        for face in range(2):
            for m in range(2):
                for j in range(8):
                    value = p_ref[face, m, j]
                    afn_ref[face, m, j] = value if opening else value + accf_ref[face, m, j]

    return stage_inner


def make_finish(scale):
    def finish(order_ref, od_ref, ev_ref, rod_ref, rev_ref, rf_ref, accf_ref, gi_ref, out_ref):
        parity = lax.axis_index("elem") % 2
        idx = jnp.broadcast_to(order_ref[...], (SUB, LANES))
        for face, (own, got) in enumerate(((od_ref, rod_ref), (ev_ref, rev_ref))):
            dst = source_plane(parity, face * ORDER)
            for m in range(2):
                for j in range(8):
                    value = (own[m, j] + got[m, j]) * (rf_ref[face, j] * np.float32(scale))
                    out_ref[m, dst, j] = gather_lanes(value + accf_ref[face, m, j], idx)
        for i in range(6):
            dst = source_plane(parity, i + 1)
            for m in range(2):
                for j in range(8):
                    out_ref[m, dst, j] = gather_lanes(gi_ref[m, i, j], idx)

    return finish


VM = pl.BlockSpec(memory_space=pltpu.VMEM)
SM = pl.BlockSpec(memory_space=pltpu.SMEM)


def call(kernel, outs, args, name, cost, smem_last=False):
    specs = [VM] * len(args)
    if smem_last:
        specs[-1] = SM
    shapes = [jax.ShapeDtypeStruct(s, jnp.float32) for s in outs]
    return pl.pallas_call(
        kernel,
        out_shape=shapes if len(shapes) > 1 else shapes[0],
        in_specs=specs,
        out_specs=[VM] * len(shapes) if len(shapes) > 1 else VM,
        name=name,
        compiler_params=pltpu.CompilerParams(vmem_limit_bytes=8 << 20),
        cost_estimate=pl.CostEstimate(flops=cost * 1000000, bytes_accessed=1 << 20, transcendentals=0),
    )(*args)


def per_device(scalars, transport, mass, element_order):
    count = lax.axis_size("elem")
    even_pairs = [(i, i ^ 1) for i in range(count)]
    odd_pairs = [(i, (i + 1) % count if i % 2 else (i - 1) % count) for i in range(count)]
    swap_od = lambda x: lax.ppermute(x, "elem", odd_pairs)
    swap_ev = lambda x: lax.ppermute(x, "elem", even_pairs)
    rot = jnp.asarray(np.broadcast_to(ROT[:, :, None], (8, SUB, LANES)))
    dmat = jnp.asarray(DM, jnp.float32)
    members = scalars.shape[0]
    grid = (EXT, EXT, SUB, LANES)
    scal = scalars.reshape((members,) + grid)
    tr = transport.reshape((3,) + grid)
    mas = mass.reshape(grid)
    tile = (EXT, SUB, LANES)

    od, ev = call(project_faces, [(3,) + tile] * 2, (element_order, scal, mas), "project", 1)
    rod, rev = swap_od(od), swap_ev(ev)
    gi, q, ri, ti, tf = call(
        prepare,
        [(2, 6) + tile, (2, 2) + tile, (6,) + tile, (6, 3) + tile, (2, 3) + tile],
        (element_order, scal, mas, tr), "prepare", 4000)
    p, rf, od, ev = call(
        start_faces, [(2, 2) + tile, (2,) + tile, (2,) + tile, (2,) + tile],
        (od, ev, rod, rev, q, tf, rot), "faces", 1)
    acci, accf = gi, p
    last = SUBSTEPS * STAGES
    for n in range(1, last + 1):
        s = (n - 1) % STAGES + 1
        rod, rev = swap_od(od), swap_ev(ev)
        gi, q, acci, accf = call(
            make_stage_inner(1.0 / s, s == 1, s == STAGES),
            [(2, 6) + tile, (2, 2) + tile, (2, 6) + tile, (2, 2) + tile],
            (p, gi, acci, accf, ri, ti, rot, dmat), "inner", 4000, smem_last=True)
        if n < last:
            p, od, ev = call(
                make_stage_faces(1.0 / s, s == STAGES),
                [(2, 2) + tile, (2,) + tile, (2,) + tile],
                (od, ev, rod, rev, rf, accf, q, tf, rot), "faces", 1)
    out = call(
        make_finish(1.0 / STAGES), [(members,) + grid],
        (element_order, od, ev, rod, rev, rf, accf, gi), "finish", 1)
    return out.reshape(scalars.shape)


def solution(mesh):
    in_specs = (P("ens", None, "elem"), P(None, None, "elem"), P(None, "elem"), P("elem", None))
    out_specs = P("ens", None, "elem")
    return jax.shard_map(
        per_device, mesh=mesh, in_specs=in_specs, out_specs=out_specs, check_vma=False
    )
```

```python
import jax
import jax.numpy as jnp
import numpy as np
from jax import lax
from jax.experimental import pallas as pl
from jax.experimental.pallas import tpu as pltpu
from jax.sharding import PartitionSpec as P

ORDER = 7
EXT = ORDER + 1
SUBSTEPS = 2
STAGES = 4
EY = 8
EZ = 16
LANES = EY * EZ
SUB = 8

time_step = 0.015


def legendre_table(points, degree):
    table = np.zeros((points.shape[0], degree + 1))
    table[:, 0] = 1.0
    table[:, 1] = points
    for level in range(2, degree + 1):
        table[:, level] = (
            (2 * level - 1) * points * table[:, level - 1] - (level - 1) * table[:, level - 2]
        ) / level
    return table


def gll_derivative(degree):
    extent = degree + 1
    points = np.cos(np.pi * np.arange(extent) / degree)
    for sweep in range(60):
        table = legendre_table(points, degree)
        points = points - (points * table[:, degree] - table[:, degree - 1]) / (
            extent * table[:, degree]
        )
    points = points[::-1].copy()
    values = legendre_table(points, degree)[:, degree]
    matrix = np.zeros((extent, extent))
    for target in range(extent):
        for source in range(extent):
            if target != source:
                matrix[target, source] = values[target] / (
                    values[source] * (points[target] - points[source])
                )
    matrix[0, 0] = -degree * (degree + 1) / 4.0
    matrix[extent - 1, extent - 1] = degree * (degree + 1) / 4.0
    return matrix


DM = gll_derivative(ORDER)
SUM_PART = [[(DM[j, a] + DM[j, 7 - a]) / 2 for a in range(4)] for j in range(4)]
DIF_PART = [[(DM[j, a] - DM[j, 7 - a]) / 2 for a in range(4)] for j in range(4)]
ROT = np.array([[DM[k, (k - r) % 8] for k in range(8)] for r in range(8)], np.float32)


def combine(coefs, items):
    total = None
    for c, x in zip(coefs, items):
        term = x * np.float32(c)
        total = term if total is None else total + term
    return total


def along_second(plane):
    even = [plane[a] + plane[7 - a] for a in range(4)]
    odd = [plane[a] - plane[7 - a] for a in range(4)]
    out = [None] * 8
    for j in range(4):
        e = combine(SUM_PART[j], even)
        o = combine(DIF_PART[j], odd)
        out[j] = o + e
        out[7 - j] = o - e
    return out


def along_third(x, rot):
    total = x * rot[0]
    for r in range(1, 8):
        total = total + pltpu.roll(x, r, 0) * rot[r]
    return total


def gather_lanes(x, idx):
    return jnp.take_along_axis(x, idx, axis=1, mode="promise_in_bounds")


def third_tables():
    lane = lax.broadcasted_iota(jnp.int32, (SUB, LANES), 1)
    k = lax.broadcasted_iota(jnp.int32, (SUB, LANES), 0)
    z = lane % EZ
    back = jnp.where(z == 0, lane + (EZ - 1), lane - 1)
    ahead = jnp.where(z == EZ - 1, lane - (EZ - 1), lane + 1)
    return jnp.where(k == 0, back, ahead), k == 0, k == ORDER


def plane_sum(plane, tables):
    idx, first, last = tables
    up = plane[7] + pltpu.roll(plane[0], LANES - EZ, 1)
    plane = [pltpu.roll(up, EZ, 1)] + list(plane[1:7]) + [up]
    out = []
    for v in plane:
        x = jnp.where(first, pltpu.roll(v, 1, 0), jnp.where(last, pltpu.roll(v, 7, 0), 0.0))
        out.append(v + gather_lanes(x, idx))
    return out


def write(ref, lead, plane):
    for j, v in enumerate(plane):
        ref[lead + (j,)] = v


def read(ref, *lead):
    return [ref[lead + (j,)] for j in range(8)]


def brick_index(order_ref):
    order = jnp.broadcast_to(order_ref[...], (LANES, LANES))
    pos = lax.broadcasted_iota(jnp.int32, (LANES, LANES), 0)
    hot = jnp.where(order == pos, 1.0, 0.0).astype(jnp.bfloat16)
    slot = lax.broadcasted_iota(jnp.int32, (SUB, LANES), 1).astype(jnp.float32).astype(jnp.bfloat16)
    found = lax.dot_general(
        slot, hot, (((1,), (1,)), ((), ())), preferred_element_type=jnp.float32
    )
    return found.astype(jnp.int32)


def source_plane(parity, i):
    return jnp.where(parity == 1, ORDER - i, i)


def source_plane(parity, i):
    return jnp.where(parity == 1, ORDER - i, i)


def project_faces(order_ref, scal_ref, mass_ref, od_ref, ev_ref, order_buf, scal_buf, mass_buf, sems):
    parity = lax.axis_index("elem") % 2
    copies = [pltpu.make_async_copy(order_ref, order_buf, sems.at[6])]
    for face in range(2):
        src = source_plane(parity, face * ORDER)
        copies.append(pltpu.make_async_copy(mass_ref.at[src], mass_buf.at[face], sems.at[face]))
        for m in range(2):
            copies.append(
                pltpu.make_async_copy(
                    scal_ref.at[m, src], scal_buf.at[face, m], sems.at[2 + 2 * face + m]
                )
            )
    for copy in copies:
        copy.start()
    tables = third_tables()
    copies[0].wait()
    idx = brick_index(order_buf)
    for copy in copies[1:]:
        copy.wait()
    for face, out in ((0, od_ref), (1, ev_ref)):
        weight = [gather_lanes(mass_buf[face, j], idx) for j in range(8)]
        write(out, (2,), plane_sum(weight, tables))
        for m in range(2):
            plane = [gather_lanes(scal_buf[face, m, j], idx) * weight[j] for j in range(8)]
            write(out, (m,), plane_sum(plane, tables))


def prepare(order_ref, scal_ref, mass_ref, tr_ref, gi_ref, q_ref, ri_ref, ti_ref, tf_ref):
    parity = lax.axis_index("elem") % 2
    idx = brick_index(order_ref)
    tables = third_tables()
    sign = jnp.where(parity == 1, time_step, -time_step).astype(jnp.float32)
    signs = (sign, np.float32(-time_step), np.float32(-time_step))

    for face in range(2):
        src = source_plane(parity, face * ORDER)
        for r in range(3):
            for j in range(8):
                tf_ref[face, r, j] = gather_lanes(tr_ref[r, src, j], idx) * signs[r]

    def body(i, carry):
        src = source_plane(parity, i + 1)
        for r in range(3):
            for j in range(8):
                ti_ref[i, r, j] = gather_lanes(tr_ref[r, src, j], idx) * signs[r]
        weight = [gather_lanes(mass_ref[src, j], idx) for j in range(8)]
        inverse = [1.0 / v for v in plane_sum(weight, tables)]
        write(ri_ref, (i,), inverse)
        for m in range(2):
            plane = [gather_lanes(scal_ref[m, src, j], idx) * weight[j] for j in range(8)]
            plane = plane_sum(plane, tables)
            write(gi_ref, (m, i), [plane[j] * inverse[j] for j in range(8)])
        return carry

    lax.fori_loop(0, 6, body, 0)
    face_partials(gi_ref, q_ref)


def face_partials(gi_ref, q_ref):
    for m in range(2):
        for j in range(8):
            rows = [gi_ref[m, i, j] for i in range(6)]
            for face in range(2):
                q_ref[face, m, j] = combine(DM[face * ORDER, 1:7], rows)


def in_plane(plane, t_ref, lead, rot):
    second = along_second(plane)
    return [
        t_ref[lead + (1, j)] * second[j] + t_ref[lead + (2, j)] * along_third(plane[j], rot)
        for j in range(8)
    ]


def inner_open(gi_ref, ti_ref, rot, d_ref, wp_ref):
    def body(i, carry):
        row = [d_ref[i + 1, a + 1] for a in range(6)]
        for m in range(2):
            rest = in_plane(read(gi_ref, m, i), ti_ref, (i,), rot)
            for j in range(8):
                first = gi_ref[m, 0, j] * row[0]
                for a in range(1, 6):
                    first = first + gi_ref[m, a, j] * row[a]
                wp_ref[m, i, j] = rest[j] + ti_ref[i, 0, j] * first
        return carry

    lax.fori_loop(0, 6, body, 0)


def inner_close(p0_ref, p7_ref, wp_ref, ri_ref, ti_ref, d_ref, scale, put):
    tables = third_tables()

    def body(i, carry):
        near, far = d_ref[i + 1, 0], d_ref[i + 1, ORDER]
        inverse = [ri_ref[i, j] * np.float32(scale) for j in range(8)]
        for m in range(2):
            plane = [
                wp_ref[m, i, j] + ti_ref[i, 0, j] * (p0_ref[m, j] * near + p7_ref[m, j] * far)
                for j in range(8)
            ]
            plane = plane_sum(plane, tables)
            put(m, i, [plane[j] * inverse[j] for j in range(8)])
        return carry

    lax.fori_loop(0, 6, body, 0)


def rotations(rot_ref):
    return [rot_ref[r] for r in range(8)]


def both_faces(p0, p7, q_ref, tf_ref, rot, tables, sod_ref, sev_ref):
    for face, own, out in ((1, p7, sev_ref), (0, p0, sod_ref)):
        for m in range(2):
            rest = in_plane(own[m], tf_ref, (face,), rot)
            plane = [
                rest[j]
                + tf_ref[face, 0, j]
                * (
                    q_ref[face, m, j]
                    + p0[m][j] * np.float32(DM[face * ORDER, 0])
                    + p7[m][j] * np.float32(DM[face * ORDER, ORDER])
                )
                for j in range(8)
            ]
            write(out, (m,), plane_sum(plane, tables))


def start_faces(od_ref, ev_ref, rod_ref, rev_ref, q_ref, tf_ref, rot_ref,
                p0_ref, p7_ref, rf_ref, sod_ref, sev_ref):
    p = []
    for face, (own, got, out) in enumerate(((od_ref, rod_ref, p0_ref), (ev_ref, rev_ref, p7_ref))):
        inverse = [1.0 / (own[2, j] + got[2, j]) for j in range(8)]
        write(rf_ref, (face,), inverse)
        p.append([[(own[m, j] + got[m, j]) * inverse[j] for j in range(8)] for m in range(2)])
        for m in range(2):
            write(out, (m,), p[face][m])
    both_faces(p[0], p[1], q_ref, tf_ref, rotations(rot_ref), third_tables(), sod_ref, sev_ref)


def shared_terms(p0, t_ref, rot, tables):
    rest = in_plane(p0, t_ref, (), rot)
    plane = [rest[j] + t_ref[0, j] * (p0[j] * np.float32(DM[0, 0])) for j in range(8)]
    return plane_sum(plane, tables)


def make_odd_face(scale, total, early):
    def odd_face(*refs):
        od_ref, rod_ref, e_ref, rf_ref, accf_ref, q_ref, tf_ref, rot_ref = refs[:8]
        p0_ref, w0_ref, w7_ref = refs[8:11]
        rot = rotations(rot_ref)
        tables = third_tables()
        if early:
            ts_ref = refs[11]
            for r in range(3):
                write(ts_ref, (r,), [tf_ref[0, r, j] + rod_ref[2 + r, j] for j in range(8)])
        for m in range(2):
            shared = read(e_ref, m)
            if early:
                shared = shared_terms(shared, ts_ref, rot, tables)
            p0 = [
                (od_ref[m, j] + rod_ref[m, j] + shared[j]) * (rf_ref[0, j] * np.float32(scale))
                for j in range(8)
            ]
            if total:
                p0 = [p0[j] + accf_ref[0, m, j] for j in range(8)]
            write(p0_ref, (m,), p0)
            rest = in_plane(p0, tf_ref, (0,), rot)
            write(w0_ref, (m,), [
                rest[j] + tf_ref[0, 0, j] * (q_ref[0, m, j] + p0[j] * np.float32(DM[0, 0]))
                for j in range(8)
            ])
            write(w7_ref, (m,), [
                tf_ref[1, 0, j] * (q_ref[1, m, j] + p0[j] * np.float32(DM[ORDER, 0]))
                for j in range(8)
            ])

    return odd_face


def make_even_face(scale, total):
    def even_face(ev_ref, rev_ref, w0_ref, w7_ref, rf_ref, accf_ref, tf_ref, rot_ref,
                  p7_ref, sod_ref, sev_ref):
        rot = rotations(rot_ref)
        tables = third_tables()
        for m in range(2):
            p7 = [
                (ev_ref[m, j] + rev_ref[m, j]) * (rf_ref[1, j] * np.float32(scale))
                for j in range(8)
            ]
            if total:
                p7 = [p7[j] + accf_ref[1, m, j] for j in range(8)]
            write(p7_ref, (m,), p7)
            rest = in_plane(p7, tf_ref, (1,), rot)
            plane = [
                rest[j] + w7_ref[m, j] + tf_ref[1, 0, j] * (p7[j] * np.float32(DM[ORDER, ORDER]))
                for j in range(8)
            ]
            write(sev_ref, (m,), plane_sum(plane, tables))
            plane = [
                w0_ref[m, j] + tf_ref[0, 0, j] * (p7[j] * np.float32(DM[0, ORDER]))
                for j in range(8)
            ]
            write(sod_ref, (m,), plane_sum(plane, tables))

    return even_face


def make_first_inner(scale, opening):
    def first_inner(p0_ref, p7_ref, gi_ref, acci_ref, wp_ref, ri_ref, ti_ref, d_ref,
                    gn_ref, an_ref, q_ref):
        def put(m, i, value):
            write(gn_ref, (m, i), value)
            base = gi_ref if opening else acci_ref
            write(an_ref, (m, i), [base[m, i, j] + value[j] for j in range(8)])

        inner_close(p0_ref, p7_ref, wp_ref, ri_ref, ti_ref, d_ref, scale, put)
        face_partials(gn_ref, q_ref)

    return first_inner


def make_ahead(scale, carry_transport):
    def ahead(ev_ref, rev_ref, rf_ref, q_ref, tf_ref, p7_ref, sod_ref):
        tables = third_tables()
        for m in range(2):
            p7 = [
                (ev_ref[m, j] + rev_ref[m, j]) * (rf_ref[1, j] * np.float32(scale))
                for j in range(8)
            ]
            write(p7_ref, (m,), p7)
            plane = [
                tf_ref[0, 0, j] * (q_ref[0, m, j] + p7[j] * np.float32(DM[0, ORDER]))
                for j in range(8)
            ]
            write(sod_ref, (m,), plane_sum(plane, tables))
        if carry_transport:
            for r in range(3):
                write(sod_ref, (2 + r,), read(tf_ref, 0, r))

    return ahead


def between(p7_ref, gi_ref, q_ref, tf_ref, ti_ref, rot_ref, d_ref, wp_ref, w7_ref):
    rot = rotations(rot_ref)
    for m in range(2):
        p7 = read(p7_ref, m)
        rest = in_plane(p7, tf_ref, (1,), rot)
        write(w7_ref, (m,), [
            rest[j] + tf_ref[1, 0, j] * (q_ref[1, m, j] + p7[j] * np.float32(DM[ORDER, ORDER]))
            for j in range(8)
        ])
    inner_open(gi_ref, ti_ref, rot, d_ref, wp_ref)


def make_behind(scale):
    def behind(od_ref, rod_ref, rf_ref, w7_ref, tf_ref, p0_ref, sev_ref):
        tables = third_tables()
        for m in range(2):
            p0 = [
                (od_ref[m, j] + rod_ref[m, j]) * (rf_ref[0, j] * np.float32(scale))
                for j in range(8)
            ]
            write(p0_ref, (m,), p0)
            plane = [
                w7_ref[m, j] + tf_ref[1, 0, j] * (p0[j] * np.float32(DM[ORDER, 0]))
                for j in range(8)
            ]
            write(sev_ref, (m,), plane_sum(plane, tables))

    return behind


def make_second_inner(scale, opening, closing, early):
    def second_inner(*refs):
        (p0_ref, p7_ref, b0_ref, b7_ref, accf_ref, acci_ref, wp_ref, ri_ref, ti_ref, ts_ref,
         rot_ref, d_ref) = refs[:12]
        gn_ref, q_ref, an_ref, afn_ref, wn_ref = refs[12:17]
        rot = rotations(rot_ref)
        if not early:
            e_ref = refs[17]
            tables = third_tables()
            for m in range(2):
                write(e_ref, (m,), shared_terms(read(p0_ref, m), ts_ref, rot, tables))
        for face, (now, before) in enumerate(((p0_ref, b0_ref), (p7_ref, b7_ref))):
            for m in range(2):
                for j in range(8):
                    value = now[m, j] + before[m, j]
                    afn_ref[face, m, j] = value if opening else value + accf_ref[face, m, j]

        def put(m, i, value):
            total = [acci_ref[m, i, j] + value[j] for j in range(8)]
            write(gn_ref, (m, i), total if closing else value)
            if not closing:
                write(an_ref, (m, i), total)

        inner_close(p0_ref, p7_ref, wp_ref, ri_ref, ti_ref, d_ref, scale, put)
        face_partials(gn_ref, q_ref)
        inner_open(gn_ref, ti_ref, rot, d_ref, wn_ref)

    return second_inner


def make_last_inner(scale):
    def last_inner(order_ref, p0_ref, p7_ref, b0_ref, b7_ref, accf_ref, acci_ref, wp_ref, ri_ref,
                   ti_ref, ts_ref, rot_ref, d_ref, out_ref, afn_ref, e_ref, buf, sems):
        parity = lax.axis_index("elem") % 2
        idx = jnp.broadcast_to(order_ref[...], (SUB, LANES))

        def put(m, i, value):
            total = [acci_ref[m, i, j] + value[j] for j in range(8)]
            dst = source_plane(parity, i + 1) - 1
            write(buf, (m, dst), [gather_lanes(v, idx) for v in total])

        inner_close(p0_ref, p7_ref, wp_ref, ri_ref, ti_ref, d_ref, scale, put)
        copies = [
            pltpu.make_async_copy(buf.at[m], out_ref.at[m, pl.ds(1, 6)], sems.at[m])
            for m in range(2)
        ]
        for copy in copies:
            copy.start()
        rot = rotations(rot_ref)
        tables = third_tables()
        for m in range(2):
            write(e_ref, (m,), shared_terms(read(p0_ref, m), ts_ref, rot, tables))
        for face, (now, before) in enumerate(((p0_ref, b0_ref), (p7_ref, b7_ref))):
            for m in range(2):
                for j in range(8):
                    afn_ref[face, m, j] = now[m, j] + before[m, j] + accf_ref[face, m, j]
        for copy in copies:
            copy.wait()

    return last_inner


def make_finish(face, scale):
    def finish(order_ref, own_ref, got_ref, e_ref, rf_ref, accf_ref, part_ref, out_ref, buf, sems):
        parity = lax.axis_index("elem") % 2
        idx = jnp.broadcast_to(order_ref[...], (SUB, LANES))
        dst = source_plane(parity, face * ORDER)
        copies = []
        for m in range(2):
            for j in range(8):
                value = own_ref[m, j] + got_ref[m, j]
                if face == 0:
                    value = value + e_ref[m, j]
                value = value * (rf_ref[face, j] * np.float32(scale)) + accf_ref[face, m, j]
                buf[m, j] = gather_lanes(value, idx)
            copy = pltpu.make_async_copy(buf.at[m], out_ref.at[m, dst], sems.at[m])
            copy.start()
            copies.append(copy)
        for copy in copies:
            copy.wait()

    return finish


VM = pl.BlockSpec(memory_space=pltpu.VMEM)
SM = pl.BlockSpec(memory_space=pltpu.SMEM)
HB = pl.BlockSpec(memory_space=pltpu.HBM)


def call(kernel, outs, args, name, cost, smem=(), hbm=(), hbm_out=(), scratch=(), alias={}):
    specs = [SM if n in smem else HB if n in hbm else VM for n in range(len(args))]
    out_specs = [HB if n in hbm_out else VM for n in range(len(outs))]
    shapes = [jax.ShapeDtypeStruct(s, jnp.float32) for s in outs]
    single = len(outs) == 1
    return pl.pallas_call(
        kernel,
        out_shape=shapes[0] if single else shapes,
        in_specs=specs,
        out_specs=out_specs[0] if single else out_specs,
        scratch_shapes=list(scratch),
        input_output_aliases=alias,
        name=name,
        compiler_params=pltpu.CompilerParams(vmem_limit_bytes=8 << 20),
        cost_estimate=pl.CostEstimate(
            flops=cost * 1000000, bytes_accessed=1 << 10, transcendentals=0
        ),
    )(*args)


def per_device(scalars, transport, mass, element_order):
    count = lax.axis_size("elem")
    even_pairs = [(i, i ^ 1) for i in range(count)]
    odd_pairs = [(i, (i + 1) % count if i % 2 else (i - 1) % count) for i in range(count)]
    swap_od = lambda x: lax.ppermute(x, "elem", odd_pairs)
    swap_ev = lambda x: lax.ppermute(x, "elem", even_pairs)
    rot = jnp.asarray(np.broadcast_to(ROT[:, :, None], (8, SUB, LANES)))
    dmat = jnp.asarray(DM, jnp.float32)
    members = scalars.shape[0]
    grid = (EXT, EXT, SUB, LANES)
    scal = scalars.reshape((members,) + grid)
    tr = transport.reshape((3,) + grid)
    mas = mass.reshape(grid)
    tile = (EXT, SUB, LANES)
    face, inner = (2,) + tile, (2, 6) + tile

    od, ev = call(
        project_faces, [(3,) + tile] * 2, (element_order, scal, mas), "project", 1, hbm=(0, 1, 2),
        scratch=[pltpu.VMEM((1, LANES), jnp.int32), pltpu.VMEM((2, 2) + tile, jnp.float32),
                 pltpu.VMEM((2,) + tile, jnp.float32), pltpu.SemaphoreType.DMA((7,))])
    rod, rev = swap_od(od), swap_ev(ev)
    gi, q, ri, ti, tf = call(
        prepare, [inner, (2,) + face, (6,) + tile, (6, 3) + tile, (2, 3) + tile],
        (element_order, scal, mas, tr), "prepare", 4000)

    def opening_terms(gi_ref, ti_ref, rot_ref, d_ref, wp_ref):
        inner_open(gi_ref, ti_ref, rotations(rot_ref), d_ref, wp_ref)

    wp = call(opening_terms, [inner], (gi, ti, rot, dmat), "terms", 2000, smem=(3,))
    p0, p7, rf, od, ev = call(
        start_faces, [face, face, (2,) + tile, face, face],
        (od, ev, rod, rev, q, tf, rot), "faces", 1)
    acci, accf, ts, shared = gi, q, tf, None
    pairs = SUBSTEPS * STAGES // 2
    for n in range(pairs):
        s = 2 * n % STAGES + 1
        opening, closing, early = s == 1, s + 1 == STAGES, n == 0
        rev, rod = swap_ev(ev), swap_od(od)
        gm, acci, q = call(
            make_first_inner(1.0 / s, opening), [inner, inner, (2,) + face],
            (p0, p7, gi, acci, wp, ri, ti, dmat), "first", 1000, smem=(7,))
        m7, od2 = call(
            make_ahead(1.0 / s, early), [face, ((5 if early else 2),) + tile],
            (ev, rev, rf, q, tf), "ahead", 1)
        rod2 = swap_od(od2)
        wp, w7 = call(
            between, [inner, face], (m7, gm, q, tf, ti, rot, dmat), "between", 2000, smem=(6,))
        m0, ev2 = call(
            make_behind(1.0 / s), [face, face], (od, rod, rf, w7, tf), "behind", 1)
        rev2 = swap_ev(ev2)
        if n < pairs - 1:
            outs = [inner, (2,) + face, inner, (2,) + face, inner] + ([] if early else [face])
            res = call(
                make_second_inner(1.0 / (s + 1), opening, closing, early), outs,
                (m0, m7, p0, p7, accf, acci, wp, ri, ti, ts, rot, dmat), "second", 3000, smem=(11,))
            gi, q, acci, accf, wp = res[:5]
            extra = m0 if early else res[5]
            res = call(
                make_odd_face(1.0 / (s + 1), closing, early),
                [face] * 3 + ([(3,) + tile] if early else []),
                (od2, rod2, extra, rf, accf, q, tf, rot), "odd", 3000)
            p0, w0, w7 = res[:3]
            if early:
                ts = res[3]
            p7, od, ev = call(
                make_even_face(1.0 / (s + 1), closing), [face] * 3,
                (ev2, rev2, w0, w7, rf, accf, tf, rot), "even", 1)
        else:
            out, accf, shared = call(
                make_last_inner(1.0 / (s + 1)), [(members,) + grid, (2,) + face, face],
                (element_order, m0, m7, p0, p7, accf, acci, wp, ri, ti, ts, rot, dmat), "last", 3000,
                smem=(12,), hbm_out=(0,),
                scratch=[pltpu.VMEM(inner, jnp.float32), pltpu.SemaphoreType.DMA((2,))])
            for side, own, got in ((0, od2, rod2), (1, ev2, rev2)):
                out = call(
                    make_finish(side, 1.0 / (s + 1)), [(members,) + grid],
                    (element_order, own, got, shared, rf, accf, out), "finish", 3000 - 2999 * side,
                    hbm=(6,), hbm_out=(0,), alias={6: 0},
                    scratch=[pltpu.VMEM(face, jnp.float32), pltpu.SemaphoreType.DMA((2,))])
    return out.reshape(scalars.shape)


def solution(mesh):
    in_specs = (P("ens", None, "elem"), P(None, None, "elem"), P(None, "elem"), P("elem", None))
    out_specs = P("ens", None, "elem")
    return jax.shard_map(
        per_device, mesh=mesh, in_specs=in_specs, out_specs=out_specs, check_vma=False
    )
```

```python
import jax
import jax.numpy as jnp
import numpy as np
from jax import lax
from jax.experimental import pallas as pl
from jax.experimental.pallas import tpu as pltpu
from jax.sharding import PartitionSpec as P

ORDER = 7
EXT = ORDER + 1
SUBSTEPS = 2
STAGES = 4
EY = 8
EZ = 16
LANES = EY * EZ
SUB = 8

time_step = 0.015


def legendre_table(points, degree):
    table = np.zeros((points.shape[0], degree + 1))
    table[:, 0] = 1.0
    table[:, 1] = points
    for level in range(2, degree + 1):
        table[:, level] = (
            (2 * level - 1) * points * table[:, level - 1] - (level - 1) * table[:, level - 2]
        ) / level
    return table


def gll_derivative(degree):
    extent = degree + 1
    points = np.cos(np.pi * np.arange(extent) / degree)
    for sweep in range(60):
        table = legendre_table(points, degree)
        points = points - (points * table[:, degree] - table[:, degree - 1]) / (
            extent * table[:, degree]
        )
    points = points[::-1].copy()
    values = legendre_table(points, degree)[:, degree]
    matrix = np.zeros((extent, extent))
    for target in range(extent):
        for source in range(extent):
            if target != source:
                matrix[target, source] = values[target] / (
                    values[source] * (points[target] - points[source])
                )
    matrix[0, 0] = -degree * (degree + 1) / 4.0
    matrix[extent - 1, extent - 1] = degree * (degree + 1) / 4.0
    return matrix


DM = gll_derivative(ORDER)
SUM_PART = [[(DM[j, a] + DM[j, 7 - a]) / 2 for a in range(4)] for j in range(4)]
DIF_PART = [[(DM[j, a] - DM[j, 7 - a]) / 2 for a in range(4)] for j in range(4)]
ROT = np.array([[DM[k, (k - r) % 8] for k in range(8)] for r in range(8)], np.float32)


def combine(coefs, items):
    total = None
    for c, x in zip(coefs, items):
        term = x * np.float32(c)
        total = term if total is None else total + term
    return total


def along_second(plane):
    even = [plane[a] + plane[7 - a] for a in range(4)]
    odd = [plane[a] - plane[7 - a] for a in range(4)]
    out = [None] * 8
    for j in range(4):
        e = combine(SUM_PART[j], even)
        o = combine(DIF_PART[j], odd)
        out[j] = o + e
        out[7 - j] = o - e
    return out


def along_third(x, rot):
    total = x * rot[0]
    for r in range(1, 8):
        total = total + pltpu.roll(x, r, 0) * rot[r]
    return total


def gather_lanes(x, idx):
    return jnp.take_along_axis(x, idx, axis=1, mode="promise_in_bounds")


def third_tables():
    lane = lax.broadcasted_iota(jnp.int32, (SUB, LANES), 1)
    k = lax.broadcasted_iota(jnp.int32, (SUB, LANES), 0)
    z = lane % EZ
    back = jnp.where(z == 0, lane + (EZ - 1), lane - 1)
    ahead = jnp.where(z == EZ - 1, lane - (EZ - 1), lane + 1)
    return jnp.where(k == 0, back, ahead), k == 0, k == ORDER


def plane_sum(plane, tables):
    idx, first, last = tables
    up = plane[7] + pltpu.roll(plane[0], LANES - EZ, 1)
    plane = [pltpu.roll(up, EZ, 1)] + list(plane[1:7]) + [up]
    out = []
    for v in plane:
        x = jnp.where(first, pltpu.roll(v, 1, 0), jnp.where(last, pltpu.roll(v, 7, 0), 0.0))
        out.append(v + gather_lanes(x, idx))
    return out


def write(ref, lead, plane):
    for j, v in enumerate(plane):
        ref[lead + (j,)] = v


def read(ref, *lead):
    return [ref[lead + (j,)] for j in range(8)]


def brick_index(order_ref):
    order = jnp.broadcast_to(order_ref[...], (LANES, LANES))
    pos = lax.broadcasted_iota(jnp.int32, (LANES, LANES), 0)
    hot = jnp.where(order == pos, 1.0, 0.0).astype(jnp.bfloat16)
    slot = lax.broadcasted_iota(jnp.int32, (SUB, LANES), 1).astype(jnp.float32).astype(jnp.bfloat16)
    found = lax.dot_general(
        slot, hot, (((1,), (1,)), ((), ())), preferred_element_type=jnp.float32
    )
    return found.astype(jnp.int32)


def source_plane(parity, i):
    return jnp.where(parity == 1, ORDER - i, i)


def source_plane(parity, i):
    return jnp.where(parity == 1, ORDER - i, i)


def project_odd(order_ref, scal_ref, mass_ref, od_ref, order_buf, scal_buf, mass_buf, sems):
    parity = lax.axis_index("elem") % 2
    src = source_plane(parity, 0)
    copies = [pltpu.make_async_copy(order_ref, order_buf, sems.at[0])]
    copies.append(pltpu.make_async_copy(mass_ref.at[src], mass_buf, sems.at[1]))
    for m in range(2):
        copies.append(pltpu.make_async_copy(scal_ref.at[m, src], scal_buf.at[m], sems.at[2 + m]))
    for copy in copies:
        copy.start()
    tables = third_tables()
    copies[0].wait()
    idx = brick_index(order_buf)
    for copy in copies[1:]:
        copy.wait()
    project(read(mass_buf), [read(scal_buf, m) for m in range(2)], idx, tables, od_ref)


def project_even(order_ref, scal_ref, mass_ref, ev_ref):
    src = source_plane(lax.axis_index("elem") % 2, ORDER)
    idx = brick_index(order_ref)
    project(read(mass_ref, src), [read(scal_ref, m, src) for m in range(2)], idx, third_tables(), ev_ref)


def project(weight, scal, idx, tables, out_ref):
    weight = [gather_lanes(v, idx) for v in weight]
    planes = [[gather_lanes(plane[j], idx) * weight[j] for j in range(8)] for plane in scal]
    planes = [plane_sum(plane, tables) for plane in planes + [weight]]
    for r in range(3):
        write(out_ref, (r,), planes[r])


def prepare(order_ref, scal_ref, mass_ref, tr_ref, gi_ref, q_ref, ri_ref, ti_ref, tf_ref):
    parity = lax.axis_index("elem") % 2
    idx = brick_index(order_ref)
    tables = third_tables()
    sign = jnp.where(parity == 1, time_step, -time_step).astype(jnp.float32)
    signs = (sign, np.float32(-time_step), np.float32(-time_step))

    for face in range(2):
        src = source_plane(parity, face * ORDER)
        for r in range(3):
            for j in range(8):
                tf_ref[face, r, j] = gather_lanes(tr_ref[r, src, j], idx) * signs[r]

    def body(i, carry):
        src = source_plane(parity, i + 1)
        for r in range(3):
            for j in range(8):
                ti_ref[i, r, j] = gather_lanes(tr_ref[r, src, j], idx) * signs[r]
        weight = [gather_lanes(mass_ref[src, j], idx) for j in range(8)]
        inverse = [1.0 / v for v in plane_sum(weight, tables)]
        write(ri_ref, (i,), inverse)
        for m in range(2):
            plane = [gather_lanes(scal_ref[m, src, j], idx) * weight[j] for j in range(8)]
            plane = plane_sum(plane, tables)
            write(gi_ref, (m, i), [plane[j] * inverse[j] for j in range(8)])
        return carry

    lax.fori_loop(0, 6, body, 0)
    face_partials(gi_ref, q_ref)


def face_partials(gi_ref, q_ref):
    for m in range(2):
        for j in range(8):
            rows = [gi_ref[m, i, j] for i in range(6)]
            for face in range(2):
                q_ref[face, m, j] = combine(DM[face * ORDER, 1:7], rows)


def in_plane(plane, t_ref, lead, rot):
    second = along_second(plane)
    return [
        t_ref[lead + (1, j)] * second[j] + t_ref[lead + (2, j)] * along_third(plane[j], rot)
        for j in range(8)
    ]


def inner_open(gi_ref, ti_ref, rot, d_ref, wp_ref):
    def body(i, carry):
        row = [d_ref[i + 1, a + 1] for a in range(6)]
        for m in range(2):
            rest = in_plane(read(gi_ref, m, i), ti_ref, (i,), rot)
            for j in range(8):
                first = gi_ref[m, 0, j] * row[0]
                for a in range(1, 6):
                    first = first + gi_ref[m, a, j] * row[a]
                wp_ref[m, i, j] = rest[j] + ti_ref[i, 0, j] * first
        return carry

    lax.fori_loop(0, 6, body, 0)


def inner_close(p0_ref, p7_ref, wp_ref, ri_ref, ti_ref, scale, put, q_ref=None):
    tables = third_tables()
    for m in range(2):
        sums = [[], []]
        for i in range(6):
            near, far = np.float32(DM[i + 1, 0]), np.float32(DM[i + 1, ORDER])
            plane = [
                wp_ref[m, i, j] + ti_ref[i, 0, j] * (p0_ref[m, j] * near + p7_ref[m, j] * far)
                for j in range(8)
            ]
            plane = plane_sum(plane, tables)
            kept = put(m, i, [plane[j] * (ri_ref[i, j] * np.float32(scale)) for j in range(8)])
            for face in range(2):
                terms = [v * np.float32(DM[face * ORDER, i + 1]) for v in kept]
                sums[face] = [x + y for x, y in zip(sums[face], terms)] if i else terms
        if q_ref is not None:
            for face in range(2):
                write(q_ref, (face, m), sums[face])


def rotations(rot_ref):
    return [rot_ref[r] for r in range(8)]


def both_faces(p0, p7, q_ref, tf_ref, rot, tables, sod_ref, sev_ref):
    for face, own, out in ((1, p7, sev_ref), (0, p0, sod_ref)):
        for m in range(2):
            rest = in_plane(own[m], tf_ref, (face,), rot)
            plane = [
                rest[j]
                + tf_ref[face, 0, j]
                * (
                    q_ref[face, m, j]
                    + p0[m][j] * np.float32(DM[face * ORDER, 0])
                    + p7[m][j] * np.float32(DM[face * ORDER, ORDER])
                )
                for j in range(8)
            ]
            write(out, (m,), plane_sum(plane, tables))


def start_faces(od_ref, ev_ref, rod_ref, rev_ref, q_ref, tf_ref, rot_ref,
                p0_ref, p7_ref, rf_ref, sod_ref, sev_ref):
    p = []
    for face, (own, got, out) in enumerate(((od_ref, rod_ref, p0_ref), (ev_ref, rev_ref, p7_ref))):
        inverse = [1.0 / (own[2, j] + got[2, j]) for j in range(8)]
        write(rf_ref, (face,), inverse)
        p.append([[(own[m, j] + got[m, j]) * inverse[j] for j in range(8)] for m in range(2)])
        for m in range(2):
            write(out, (m,), p[face][m])
    both_faces(p[0], p[1], q_ref, tf_ref, rotations(rot_ref), third_tables(), sod_ref, sev_ref)


def shared_terms(p0, t_ref, rot, tables):
    rest = in_plane(p0, t_ref, (), rot)
    plane = [rest[j] + t_ref[0, j] * (p0[j] * np.float32(DM[0, 0])) for j in range(8)]
    return plane_sum(plane, tables)


def make_odd_face(scale, total, early):
    def odd_face(*refs):
        od_ref, rod_ref, e_ref, rf_ref, accf_ref, q_ref, tf_ref, rot_ref = refs[:8]
        p0_ref, w0_ref, w7_ref = refs[8:11]
        rot = rotations(rot_ref)
        tables = third_tables()
        if early:
            ts_ref = refs[11]
            for r in range(3):
                write(ts_ref, (r,), [tf_ref[0, r, j] + rod_ref[2 + r, j] for j in range(8)])
        for m in range(2):
            shared = read(e_ref, m)
            if early:
                shared = shared_terms(shared, ts_ref, rot, tables)
            p0 = [
                (od_ref[m, j] + rod_ref[m, j] + shared[j]) * (rf_ref[0, j] * np.float32(scale))
                for j in range(8)
            ]
            if total:
                p0 = [p0[j] + accf_ref[0, m, j] for j in range(8)]
            write(p0_ref, (m,), p0)
            rest = in_plane(p0, tf_ref, (0,), rot)
            write(w0_ref, (m,), [
                rest[j] + tf_ref[0, 0, j] * (q_ref[0, m, j] + p0[j] * np.float32(DM[0, 0]))
                for j in range(8)
            ])
            write(w7_ref, (m,), [
                tf_ref[1, 0, j] * (q_ref[1, m, j] + p0[j] * np.float32(DM[ORDER, 0]))
                for j in range(8)
            ])

    return odd_face


def make_even_face(scale, total):
    def even_face(ev_ref, rev_ref, w0_ref, w7_ref, rf_ref, accf_ref, tf_ref, rot_ref,
                  p7_ref, sod_ref, sev_ref):
        rot = rotations(rot_ref)
        tables = third_tables()
        weight = [rf_ref[1, j] * np.float32(scale) for j in range(8)]
        p7 = [[(ev_ref[m, j] + rev_ref[m, j]) * weight[j] for j in range(8)] for m in range(2)]
        if total:
            p7 = [[p7[m][j] + accf_ref[1, m, j] for j in range(8)] for m in range(2)]
        evens, odds = [], []
        for m in range(2):
            rest = in_plane(p7[m], tf_ref, (1,), rot)
            evens.append([
                rest[j] + w7_ref[m, j] + tf_ref[1, 0, j] * (p7[m][j] * np.float32(DM[ORDER, ORDER]))
                for j in range(8)
            ])
            odds.append([
                w0_ref[m, j] + tf_ref[0, 0, j] * (p7[m][j] * np.float32(DM[0, ORDER]))
                for j in range(8)
            ])
        evens = [plane_sum(plane, tables) for plane in evens]
        odds = [plane_sum(plane, tables) for plane in odds]
        for m in range(2):
            write(sev_ref, (m,), evens[m])
            write(sod_ref, (m,), odds[m])
            write(p7_ref, (m,), p7[m])

    return even_face


def make_first_inner(scale, opening):
    def first_inner(p0_ref, p7_ref, gi_ref, acci_ref, wp_ref, ri_ref, ti_ref,
                    gn_ref, an_ref, q_ref):
        def put(m, i, value):
            base = gi_ref if opening else acci_ref
            total = [base[m, i, j] + value[j] for j in range(8)]
            write(gn_ref, (m, i), value)
            write(an_ref, (m, i), total)
            return value

        inner_close(p0_ref, p7_ref, wp_ref, ri_ref, ti_ref, scale, put, q_ref)

    return first_inner


def make_ahead(scale, carry_transport):
    def ahead(ev_ref, rev_ref, rf_ref, q_ref, tf_ref, p7_ref, sod_ref):
        tables = third_tables()
        weight = [rf_ref[1, j] * np.float32(scale) for j in range(8)]
        p7 = [[(ev_ref[m, j] + rev_ref[m, j]) * weight[j] for j in range(8)] for m in range(2)]
        planes = [
            [
                tf_ref[0, 0, j] * (q_ref[0, m, j] + p7[m][j] * np.float32(DM[0, ORDER]))
                for j in range(8)
            ]
            for m in range(2)
        ]
        planes = [plane_sum(plane, tables) for plane in planes]
        for m in range(2):
            write(sod_ref, (m,), planes[m])
            write(p7_ref, (m,), p7[m])
        if carry_transport:
            for r in range(3):
                write(sod_ref, (2 + r,), read(tf_ref, 0, r))

    return ahead


def between(p7_ref, gi_ref, q_ref, tf_ref, ti_ref, rot_ref, d_ref, wp_ref, w7_ref):
    rot = rotations(rot_ref)
    for m in range(2):
        p7 = read(p7_ref, m)
        rest = in_plane(p7, tf_ref, (1,), rot)
        write(w7_ref, (m,), [
            rest[j] + tf_ref[1, 0, j] * (q_ref[1, m, j] + p7[j] * np.float32(DM[ORDER, ORDER]))
            for j in range(8)
        ])
    inner_open(gi_ref, ti_ref, rot, d_ref, wp_ref)


def make_behind(scale):
    def behind(od_ref, rod_ref, rf_ref, w7_ref, tf_ref, p0_ref, sev_ref):
        tables = third_tables()
        weight = [rf_ref[0, j] * np.float32(scale) for j in range(8)]
        p0 = [[(od_ref[m, j] + rod_ref[m, j]) * weight[j] for j in range(8)] for m in range(2)]
        planes = [
            [
                w7_ref[m, j] + tf_ref[1, 0, j] * (p0[m][j] * np.float32(DM[ORDER, 0]))
                for j in range(8)
            ]
            for m in range(2)
        ]
        planes = [plane_sum(plane, tables) for plane in planes]
        for m in range(2):
            write(sev_ref, (m,), planes[m])
            write(p0_ref, (m,), p0[m])

    return behind


def make_second_inner(scale, opening, closing, early):
    def second_inner(*refs):
        (p0_ref, p7_ref, b0_ref, b7_ref, accf_ref, acci_ref, wp_ref, ri_ref, ti_ref, ts_ref,
         rot_ref, d_ref) = refs[:12]
        gn_ref, q_ref, an_ref, afn_ref, wn_ref = refs[12:17]
        rot = rotations(rot_ref)
        if not early:
            e_ref = refs[17]
            tables = third_tables()
            for m in range(2):
                write(e_ref, (m,), shared_terms(read(p0_ref, m), ts_ref, rot, tables))
        for face, (now, before) in enumerate(((p0_ref, b0_ref), (p7_ref, b7_ref))):
            for m in range(2):
                for j in range(8):
                    value = now[m, j] + before[m, j]
                    afn_ref[face, m, j] = value if opening else value + accf_ref[face, m, j]

        def put(m, i, value):
            total = [acci_ref[m, i, j] + value[j] for j in range(8)]
            kept = total if closing else value
            write(gn_ref, (m, i), kept)
            if not closing:
                write(an_ref, (m, i), total)
            return kept

        inner_close(p0_ref, p7_ref, wp_ref, ri_ref, ti_ref, scale, put, q_ref)
        inner_open(gn_ref, ti_ref, rot, d_ref, wn_ref)

    return second_inner


def make_last_inner(scale):
    def last_inner(order_ref, p0_ref, p7_ref, b0_ref, b7_ref, accf_ref, acci_ref, wp_ref, ri_ref,
                   ti_ref, ts_ref, rot_ref, out_ref, afn_ref, e_ref, buf, sems):
        parity = lax.axis_index("elem") % 2
        idx = jnp.broadcast_to(order_ref[...], (SUB, LANES))

        def put(m, i, value):
            total = [acci_ref[m, i, j] + value[j] for j in range(8)]
            dst = source_plane(parity, i + 1) - 1
            write(buf, (m, dst), [gather_lanes(v, idx) for v in total])
            return total

        inner_close(p0_ref, p7_ref, wp_ref, ri_ref, ti_ref, scale, put)
        copies = [
            pltpu.make_async_copy(buf.at[m], out_ref.at[m, pl.ds(1, 6)], sems.at[m])
            for m in range(2)
        ]
        for copy in copies:
            copy.start()
        rot = rotations(rot_ref)
        tables = third_tables()
        for m in range(2):
            write(e_ref, (m,), shared_terms(read(p0_ref, m), ts_ref, rot, tables))
        for face, (now, before) in enumerate(((p0_ref, b0_ref), (p7_ref, b7_ref))):
            for m in range(2):
                for j in range(8):
                    afn_ref[face, m, j] = now[m, j] + before[m, j] + accf_ref[face, m, j]
        for copy in copies:
            copy.wait()

    return last_inner


def make_finish_odd(scale):
    def finish_odd(order_ref, own_ref, got_ref, e_ref, rf_ref, accf_ref, face_ref):
        idx = jnp.broadcast_to(order_ref[...], (SUB, LANES))
        for m in range(2):
            write(face_ref, (m,), [
                gather_lanes(
                    (own_ref[m, j] + got_ref[m, j] + e_ref[m, j])
                    * (rf_ref[0, j] * np.float32(scale))
                    + accf_ref[0, m, j],
                    idx,
                )
                for j in range(8)
            ])

    return finish_odd


def make_finish_even(scale):
    def finish_even(order_ref, own_ref, got_ref, rf_ref, accf_ref, face_ref, part_ref,
                    out_ref, buf, sems):
        parity = lax.axis_index("elem") % 2
        idx = jnp.broadcast_to(order_ref[...], (SUB, LANES))
        dst = source_plane(parity, ORDER)
        copies = []
        for m in range(2):
            write(buf, (m,), [
                gather_lanes(
                    (own_ref[m, j] + got_ref[m, j]) * (rf_ref[1, j] * np.float32(scale))
                    + accf_ref[1, m, j],
                    idx,
                )
                for j in range(8)
            ])
            copies.append(pltpu.make_async_copy(buf.at[m], out_ref.at[m, dst], sems.at[0, m]))
            copies[-1].start()
        for m in range(2):
            copies.append(
                pltpu.make_async_copy(face_ref.at[m], out_ref.at[m, ORDER - dst], sems.at[1, m])
            )
            copies[-1].start()
        for copy in copies:
            copy.wait()

    return finish_even


VM = pl.BlockSpec(memory_space=pltpu.VMEM)
SM = pl.BlockSpec(memory_space=pltpu.SMEM)
HB = pl.BlockSpec(memory_space=pltpu.HBM)


def call(kernel, outs, args, name, cost, smem=(), hbm=(), hbm_out=(), scratch=(), alias={}):
    specs = [SM if n in smem else HB if n in hbm else VM for n in range(len(args))]
    out_specs = [HB if n in hbm_out else VM for n in range(len(outs))]
    shapes = [jax.ShapeDtypeStruct(s, jnp.float32) for s in outs]
    single = len(outs) == 1
    return pl.pallas_call(
        kernel,
        out_shape=shapes[0] if single else shapes,
        in_specs=specs,
        out_specs=out_specs[0] if single else out_specs,
        scratch_shapes=list(scratch),
        input_output_aliases=alias,
        name=name,
        compiler_params=pltpu.CompilerParams(vmem_limit_bytes=8 << 20),
        cost_estimate=pl.CostEstimate(
            flops=cost * 1000000, bytes_accessed=1 << 10, transcendentals=0
        ),
    )(*args)


def per_device(scalars, transport, mass, element_order):
    count = lax.axis_size("elem")
    even_pairs = [(i, i ^ 1) for i in range(count)]
    odd_pairs = [(i, (i + 1) % count if i % 2 else (i - 1) % count) for i in range(count)]
    swap_od = lambda x: lax.ppermute(x, "elem", odd_pairs)
    swap_ev = lambda x: lax.ppermute(x, "elem", even_pairs)
    rot = jnp.asarray(np.broadcast_to(ROT[:, :, None], (8, SUB, LANES)))
    dmat = jnp.asarray(DM, jnp.float32)
    members = scalars.shape[0]
    grid = (EXT, EXT, SUB, LANES)
    scal = scalars.reshape((members,) + grid)
    tr = transport.reshape((3,) + grid)
    mas = mass.reshape(grid)
    tile = (EXT, SUB, LANES)
    face, inner = (2,) + tile, (2, 6) + tile

    stay = lambda x: pltpu.with_memory_space_constraint(x, pltpu.HBM)
    od = call(
        project_odd, [(3,) + tile], (stay(element_order), stay(scal), stay(mas)), "project", 1,
        hbm=(0, 1, 2),
        scratch=[pltpu.VMEM((1, LANES), jnp.int32), pltpu.VMEM(face, jnp.float32),
                 pltpu.VMEM(tile, jnp.float32), pltpu.SemaphoreType.DMA((4,))])
    ev = call(project_even, [(3,) + tile], (element_order, scal, mas), "project", 1)
    rod, rev = swap_od(od), swap_ev(ev)
    gi, q, ri, ti, tf = call(
        prepare, [inner, (2,) + face, (6,) + tile, (6, 3) + tile, (2, 3) + tile],
        (element_order, scal, mas, tr), "prepare", 4000)

    def opening_terms(gi_ref, ti_ref, rot_ref, d_ref, wp_ref):
        inner_open(gi_ref, ti_ref, rotations(rot_ref), d_ref, wp_ref)

    wp = call(opening_terms, [inner], (gi, ti, rot, dmat), "terms", 2000, smem=(3,))
    p0, p7, rf, od, ev = call(
        start_faces, [face, face, (2,) + tile, face, face],
        (od, ev, rod, rev, q, tf, rot), "faces", 1)
    acci, accf, ts, shared = gi, q, tf, None
    pairs = SUBSTEPS * STAGES // 2
    for n in range(pairs):
        s = 2 * n % STAGES + 1
        opening, closing, early = s == 1, s + 1 == STAGES, n == 0
        rev, rod = swap_ev(ev), swap_od(od)
        gm, acci, q = call(
            make_first_inner(1.0 / s, opening), [inner, inner, (2,) + face],
            (p0, p7, gi, acci, wp, ri, ti), "first", 1000)
        m7, od2 = call(
            make_ahead(1.0 / s, early), [face, ((5 if early else 2),) + tile],
            (ev, rev, rf, q, tf), "ahead", 1)
        rod2 = swap_od(od2)
        wp, w7 = call(
            between, [inner, face], (m7, gm, q, tf, ti, rot, dmat), "between", 2000, smem=(6,))
        m0, ev2 = call(
            make_behind(1.0 / s), [face, face], (od, rod, rf, w7, tf), "behind", 1)
        rev2 = swap_ev(ev2)
        if n < pairs - 1:
            outs = [inner, (2,) + face, inner, (2,) + face, inner] + ([] if early else [face])
            res = call(
                make_second_inner(1.0 / (s + 1), opening, closing, early), outs,
                (m0, m7, p0, p7, accf, acci, wp, ri, ti, ts, rot, dmat), "second", 3000, smem=(11,))
            gi, q, acci, accf, wp = res[:5]
            extra = m0 if early else res[5]
            res = call(
                make_odd_face(1.0 / (s + 1), closing, early),
                [face] * 3 + ([(3,) + tile] if early else []),
                (od2, rod2, extra, rf, accf, q, tf, rot), "odd", 3000)
            p0, w0, w7 = res[:3]
            if early:
                ts = res[3]
            p7, od, ev = call(
                make_even_face(1.0 / (s + 1), closing), [face] * 3,
                (ev2, rev2, w0, w7, rf, accf, tf, rot), "even", 1)
        else:
            out, accf, shared = call(
                make_last_inner(1.0 / (s + 1)), [(members,) + grid, (2,) + face, face],
                (element_order, m0, m7, p0, p7, accf, acci, wp, ri, ti, ts, rot), "last", 3000,
                hbm_out=(0,),
                scratch=[pltpu.VMEM(inner, jnp.float32), pltpu.SemaphoreType.DMA((2,))])
            odd = call(
                make_finish_odd(1.0 / (s + 1)), [face],
                (element_order, od2, rod2, shared, rf, accf), "finish", 3000)
            out = call(
                make_finish_even(1.0 / (s + 1)), [(members,) + grid],
                (element_order, ev2, rev2, rf, accf, odd, out), "finish", 1,
                hbm=(6,), hbm_out=(0,), alias={6: 0},
                scratch=[pltpu.VMEM(face, jnp.float32), pltpu.SemaphoreType.DMA((2, 2))])
    return out.reshape(scalars.shape)


def solution(mesh):
    in_specs = (P("ens", None, "elem"), P(None, None, "elem"), P(None, "elem"), P("elem", None))
    out_specs = P("ens", None, "elem")
    return jax.shard_map(
        per_device, mesh=mesh, in_specs=in_specs, out_specs=out_specs, check_vma=False
    )
```

```python
import jax
import jax.numpy as jnp
import numpy as np
from jax import lax
from jax.experimental import pallas as pl
from jax.experimental.pallas import tpu as pltpu
from jax.sharding import PartitionSpec as P

ORDER = 7
EXT = ORDER + 1
SUBSTEPS = 2
STAGES = 4
EY = 8
EZ = 16
LANES = EY * EZ
SUB = 8
ROWS = 7

time_step = 0.015


def legendre_table(points, degree):
    table = np.zeros((points.shape[0], degree + 1))
    table[:, 0] = 1.0
    table[:, 1] = points
    for level in range(2, degree + 1):
        table[:, level] = (
            (2 * level - 1) * points * table[:, level - 1] - (level - 1) * table[:, level - 2]
        ) / level
    return table


def gll_derivative(degree):
    extent = degree + 1
    points = np.cos(np.pi * np.arange(extent) / degree)
    for sweep in range(60):
        table = legendre_table(points, degree)
        points = points - (points * table[:, degree] - table[:, degree - 1]) / (
            extent * table[:, degree]
        )
    points = points[::-1].copy()
    values = legendre_table(points, degree)[:, degree]
    matrix = np.zeros((extent, extent))
    for target in range(extent):
        for source in range(extent):
            if target != source:
                matrix[target, source] = values[target] / (
                    values[source] * (points[target] - points[source])
                )
    matrix[0, 0] = -degree * (degree + 1) / 4.0
    matrix[extent - 1, extent - 1] = degree * (degree + 1) / 4.0
    return matrix


DM = gll_derivative(ORDER)
SUM_PART = [[(DM[j, a] + DM[j, 7 - a]) / 2 for a in range(4)] for j in range(4)]
DIF_PART = [[(DM[j, a] - DM[j, 7 - a]) / 2 for a in range(4)] for j in range(4)]
ROT = np.array([[DM[k, (k - r) % 8] for k in range(8)] for r in range(8)], np.float32)


def combine(coefs, items):
    total = None
    for c, x in zip(coefs, items):
        term = x * np.float32(c)
        total = term if total is None else total + term
    return total


def along_second(plane):
    even = [plane[a] + plane[7 - a] for a in range(4)]
    odd = [plane[a] - plane[7 - a] for a in range(4)]
    out = [None] * 8
    for j in range(4):
        e = combine(SUM_PART[j], even)
        o = combine(DIF_PART[j], odd)
        out[j] = o + e
        out[7 - j] = o - e
    return out


def along_third(x, rot):
    total = x * rot[0]
    for r in range(1, 8):
        total = total + pltpu.roll(x, r, 0) * rot[r]
    return total


def gather_lanes(x, idx):
    return jnp.take_along_axis(x, idx, axis=1, mode="promise_in_bounds")


def third_tables():
    lane = lax.broadcasted_iota(jnp.int32, (SUB, LANES), 1)
    k = lax.broadcasted_iota(jnp.int32, (SUB, LANES), 0)
    z = lane % EZ
    back = jnp.where(z == 0, lane + (EZ - 1), lane - 1)
    ahead = jnp.where(z == EZ - 1, lane - (EZ - 1), lane + 1)
    return jnp.where(k == 0, back, ahead), k == 0, k == ORDER


def plane_sum(plane, tables, rows=EXT):
    idx, first, last = tables
    up = plane[7] + pltpu.roll(plane[0], LANES - EZ, 1)
    plane = [pltpu.roll(up, EZ, 1)] + list(plane[1:7]) + [up]
    out = []
    for v in plane[:rows]:
        x = jnp.where(first, pltpu.roll(v, 1, 0), jnp.where(last, pltpu.roll(v, 7, 0), 0.0))
        out.append(v + gather_lanes(x, idx))
    return out


def full(rows):
    return list(rows) + [pltpu.roll(rows[0], LANES - EZ, 1)]


def write(ref, lead, plane):
    for j, v in enumerate(plane):
        ref[lead + (j,)] = v


def read(ref, *lead, rows=EXT):
    return [ref[lead + (j,)] for j in range(rows)]


def brick_index(order_ref):
    order = jnp.broadcast_to(order_ref[...], (LANES, LANES))
    pos = lax.broadcasted_iota(jnp.int32, (LANES, LANES), 0)
    hot = jnp.where(order == pos, 1.0, 0.0).astype(jnp.bfloat16)
    slot = lax.broadcasted_iota(jnp.int32, (SUB, LANES), 1).astype(jnp.float32).astype(jnp.bfloat16)
    found = lax.dot_general(
        slot, hot, (((1,), (1,)), ((), ())), preferred_element_type=jnp.float32
    )
    return found.astype(jnp.int32)


def source_plane(parity, i):
    return jnp.where(parity == 1, ORDER - i, i)


def source_plane(parity, i):
    return jnp.where(parity == 1, ORDER - i, i)


def project(weight, scal, idx, tables):
    weight = [gather_lanes(v, idx) for v in weight]
    planes = [[gather_lanes(plane[j], idx) * weight[j] for j in range(8)] for plane in scal]
    return [plane_sum(plane, tables, ROWS) for plane in planes + [weight]]


def project_odd(order_ref, scal_ref, mass_ref, od_ref, idx_ref, order_buf, scal_buf, mass_buf, sems):
    src = source_plane(lax.axis_index("elem") % 2, 0)
    copies = [pltpu.make_async_copy(order_ref, order_buf, sems.at[0])]
    copies.append(pltpu.make_async_copy(mass_ref.at[src], mass_buf, sems.at[1]))
    for m in range(2):
        copies.append(pltpu.make_async_copy(scal_ref.at[m, src], scal_buf.at[m], sems.at[2 + m]))
    for copy in copies:
        copy.start()
    tables = third_tables()
    copies[0].wait()
    idx = brick_index(order_buf)
    idx_ref[...] = idx
    for copy in copies[1:]:
        copy.wait()
    planes = project(read(mass_buf), [read(scal_buf, m) for m in range(2)], idx, tables)
    for r in range(3):
        write(od_ref, (r,), planes[r])


def signs_of(parity):
    first = jnp.where(parity == 1, time_step, -time_step).astype(jnp.float32)
    return first, np.float32(-time_step), np.float32(-time_step)


def project_even(idx_ref, scal_ref, mass_ref, tr_ref, ev_ref):
    parity = lax.axis_index("elem") % 2
    src = source_plane(parity, ORDER)
    idx = idx_ref[...]
    signs = signs_of(parity)
    planes = project(
        read(mass_ref, src), [read(scal_ref, m, src) for m in range(2)], idx, third_tables())
    planes.extend([gather_lanes(v, idx) * signs[r] for v in read(tr_ref, r, src)] for r in range(3))
    write(ev_ref, (), sum(planes, []))


def prepare(idx_ref, scal_ref, mass_ref, tr_ref,
            gi_ref, q_ref, ri_ref, rt_ref, ti_ref, tf_ref, st_ref):
    parity = lax.axis_index("elem") % 2
    idx = idx_ref[...]
    tables = third_tables()
    signs = signs_of(parity)
    for face in range(2):
        src = source_plane(parity, face * ORDER)
        first = [gather_lanes(v, idx) * signs[0] for v in read(tr_ref, 0, src)]
        write(st_ref, (face,), plane_sum(first, tables, ROWS))
        if face == 0:
            write(tf_ref, (0,), first)
            for r in (1, 2):
                write(tf_ref, (r,), [gather_lanes(v, idx) * signs[r] for v in read(tr_ref, r, src)])
    sums = [[None, None], [None, None]]
    for i in range(6):
        src = source_plane(parity, i + 1)
        for r in (1, 2):
            write(ti_ref, (i, r - 1), [gather_lanes(v, idx) * signs[r] for v in read(tr_ref, r, src)])
        first = plane_sum([gather_lanes(v, idx) * signs[0] for v in read(tr_ref, 0, src)], tables)
        weight = [gather_lanes(v, idx) for v in read(mass_ref, src)]
        inverse = [1.0 / v for v in plane_sum(weight, tables)]
        write(ri_ref, (i,), inverse)
        write(rt_ref, (i,), [first[j] * inverse[j] for j in range(8)])
        for m in range(2):
            scal = read(scal_ref, m, src)
            plane = plane_sum([gather_lanes(scal[j], idx) * weight[j] for j in range(8)], tables)
            plane = [plane[j] * inverse[j] for j in range(8)]
            write(gi_ref, (m, i), plane)
            for face in range(2):
                terms = [v * np.float32(DM[face * ORDER, i + 1]) for v in plane[:ROWS]]
                old = sums[face][m]
                sums[face][m] = [x + y for x, y in zip(old, terms)] if old else terms
    for face in range(2):
        for m in range(2):
            write(q_ref, (face, m), sums[face][m])


def rotations(rot_ref):
    return [rot_ref[r] for r in range(8)]


def in_plane(plane, second_t, third_t, rot):
    second = along_second(plane)
    return [second_t[j] * second[j] + third_t[j] * along_third(plane[j], rot) for j in range(8)]


def inner_open(gi_ref, ri_ref, rt_ref, ti_ref, rot, wp_ref):
    tables = third_tables()
    for m in range(2):
        for j in range(8):
            rows = [gi_ref[m, a, j] for a in range(6)]
            even = [rows[a] + rows[5 - a] for a in range(3)]
            odd = [rows[a] - rows[5 - a] for a in range(3)]
            for i in range(3):
                e = combine([(DM[i + 1, a + 1] + DM[i + 1, 6 - a]) / 2 for a in range(3)], even)
                o = combine([(DM[i + 1, a + 1] - DM[i + 1, 6 - a]) / 2 for a in range(3)], odd)
                wp_ref[m, i, j] = (o + e) * rt_ref[i, j]
                wp_ref[m, 5 - i, j] = (o - e) * rt_ref[5 - i, j]
    for i in range(6):
        for m in range(2):
            plane = in_plane(read(gi_ref, m, i), read(ti_ref, i, 0), read(ti_ref, i, 1), rot)
            plane = plane_sum(plane, tables)
            write(wp_ref, (m, i), [wp_ref[m, i, j] + ri_ref[i, j] * plane[j] for j in range(8)])


def inner_close(p0_ref, p7_ref, wp_ref, rt_ref, scale, put, q_ref=None):
    for m in range(2):
        p0, p7 = full(read(p0_ref, m, rows=ROWS)), full(read(p7_ref, m, rows=ROWS))
        sums = [[], []]
        for i in range(6):
            near, far = np.float32(scale * DM[i + 1, 0]), np.float32(scale * DM[i + 1, ORDER])
            kept = put(m, i, [
                wp_ref[m, i, j] * np.float32(scale) + rt_ref[i, j] * (p0[j] * near + p7[j] * far)
                for j in range(8)
            ])
            for face in range(2):
                terms = [v * np.float32(DM[face * ORDER, i + 1]) for v in kept[:ROWS]]
                sums[face] = [x + y for x, y in zip(sums[face], terms)] if i else terms
        if q_ref is not None:
            for face in range(2):
                write(q_ref, (face, m), sums[face])


def own_terms(p_ref, a_ref, rf_ref, face, rot, tables, e_ref):
    second_t, third_t = read(a_ref, 0), read(a_ref, 1)
    for m in range(2):
        p = full(read(p_ref, m, rows=ROWS))
        plane = plane_sum(in_plane(p, second_t, third_t, rot), tables, ROWS)
        write(e_ref, (m,), [
            rf_ref[j] * (plane[j] + a_ref[2, j] * (p[j] * np.float32(DM[face * ORDER, face * ORDER])))
            for j in range(ROWS)
        ])


def both_sides(own, got, tables, a_ref):
    total = [[own[r][j] + got[r][j] for j in range(8)] for r in range(3)]
    write(a_ref, (0,), total[1])
    write(a_ref, (1,), total[2])
    write(a_ref, (2,), plane_sum(total[0], tables, ROWS))


def transports(ref, start):
    return [[ref[start + 8 * r + j] for j in range(8)] for r in range(3)]


def make_field_face(face, carry):
    far = np.float32(DM[ORDER - face * ORDER, face * ORDER])

    def field_face(own_ref, got_ref, q_ref, st_ref, *refs):
        tf_ref = refs[0] if carry else None
        p_ref, rf_ref, send_ref = refs[-3:]
        inverse = [1.0 / (own_ref[14 + j] + got_ref[14 + j]) for j in range(ROWS)]
        p = [
            [(own_ref[ROWS * m + j] + got_ref[ROWS * m + j]) * inverse[j] for j in range(ROWS)]
            for m in range(2)
        ]
        sent = [
            [st_ref[1 - face, j] * (q_ref[1 - face, m, j] + p[m][j] * far) for j in range(ROWS)]
            for m in range(2)
        ]
        write(send_ref, (), sent[0] + sent[1])
        for m in range(2):
            write(p_ref, (m,), p[m])
        write(rf_ref, (), inverse)
        if carry:
            for r in range(3):
                for j in range(8):
                    send_ref[2 * ROWS + 8 * r + j] = tf_ref[r, j]

    return field_face


def make_stage_face(face, scale, total, raw, early):
    far = np.float32(DM[ORDER - face * ORDER, face * ORDER])
    scale = np.float32(scale)

    def stage_face(*refs):
        own_ref, got_ref, e_ref, acc_ref, q_ref, rt_ref, rf_ref = refs[:7]
        if early:
            tf_ref, rot_ref, p_ref, send_ref, a_ref, e_buf = refs[7:]
            tables = third_tables()
            both_sides([read(tf_ref, r) for r in range(3)], transports(got_ref, 2 * ROWS), tables, a_ref)
            own_terms(e_ref, a_ref, rf_ref, face, rotations(rot_ref), tables, e_buf)
            e_ref = e_buf
        else:
            p_ref, send_ref = refs[7:]
        p = []
        for m in range(2):
            value = [own_ref[ROWS * m + j] + got_ref[ROWS * m + j] for j in range(ROWS)]
            if raw:
                value = [value[j] * rf_ref[j] for j in range(ROWS)]
            value = [(value[j] + e_ref[m, j]) * scale for j in range(ROWS)]
            if total:
                value = [value[j] + acc_ref[face, m, j] for j in range(ROWS)]
            p.append(value)
        sent = [
            [rt_ref[1 - face, j] * (q_ref[1 - face, m, j] + p[m][j] * far) for j in range(ROWS)]
            for m in range(2)
        ]
        write(send_ref, (), sent[0] + sent[1])
        for m in range(2):
            write(p_ref, (m,), p[m])

    return stage_face


def make_first_inner(scale, opening, start):
    def first_inner(*refs):
        p0_ref, p7_ref, gi_ref, acci_ref, wp_ref, rt_ref, r7_ref, rot_ref = refs[:8]
        tables = third_tables()
        if start:
            ev_ref, rev_ref, st_ref, r0_ref = refs[8:12]
            gn_ref, an_ref, q_ref, e7_ref, a7_ref, rs_ref = refs[12:]
            both_sides(transports(ev_ref, 3 * ROWS), transports(rev_ref, 3 * ROWS), tables, a7_ref)
            write(rs_ref, (0,), [st_ref[0, j] * r0_ref[j] for j in range(ROWS)])
            write(rs_ref, (1,), [st_ref[1, j] * r7_ref[j] for j in range(ROWS)])
        else:
            a7_ref = refs[8]
            gn_ref, an_ref, q_ref, e7_ref = refs[9:]
        own_terms(p7_ref, a7_ref, r7_ref, 1, rotations(rot_ref), tables, e7_ref)

        def put(m, i, value):
            base = gi_ref if opening else acci_ref
            write(gn_ref, (m, i), value)
            write(an_ref, (m, i), [base[m, i, j] + value[j] for j in range(8)])
            return value

        inner_close(p0_ref, p7_ref, wp_ref, rt_ref, scale, put, q_ref)

    return first_inner


def make_between(early):
    def between(*refs):
        m7_ref, gi_ref, a7_ref, r7_ref, ri_ref, rt_ref, ti_ref, rot_ref = refs[:8]
        rot = rotations(rot_ref)
        tables = third_tables()
        if early:
            wp_ref, e7_ref = refs[8:]
        else:
            p0_ref, a0_ref, r0_ref, wp_ref, e7_ref, e0_ref = refs[8:]
            own_terms(p0_ref, a0_ref, r0_ref, 0, rot, tables, e0_ref)
        own_terms(m7_ref, a7_ref, r7_ref, 1, rot, tables, e7_ref)
        inner_open(gi_ref, ri_ref, rt_ref, ti_ref, rot, wp_ref)

    return between


def face_totals(now, before, accf_ref, afn_ref, opening):
    for face in range(2):
        for m in range(2):
            for j in range(ROWS):
                value = now[face][m, j] + before[face][m, j]
                afn_ref[face, m, j] = value if opening else value + accf_ref[face, m, j]


def make_second_inner(scale, opening, closing):
    def second_inner(m0_ref, m7_ref, p0_ref, p7_ref, accf_ref, acci_ref, wp_ref, ri_ref, rt_ref,
                     ti_ref, a0_ref, r0_ref, rot_ref, gn_ref, q_ref, an_ref, afn_ref, wn_ref, e0_ref):
        rot = rotations(rot_ref)

        def put(m, i, value):
            total = [acci_ref[m, i, j] + value[j] for j in range(8)]
            kept = total if closing else value
            write(gn_ref, (m, i), kept)
            if not closing:
                write(an_ref, (m, i), total)
            return kept

        inner_close(m0_ref, m7_ref, wp_ref, rt_ref, scale, put, q_ref)
        own_terms(m0_ref, a0_ref, r0_ref, 0, rot, third_tables(), e0_ref)
        face_totals((m0_ref, m7_ref), (p0_ref, p7_ref), accf_ref, afn_ref, opening)
        inner_open(gn_ref, ri_ref, rt_ref, ti_ref, rot, wn_ref)

    return second_inner


def make_last_inner(scale):
    def last_inner(order_ref, m0_ref, m7_ref, p0_ref, p7_ref, accf_ref, acci_ref, wp_ref, rt_ref,
                   a0_ref, r0_ref, rot_ref, out_ref, afn_ref, e0_ref, buf, sems):
        parity = lax.axis_index("elem") % 2
        idx = jnp.broadcast_to(order_ref[...], (SUB, LANES))

        def put(m, i, value):
            total = [acci_ref[m, i, j] + value[j] for j in range(8)]
            dst = source_plane(parity, i + 1) - 1
            write(buf, (m, dst), [gather_lanes(v, idx) for v in total])
            return total

        inner_close(m0_ref, m7_ref, wp_ref, rt_ref, scale, put)
        copies = [
            pltpu.make_async_copy(buf.at[m], out_ref.at[m, pl.ds(1, 6)], sems.at[m])
            for m in range(2)
        ]
        for copy in copies:
            copy.start()
        own_terms(m0_ref, a0_ref, r0_ref, 0, rotations(rot_ref), third_tables(), e0_ref)
        face_totals((m0_ref, m7_ref), (p0_ref, p7_ref), accf_ref, afn_ref, False)
        for copy in copies:
            copy.wait()

    return last_inner


def final_face(face, scale, order_ref, own_ref, got_ref, e_ref, accf_ref, m):
    idx = jnp.broadcast_to(order_ref[...], (SUB, LANES))
    rows = [
        (own_ref[ROWS * m + j] + got_ref[ROWS * m + j] + e_ref[m, j]) * np.float32(scale)
        + accf_ref[face, m, j]
        for j in range(ROWS)
    ]
    return [gather_lanes(v, idx) for v in full(rows)]


def make_finish_near(face, scale):
    def finish_near(order_ref, own_ref, got_ref, e_ref, accf_ref, face_ref):
        for m in range(2):
            write(face_ref, (m,), final_face(face, scale, order_ref, own_ref, got_ref, e_ref, accf_ref, m))

    return finish_near


def make_finish_far(face, scale):
    def finish_far(order_ref, own_ref, got_ref, e_ref, accf_ref, near_ref, part_ref,
                   out_ref, buf, sems):
        dst = source_plane(lax.axis_index("elem") % 2, face * ORDER)
        copies = []
        for m in range(2):
            copies.append(
                pltpu.make_async_copy(near_ref.at[m], out_ref.at[m, ORDER - dst], sems.at[1, m])
            )
            copies[-1].start()
        for m in range(2):
            write(buf, (m,), final_face(face, scale, order_ref, own_ref, got_ref, e_ref, accf_ref, m))
            copies.append(pltpu.make_async_copy(buf.at[m], out_ref.at[m, dst], sems.at[0, m]))
            copies[-1].start()
        for copy in copies:
            copy.wait()

    return finish_far


VM = pl.BlockSpec(memory_space=pltpu.VMEM)
HB = pl.BlockSpec(memory_space=pltpu.HBM)


def call(kernel, outs, args, name, cost, hbm=(), hbm_out=(), scratch=(), alias={}):
    specs = [HB if n in hbm else VM for n in range(len(args))]
    out_specs = [HB if n in hbm_out else VM for n in range(len(outs))]
    shapes = [jax.ShapeDtypeStruct(s, jnp.int32 if s == (SUB, LANES) else jnp.float32) for s in outs]
    single = len(outs) == 1
    return pl.pallas_call(
        kernel,
        out_shape=shapes[0] if single else shapes,
        in_specs=specs,
        out_specs=out_specs[0] if single else out_specs,
        scratch_shapes=list(scratch),
        input_output_aliases=alias,
        name=name,
        compiler_params=pltpu.CompilerParams(vmem_limit_bytes=8 << 20),
        cost_estimate=pl.CostEstimate(
            flops=cost * 1000000, bytes_accessed=1 << 10, transcendentals=0
        ),
    )(*args)


def per_device(scalars, transport, mass, element_order):
    count = lax.axis_size("elem")
    even_pairs = [(i, i ^ 1) for i in range(count)]
    odd_pairs = [(i, (i + 1) % count if i % 2 else (i - 1) % count) for i in range(count)]
    swap_od = lambda x: lax.ppermute(x, "elem", odd_pairs)
    swap_ev = lambda x: lax.ppermute(x, "elem", even_pairs)
    rot = jnp.asarray(np.broadcast_to(ROT[:, :, None], (8, SUB, LANES)))
    members = scalars.shape[0]
    grid = (EXT, EXT, SUB, LANES)
    scal = scalars.reshape((members,) + grid)
    tr = transport.reshape((3,) + grid)
    mas = mass.reshape(grid)
    tile, part = (EXT, SUB, LANES), (ROWS, SUB, LANES)
    inner, face, faces = (2, 6) + tile, (2,) + part, (2, 2) + part
    sent, geometry = (2 * ROWS, SUB, LANES), (3,) + tile
    f32 = jnp.float32

    stay = lambda x: pltpu.with_memory_space_constraint(x, pltpu.HBM)
    od, idx = call(
        project_odd, [(3,) + part, (SUB, LANES)], (stay(element_order), stay(scal), stay(mas)), "project", 1,
        hbm=(0, 1, 2),
        scratch=[pltpu.VMEM((1, LANES), jnp.int32), pltpu.VMEM((2,) + tile, f32),
                 pltpu.VMEM(tile, f32), pltpu.SemaphoreType.DMA((4,))])
    od = od.reshape(3 * ROWS, SUB, LANES)
    rod = swap_od(od)
    ev = call(
        project_even, [(3 * ROWS + 24, SUB, LANES)], (idx, scal, mas, tr), "project", 1)
    rev = swap_ev(ev)
    gi, q, ri, rt, ti, tf, st = call(
        prepare,
        [inner, faces, (6,) + tile, (6,) + tile, (6, 2) + tile, geometry, (2,) + part],
        (idx, scal, mas, tr), "prepare", 1)

    def opening_terms(gi_ref, ri_ref, rt_ref, ti_ref, rot_ref, wp_ref):
        inner_open(gi_ref, ri_ref, rt_ref, ti_ref, rotations(rot_ref), wp_ref)

    wp = call(opening_terms, [inner], (gi, ri, rt, ti, rot), "terms", 1)
    p0, r0, cev = call(
        make_field_face(0, False), [face, part, sent], (od, rod, q, st), "odd", 3000)
    p7, r7, cod = call(
        make_field_face(1, True), [face, part, (2 * ROWS + 24, SUB, LANES)],
        (ev, rev, q, st, tf), "even", 1)
    acci, accf = gi, q
    pairs = SUBSTEPS * STAGES // 2
    for n in range(pairs):
        s = 2 * n % STAGES + 1
        opening, closing, early = s == 1, s + 1 == STAGES, n == 0
        got_ev, got_od = swap_ev(cev), swap_od(cod)
        extra = (ev, rev, st, r0) if early else (a7,)
        res = call(
            make_first_inner(1.0 / s, opening, early),
            [inner, inner, faces, face] + ([geometry, (2,) + part] if early else []),
            (p0, p7, gi, acci, wp, rt, r7, rot) + extra, "first", 1000)
        gm, acci, q, e7 = res[:4]
        if early:
            a7, rs = res[4:]
        m7, cod2 = call(
            make_stage_face(1, 1.0 / s, False, early, False), [face, sent],
            (cev, got_ev, e7, accf, q, rs, r7), "ahead", 1)
        got_od2 = swap_od(cod2)
        res = call(
            make_between(early), [inner, face] + ([] if early else [face]),
            (m7, gm, a7, r7, ri, rt, ti, rot) + (() if early else (p0, a0, r0)), "between", 2000)
        wp, e7 = res[:2]
        if early:
            m0, cev2, a0 = call(
                make_stage_face(0, 1.0 / s, False, True, True), [face, sent, geometry],
                (cod, got_od, p0, accf, q, rs, r0, tf, rot), "behind", 1,
                scratch=[pltpu.VMEM(face, f32)])
        else:
            m0, cev2 = call(
                make_stage_face(0, 1.0 / s, False, False, False), [face, sent],
                (cod, got_od, res[2], accf, q, rs, r0), "behind", 1)
        got_ev2 = swap_ev(cev2)
        scale = 1.0 / (s + 1)
        if n < pairs - 1:
            gi, q, acci, accf, wp, e0 = call(
                make_second_inner(scale, opening, closing),
                [inner, faces, inner, faces, inner, face],
                (m0, m7, p0, p7, accf, acci, wp, ri, rt, ti, a0, r0, rot), "second", 3000)
            p0, cev = call(
                make_stage_face(0, scale, closing, False, False), [face, sent],
                (cod2, got_od2, e0, accf, q, rs, r0), "odd", 3000)
            p7, cod = call(
                make_stage_face(1, scale, closing, False, False), [face, sent],
                (cev2, got_ev2, e7, accf, q, rs, r7), "even", 1)
        else:
            out, accf, e0 = call(
                make_last_inner(scale), [(members,) + grid, faces, face],
                (element_order, m0, m7, p0, p7, accf, acci, wp, rt, a0, r0, rot), "last", 3000,
                hbm_out=(0,), scratch=[pltpu.VMEM(inner, f32), pltpu.SemaphoreType.DMA((2,))])
            near = call(
                make_finish_near(0, scale), [(2,) + tile],
                (element_order, cod2, got_od2, e0, accf), "finish", 3000)
            out = call(
                make_finish_far(1, scale), [(members,) + grid],
                (element_order, cev2, got_ev2, e7, accf, near, out), "finish", 1,
                hbm=(6,), hbm_out=(0,), alias={6: 0},
                scratch=[pltpu.VMEM((2,) + tile, f32), pltpu.SemaphoreType.DMA((2, 2))])
    return out.reshape(scalars.shape)


def solution(mesh):
    in_specs = (P("ens", None, "elem"), P(None, None, "elem"), P(None, "elem"), P("elem", None))
    out_specs = P("ens", None, "elem")
    return jax.shard_map(
        per_device, mesh=mesh, in_specs=in_specs, out_specs=out_specs, check_vma=False
    )
```

```python
import jax
import jax.numpy as jnp
import numpy as np
from jax import lax
from jax.experimental import pallas as pl
from jax.experimental.pallas import tpu as pltpu
from jax.sharding import PartitionSpec as P

ORDER = 7
EXT = ORDER + 1
SUBSTEPS = 2
STAGES = 4
EY = 8
EZ = 16
LANES = EY * EZ
SUB = 8
ROWS = 7

time_step = 0.015


def legendre_table(points, degree):
    table = np.zeros((points.shape[0], degree + 1))
    table[:, 0] = 1.0
    table[:, 1] = points
    for level in range(2, degree + 1):
        table[:, level] = (
            (2 * level - 1) * points * table[:, level - 1] - (level - 1) * table[:, level - 2]
        ) / level
    return table


def gll_derivative(degree):
    extent = degree + 1
    points = np.cos(np.pi * np.arange(extent) / degree)
    for sweep in range(60):
        table = legendre_table(points, degree)
        points = points - (points * table[:, degree] - table[:, degree - 1]) / (
            extent * table[:, degree]
        )
    points = points[::-1].copy()
    values = legendre_table(points, degree)[:, degree]
    matrix = np.zeros((extent, extent))
    for target in range(extent):
        for source in range(extent):
            if target != source:
                matrix[target, source] = values[target] / (
                    values[source] * (points[target] - points[source])
                )
    matrix[0, 0] = -degree * (degree + 1) / 4.0
    matrix[extent - 1, extent - 1] = degree * (degree + 1) / 4.0
    return matrix


DM = gll_derivative(ORDER)
SUM_PART = [[(DM[j, a] + DM[j, 7 - a]) / 2 for a in range(4)] for j in range(4)]
DIF_PART = [[(DM[j, a] - DM[j, 7 - a]) / 2 for a in range(4)] for j in range(4)]


def combine(coefs, items):
    total = None
    for c, x in zip(coefs, items):
        term = x * np.float32(c)
        total = term if total is None else total + term
    return total


def along_second(plane):
    even = [plane[a] + plane[7 - a] for a in range(4)]
    odd = [plane[a] - plane[7 - a] for a in range(4)]
    out = [None] * 8
    for j in range(4):
        e = combine(SUM_PART[j], even)
        o = combine(DIF_PART[j], odd)
        out[j] = o + e
        out[7 - j] = o - e
    return out


def along_third(x, rot):
    total = x * rot[0]
    for r in range(1, 8):
        total = total + pltpu.roll(x, r, 0) * rot[r]
    return total


def gather_lanes(x, idx):
    return jnp.take_along_axis(x, idx, axis=1, mode="promise_in_bounds")


def third_tables():
    lane = lax.broadcasted_iota(jnp.int32, (SUB, LANES), 1)
    k = lax.broadcasted_iota(jnp.int32, (SUB, LANES), 0)
    z = lane % EZ
    back = jnp.where(z == 0, lane + (EZ - 1), lane - 1)
    ahead = jnp.where(z == EZ - 1, lane - (EZ - 1), lane + 1)
    return jnp.where(k == 0, back, ahead), k == 0, k == ORDER


def plane_sum(plane, tables, rows=EXT):
    idx, first, last = tables
    up = plane[7] + pltpu.roll(plane[0], LANES - EZ, 1)
    plane = [pltpu.roll(up, EZ, 1)] + list(plane[1:7]) + [up]
    out = []
    for v in plane[:rows]:
        x = jnp.where(first, pltpu.roll(v, 1, 0), jnp.where(last, pltpu.roll(v, 7, 0), 0.0))
        out.append(v + gather_lanes(x, idx))
    return out


def full(rows):
    return list(rows) + [pltpu.roll(rows[0], LANES - EZ, 1)]


def write(ref, lead, plane):
    for j, v in enumerate(plane):
        ref[lead + (j,)] = v


def read(ref, *lead, rows=EXT):
    return [ref[lead + (j,)] for j in range(rows)]


def brick_index(order_ref):
    order = jnp.broadcast_to(order_ref[...], (LANES, LANES))
    pos = lax.broadcasted_iota(jnp.int32, (LANES, LANES), 0)
    hot = jnp.where(order == pos, 1.0, 0.0).astype(jnp.bfloat16)
    slot = lax.broadcasted_iota(jnp.int32, (SUB, LANES), 1).astype(jnp.float32).astype(jnp.bfloat16)
    found = lax.dot_general(
        slot, hot, (((1,), (1,)), ((), ())), preferred_element_type=jnp.float32
    )
    return found.astype(jnp.int32)


def source_plane(parity, i):
    return jnp.where(parity == 1, ORDER - i, i)


def source_plane(parity, i):
    return jnp.where(parity == 1, ORDER - i, i)


def project(weight, scal, idx, tables):
    weight = [gather_lanes(v, idx) for v in weight]
    planes = [[gather_lanes(plane[j], idx) * weight[j] for j in range(8)] for plane in scal]
    return [plane_sum(plane, tables, ROWS) for plane in planes + [weight]]


def project_odd(order_ref, scal_ref, mass_ref, tr_ref, od_ref, idx_ref, slot_ref, far_ref,
                order_buf, near_buf, sems):
    parity = lax.axis_index("elem") % 2
    near, far = source_plane(parity, 0), source_plane(parity, ORDER)
    copies = [pltpu.make_async_copy(order_ref, order_buf, sems.at[0])]
    for r, source in enumerate((scal_ref.at[0, near], scal_ref.at[1, near], mass_ref.at[near])):
        copies.append(pltpu.make_async_copy(source, near_buf.at[r], sems.at[1 + r]))
    late = []
    sources = [scal_ref.at[0, far], scal_ref.at[1, far], mass_ref.at[far]]
    sources += [tr_ref.at[r, far] for r in range(3)]
    for r, source in enumerate(sources):
        late.append(pltpu.make_async_copy(source, far_ref.at[r], sems.at[4 + r]))
    for copy in copies + late:
        copy.start()
    tables = third_tables()
    copies[0].wait()
    idx = brick_index(order_buf)
    idx_ref[...] = idx
    slot_ref[...] = jnp.broadcast_to(order_buf[...], (SUB, LANES))
    for copy in copies[1:]:
        copy.wait()
    planes = project(read(near_buf, 2), [read(near_buf, m) for m in range(2)], idx, tables)
    for r in range(3):
        write(od_ref, (r,), planes[r])
    for copy in late:
        copy.wait()


def signs_of(parity):
    first = jnp.where(parity == 1, time_step, -time_step).astype(jnp.float32)
    return first, np.float32(-time_step), np.float32(-time_step)


def project_even(idx_ref, far_ref, ev_ref):
    idx = idx_ref[...]
    signs = signs_of(lax.axis_index("elem") % 2)
    planes = project(read(far_ref, 2), [read(far_ref, m) for m in range(2)], idx, third_tables())
    planes.extend(
        [gather_lanes(v, idx) * signs[r] for v in read(far_ref, 3 + r)] for r in range(3))
    write(ev_ref, (), sum(planes, []))


def prepare(idx_ref, scal_ref, mass_ref, tr_ref,
            gi_ref, q_ref, ri_ref, rt_ref, ti_ref, tf_ref, st_ref):
    parity = lax.axis_index("elem") % 2
    idx = idx_ref[...]
    tables = third_tables()
    signs = signs_of(parity)

    def load(i):
        src = source_plane(parity, i)
        planes = [read(scal_ref, m, src) for m in range(2)] + [read(mass_ref, src)]
        return planes + [read(tr_ref, r, src) for r in range(3)]

    near, far = source_plane(parity, 0), source_plane(parity, ORDER)
    faces = [read(tr_ref, r, near) for r in range(3)] + [read(tr_ref, 0, far)]
    faces = [
        [gather_lanes(v, idx) * signs[r] for v in plane] for r, plane in zip((0, 1, 2, 0), faces)
    ]
    assembled = [plane_sum(faces[0], tables, ROWS), plane_sum(faces[3], tables, ROWS)]
    ahead = load(1)
    for r in range(3):
        write(tf_ref, (r,), faces[r])
    for face in range(2):
        write(st_ref, (face,), assembled[face])
    sums = [[None, None], [None, None]]
    for i in range(6):
        raw = [[gather_lanes(v, idx) for v in plane] for plane in ahead]
        weight = raw[2]
        first = plane_sum([v * signs[0] for v in raw[3]], tables)
        inverse = [1.0 / v for v in plane_sum(weight, tables)]
        rest = [[v * signs[r] for v in raw[3 + r]] for r in (1, 2)]
        planes = []
        for m in range(2):
            plane = plane_sum([raw[m][j] * weight[j] for j in range(8)], tables)
            planes.append([plane[j] * inverse[j] for j in range(8)])
        if i < 5:
            ahead = load(i + 2)
        for r in range(2):
            write(ti_ref, (i, r), rest[r])
        write(ri_ref, (i,), inverse)
        write(rt_ref, (i,), [first[j] * inverse[j] for j in range(8)])
        for m in range(2):
            write(gi_ref, (m, i), planes[m])
            for face in range(2):
                terms = [v * np.float32(DM[face * ORDER, i + 1]) for v in planes[m][:ROWS]]
                old = sums[face][m]
                sums[face][m] = [x + y for x, y in zip(old, terms)] if old else terms
    for face in range(2):
        for m in range(2):
            write(q_ref, (face, m), sums[face][m])


def rotations():
    k = lax.broadcasted_iota(jnp.int32, (SUB, LANES), 0)
    out = []
    for r in range(8):
        value = jnp.full((SUB, LANES), np.float32(DM[7, (7 - r) % 8]))
        for row in range(7):
            value = jnp.where(k == row, np.float32(DM[row, (row - r) % 8]), value)
        out.append(value)
    return out


def in_plane(plane, second_t, third_t, rot):
    second = along_second(plane)
    return [second_t[j] * second[j] + third_t[j] * along_third(plane[j], rot) for j in range(8)]


def inner_open(gi_ref, ri_ref, rt_ref, ti_ref, rot, wp_ref):
    tables = third_tables()
    for m in range(2):
        for j in range(8):
            rows = [gi_ref[m, a, j] for a in range(6)]
            even = [rows[a] + rows[5 - a] for a in range(3)]
            odd = [rows[a] - rows[5 - a] for a in range(3)]
            for i in range(3):
                e = combine([(DM[i + 1, a + 1] + DM[i + 1, 6 - a]) / 2 for a in range(3)], even)
                o = combine([(DM[i + 1, a + 1] - DM[i + 1, 6 - a]) / 2 for a in range(3)], odd)
                wp_ref[m, i, j] = (o + e) * rt_ref[i, j]
                wp_ref[m, 5 - i, j] = (o - e) * rt_ref[5 - i, j]
    for i in range(6):
        for m in range(2):
            plane = in_plane(read(gi_ref, m, i), read(ti_ref, i, 0), read(ti_ref, i, 1), rot)
            plane = plane_sum(plane, tables)
            write(wp_ref, (m, i), [wp_ref[m, i, j] + ri_ref[i, j] * plane[j] for j in range(8)])


def inner_close(p0_ref, p7_ref, wp_ref, rt_ref, scale, put, q_ref=None):
    for m in range(2):
        p0, p7 = full(read(p0_ref, m, rows=ROWS)), full(read(p7_ref, m, rows=ROWS))
        sums = [[], []]
        for i in range(6):
            near, far = np.float32(scale * DM[i + 1, 0]), np.float32(scale * DM[i + 1, ORDER])
            kept = put(m, i, [
                wp_ref[m, i, j] * np.float32(scale) + rt_ref[i, j] * (p0[j] * near + p7[j] * far)
                for j in range(8)
            ])
            for face in range(2):
                terms = [v * np.float32(DM[face * ORDER, i + 1]) for v in kept[:ROWS]]
                sums[face] = [x + y for x, y in zip(sums[face], terms)] if i else terms
        if q_ref is not None:
            for face in range(2):
                write(q_ref, (face, m), sums[face])


def own_terms(p_ref, a_ref, rf_ref, face, rot, tables, e_ref):
    second_t, third_t = read(a_ref, 0), read(a_ref, 1)
    for m in range(2):
        p = full(read(p_ref, m, rows=ROWS))
        plane = plane_sum(in_plane(p, second_t, third_t, rot), tables, ROWS)
        write(e_ref, (m,), [
            rf_ref[j] * (plane[j] + a_ref[2, j] * (p[j] * np.float32(DM[face * ORDER, face * ORDER])))
            for j in range(ROWS)
        ])


def both_sides(own, got, tables, a_ref):
    total = [[own[r][j] + got[r][j] for j in range(8)] for r in range(3)]
    write(a_ref, (0,), total[1])
    write(a_ref, (1,), total[2])
    write(a_ref, (2,), plane_sum(total[0], tables, ROWS))


def transports(ref, start):
    return [[ref[start + 8 * r + j] for j in range(8)] for r in range(3)]


def make_field_face(face, carry):
    far = np.float32(DM[ORDER - face * ORDER, face * ORDER])

    def field_face(own_ref, got_ref, q_ref, st_ref, *refs):
        tf_ref = refs[0] if carry else None
        p_ref, rf_ref, send_ref = refs[-3:]
        inverse = [1.0 / (own_ref[14 + j] + got_ref[14 + j]) for j in range(ROWS)]
        p = [
            [(own_ref[ROWS * m + j] + got_ref[ROWS * m + j]) * inverse[j] for j in range(ROWS)]
            for m in range(2)
        ]
        sent = [
            [st_ref[1 - face, j] * (q_ref[1 - face, m, j] + p[m][j] * far) for j in range(ROWS)]
            for m in range(2)
        ]
        write(send_ref, (), sent[0] + sent[1])
        for m in range(2):
            write(p_ref, (m,), p[m])
        write(rf_ref, (), inverse)
        if carry:
            for r in range(3):
                for j in range(8):
                    send_ref[2 * ROWS + 8 * r + j] = tf_ref[r, j]

    return field_face


def make_stage_face(face, scale, total, raw, early):
    far = np.float32(DM[ORDER - face * ORDER, face * ORDER])
    scale = np.float32(scale)

    def stage_face(*refs):
        own_ref, got_ref, e_ref, acc_ref, q_ref, rt_ref, rf_ref = refs[:7]
        if early:
            tf_ref, p_ref, send_ref, a_ref, e_buf = refs[7:]
            tables = third_tables()
            both_sides([read(tf_ref, r) for r in range(3)], transports(got_ref, 2 * ROWS), tables, a_ref)
            own_terms(e_ref, a_ref, rf_ref, face, rotations(), tables, e_buf)
            e_ref = e_buf
        else:
            p_ref, send_ref = refs[7:]
        p = []
        for m in range(2):
            value = [own_ref[ROWS * m + j] + got_ref[ROWS * m + j] for j in range(ROWS)]
            if raw:
                value = [value[j] * rf_ref[j] for j in range(ROWS)]
            value = [(value[j] + e_ref[m, j]) * scale for j in range(ROWS)]
            if total:
                value = [value[j] + acc_ref[face, m, j] for j in range(ROWS)]
            p.append(value)
        sent = [
            [rt_ref[1 - face, j] * (q_ref[1 - face, m, j] + p[m][j] * far) for j in range(ROWS)]
            for m in range(2)
        ]
        write(send_ref, (), sent[0] + sent[1])
        for m in range(2):
            write(p_ref, (m,), p[m])

    return stage_face


def make_first_inner(scale, opening, start):
    def first_inner(*refs):
        p0_ref, p7_ref, gi_ref, acci_ref, wp_ref, rt_ref, r7_ref = refs[:7]
        tables = third_tables()
        if start:
            ev_ref, rev_ref, st_ref, r0_ref = refs[7:11]
            gn_ref, an_ref, q_ref, e7_ref, a7_ref, rs_ref = refs[11:]
            both_sides(transports(ev_ref, 3 * ROWS), transports(rev_ref, 3 * ROWS), tables, a7_ref)
            write(rs_ref, (0,), [st_ref[0, j] * r0_ref[j] for j in range(ROWS)])
            write(rs_ref, (1,), [st_ref[1, j] * r7_ref[j] for j in range(ROWS)])
        else:
            a7_ref = refs[7]
            gn_ref, an_ref, q_ref, e7_ref = refs[8:]
        own_terms(p7_ref, a7_ref, r7_ref, 1, rotations(), tables, e7_ref)

        def put(m, i, value):
            base = gi_ref if opening else acci_ref
            write(gn_ref, (m, i), value)
            write(an_ref, (m, i), [base[m, i, j] + value[j] for j in range(8)])
            return value

        inner_close(p0_ref, p7_ref, wp_ref, rt_ref, scale, put, q_ref)

    return first_inner


def make_between(early):
    def between(*refs):
        m7_ref, gi_ref, a7_ref, r7_ref, ri_ref, rt_ref, ti_ref = refs[:7]
        rot = rotations()
        tables = third_tables()
        if early:
            wp_ref, e7_ref = refs[7:]
        else:
            p0_ref, a0_ref, r0_ref, wp_ref, e7_ref, e0_ref = refs[7:]
            own_terms(p0_ref, a0_ref, r0_ref, 0, rot, tables, e0_ref)
        own_terms(m7_ref, a7_ref, r7_ref, 1, rot, tables, e7_ref)
        inner_open(gi_ref, ri_ref, rt_ref, ti_ref, rot, wp_ref)

    return between


def face_totals(now, before, accf_ref, afn_ref, opening):
    for face in range(2):
        for m in range(2):
            for j in range(ROWS):
                value = now[face][m, j] + before[face][m, j]
                afn_ref[face, m, j] = value if opening else value + accf_ref[face, m, j]


def make_second_inner(scale, opening, closing):
    def second_inner(m0_ref, m7_ref, p0_ref, p7_ref, accf_ref, acci_ref, wp_ref, ri_ref, rt_ref,
                     ti_ref, a0_ref, r0_ref, gn_ref, q_ref, an_ref, afn_ref, wn_ref, e0_ref):
        rot = rotations()

        def put(m, i, value):
            total = [acci_ref[m, i, j] + value[j] for j in range(8)]
            kept = total if closing else value
            write(gn_ref, (m, i), kept)
            if not closing:
                write(an_ref, (m, i), total)
            return kept

        inner_close(m0_ref, m7_ref, wp_ref, rt_ref, scale, put, q_ref)
        own_terms(m0_ref, a0_ref, r0_ref, 0, rot, third_tables(), e0_ref)
        face_totals((m0_ref, m7_ref), (p0_ref, p7_ref), accf_ref, afn_ref, opening)
        inner_open(gn_ref, ri_ref, rt_ref, ti_ref, rot, wn_ref)

    return second_inner


def make_last_inner(scale):
    def last_inner(slot_ref, m0_ref, m7_ref, p0_ref, p7_ref, accf_ref, acci_ref, wp_ref, rt_ref,
                   a0_ref, r0_ref, out_ref, afn_ref, e0_ref, buf, sems):
        parity = lax.axis_index("elem") % 2
        idx = slot_ref[...]

        def put(m, i, value):
            total = [acci_ref[m, i, j] + value[j] for j in range(8)]
            dst = source_plane(parity, i + 1) - 1
            write(buf, (m, dst), [gather_lanes(v, idx) for v in total])
            return total

        inner_close(m0_ref, m7_ref, wp_ref, rt_ref, scale, put)
        copies = [
            pltpu.make_async_copy(buf.at[m], out_ref.at[m, pl.ds(1, 6)], sems.at[m])
            for m in range(2)
        ]
        for copy in copies:
            copy.start()
        own_terms(m0_ref, a0_ref, r0_ref, 0, rotations(), third_tables(), e0_ref)
        face_totals((m0_ref, m7_ref), (p0_ref, p7_ref), accf_ref, afn_ref, False)
        for copy in copies:
            copy.wait()

    return last_inner


def final_face(face, scale, slot_ref, own_ref, got_ref, e_ref, accf_ref, m):
    idx = slot_ref[...]
    rows = [
        (own_ref[ROWS * m + j] + got_ref[ROWS * m + j] + e_ref[m, j]) * np.float32(scale)
        + accf_ref[face, m, j]
        for j in range(ROWS)
    ]
    return [gather_lanes(v, idx) for v in full(rows)]


def make_finish_near(face, scale):
    def finish_near(slot_ref, own_ref, got_ref, e_ref, accf_ref, face_ref):
        for m in range(2):
            write(face_ref, (m,), final_face(face, scale, slot_ref, own_ref, got_ref, e_ref, accf_ref, m))

    return finish_near


def make_finish_far(face, scale):
    def finish_far(slot_ref, own_ref, got_ref, e_ref, accf_ref, near_ref, part_ref,
                   out_ref, buf, sems):
        dst = source_plane(lax.axis_index("elem") % 2, face * ORDER)
        copies = []
        for m in range(2):
            copies.append(
                pltpu.make_async_copy(near_ref.at[m], out_ref.at[m, ORDER - dst], sems.at[1, m])
            )
            copies[-1].start()
        for m in range(2):
            write(buf, (m,), final_face(face, scale, slot_ref, own_ref, got_ref, e_ref, accf_ref, m))
            copies.append(pltpu.make_async_copy(buf.at[m], out_ref.at[m, dst], sems.at[0, m]))
            copies[-1].start()
        for copy in copies:
            copy.wait()

    return finish_far


VM = pl.BlockSpec(memory_space=pltpu.VMEM)
HB = pl.BlockSpec(memory_space=pltpu.HBM)


def call(kernel, outs, args, name, cost, hbm=(), hbm_out=(), scratch=(), alias={}):
    specs = [HB if n in hbm else VM for n in range(len(args))]
    out_specs = [HB if n in hbm_out else VM for n in range(len(outs))]
    shapes = [jax.ShapeDtypeStruct(s, jnp.int32 if s == (SUB, LANES) else jnp.float32) for s in outs]
    single = len(outs) == 1
    return pl.pallas_call(
        kernel,
        out_shape=shapes[0] if single else shapes,
        in_specs=specs,
        out_specs=out_specs[0] if single else out_specs,
        scratch_shapes=list(scratch),
        input_output_aliases=alias,
        name=name,
        compiler_params=pltpu.CompilerParams(vmem_limit_bytes=8 << 20),
        cost_estimate=pl.CostEstimate(
            flops=cost * 1000000, bytes_accessed=1 << 10, transcendentals=0
        ),
    )(*args)


def per_device(scalars, transport, mass, element_order):
    count = lax.axis_size("elem")
    even_pairs = [(i, i ^ 1) for i in range(count)]
    odd_pairs = [(i, (i + 1) % count if i % 2 else (i - 1) % count) for i in range(count)]
    swap_od = lambda x: lax.ppermute(x, "elem", odd_pairs)
    swap_ev = lambda x: lax.ppermute(x, "elem", even_pairs)
    members = scalars.shape[0]
    grid = (EXT, EXT, SUB, LANES)
    scal = scalars.reshape((members,) + grid)
    tr = transport.reshape((3,) + grid)
    mas = mass.reshape(grid)
    tile, part = (EXT, SUB, LANES), (ROWS, SUB, LANES)
    inner, face, faces = (2, 6) + tile, (2,) + part, (2, 2) + part
    sent, geometry = (2 * ROWS, SUB, LANES), (3,) + tile
    f32 = jnp.float32

    stay = lambda x: pltpu.with_memory_space_constraint(x, pltpu.HBM)
    od, idx, slots, far = call(
        project_odd, [(3,) + part, (SUB, LANES), (SUB, LANES), (6,) + tile],
        (stay(element_order), stay(scal), stay(mas), stay(tr)), "project", 1, hbm=(0, 1, 2, 3),
        scratch=[pltpu.VMEM((1, LANES), jnp.int32), pltpu.VMEM((3,) + tile, f32),
                 pltpu.SemaphoreType.DMA((10,))])
    od = od.reshape(3 * ROWS, SUB, LANES)
    rod = swap_od(od)
    ev = call(project_even, [(3 * ROWS + 24, SUB, LANES)], (idx, far), "project", 1)
    rev = swap_ev(ev)
    gi, q, ri, rt, ti, tf, st = call(
        prepare,
        [inner, faces, (6,) + tile, (6,) + tile, (6, 2) + tile, geometry, (2,) + part],
        (idx, scal, mas, tr), "prepare", 1)

    def opening_terms(gi_ref, ri_ref, rt_ref, ti_ref, wp_ref):
        inner_open(gi_ref, ri_ref, rt_ref, ti_ref, rotations(), wp_ref)

    wp = call(opening_terms, [inner], (gi, ri, rt, ti), "terms", 1)
    p0, r0, cev = call(
        make_field_face(0, False), [face, part, sent], (od, rod, q, st), "odd", 3000)
    p7, r7, cod = call(
        make_field_face(1, True), [face, part, (2 * ROWS + 24, SUB, LANES)],
        (ev, rev, q, st, tf), "even", 1)
    acci, accf = gi, q
    pairs = SUBSTEPS * STAGES // 2
    for n in range(pairs):
        s = 2 * n % STAGES + 1
        opening, closing, early = s == 1, s + 1 == STAGES, n == 0
        got_ev, got_od = swap_ev(cev), swap_od(cod)
        extra = (ev, rev, st, r0) if early else (a7,)
        res = call(
            make_first_inner(1.0 / s, opening, early),
            [inner, inner, faces, face] + ([geometry, (2,) + part] if early else []),
            (p0, p7, gi, acci, wp, rt, r7) + extra, "first", 1000)
        gm, acci, q, e7 = res[:4]
        if early:
            a7, rs = res[4:]
        m7, cod2 = call(
            make_stage_face(1, 1.0 / s, False, early, False), [face, sent],
            (cev, got_ev, e7, accf, q, rs, r7), "ahead", 1)
        got_od2 = swap_od(cod2)
        res = call(
            make_between(early), [inner, face] + ([] if early else [face]),
            (m7, gm, a7, r7, ri, rt, ti) + (() if early else (p0, a0, r0)), "between", 2000)
        wp, e7 = res[:2]
        if early:
            m0, cev2, a0 = call(
                make_stage_face(0, 1.0 / s, False, True, True), [face, sent, geometry],
                (cod, got_od, p0, accf, q, rs, r0, tf), "behind", 1,
                scratch=[pltpu.VMEM(face, f32)])
        else:
            m0, cev2 = call(
                make_stage_face(0, 1.0 / s, False, False, False), [face, sent],
                (cod, got_od, res[2], accf, q, rs, r0), "behind", 1)
        got_ev2 = swap_ev(cev2)
        scale = 1.0 / (s + 1)
        if n < pairs - 1:
            gi, q, acci, accf, wp, e0 = call(
                make_second_inner(scale, opening, closing),
                [inner, faces, inner, faces, inner, face],
                (m0, m7, p0, p7, accf, acci, wp, ri, rt, ti, a0, r0), "second", 3000)
            p0, cev = call(
                make_stage_face(0, scale, closing, False, False), [face, sent],
                (cod2, got_od2, e0, accf, q, rs, r0), "odd", 3000)
            p7, cod = call(
                make_stage_face(1, scale, closing, False, False), [face, sent],
                (cev2, got_ev2, e7, accf, q, rs, r7), "even", 1)
        else:
            out, accf, e0 = call(
                make_last_inner(scale), [(members,) + grid, faces, face],
                (slots, m0, m7, p0, p7, accf, acci, wp, rt, a0, r0), "last", 3000,
                hbm_out=(0,), scratch=[pltpu.VMEM(inner, f32), pltpu.SemaphoreType.DMA((2,))])
            near = call(
                make_finish_near(0, scale), [(2,) + tile],
                (slots, cod2, got_od2, e0, accf), "finish", 3000)
            out = call(
                make_finish_far(1, scale), [(members,) + grid],
                (slots, cev2, got_ev2, e7, accf, near, out), "finish", 1,
                hbm=(6,), hbm_out=(0,), alias={6: 0},
                scratch=[pltpu.VMEM((2,) + tile, f32), pltpu.SemaphoreType.DMA((2, 2))])
    return out.reshape(scalars.shape)


def solution(mesh):
    in_specs = (P("ens", None, "elem"), P(None, None, "elem"), P(None, "elem"), P("elem", None))
    out_specs = P("ens", None, "elem")
    return jax.shard_map(
        per_device, mesh=mesh, in_specs=in_specs, out_specs=out_specs, check_vma=False
    )
```

```python
import jax
import jax.numpy as jnp
import numpy as np
from jax import lax
from jax.experimental import pallas as pl
from jax.experimental.pallas import tpu as pltpu
from jax.sharding import PartitionSpec as P

ORDER = 7
EXT = ORDER + 1
SUBSTEPS = 2
STAGES = 4
EY = 8
EZ = 16
LANES = EY * EZ
SUB = 8
ROWS = 7

time_step = 0.015


def legendre_table(points, degree):
    table = np.zeros((points.shape[0], degree + 1))
    table[:, 0] = 1.0
    table[:, 1] = points
    for level in range(2, degree + 1):
        table[:, level] = (
            (2 * level - 1) * points * table[:, level - 1] - (level - 1) * table[:, level - 2]
        ) / level
    return table


def gll_derivative(degree):
    extent = degree + 1
    points = np.cos(np.pi * np.arange(extent) / degree)
    for sweep in range(60):
        table = legendre_table(points, degree)
        points = points - (points * table[:, degree] - table[:, degree - 1]) / (
            extent * table[:, degree]
        )
    points = points[::-1].copy()
    values = legendre_table(points, degree)[:, degree]
    matrix = np.zeros((extent, extent))
    for target in range(extent):
        for source in range(extent):
            if target != source:
                matrix[target, source] = values[target] / (
                    values[source] * (points[target] - points[source])
                )
    matrix[0, 0] = -degree * (degree + 1) / 4.0
    matrix[extent - 1, extent - 1] = degree * (degree + 1) / 4.0
    return matrix


DM = gll_derivative(ORDER)
SUM_PART = [[(DM[j, a] + DM[j, 7 - a]) / 2 for a in range(4)] for j in range(4)]
DIF_PART = [[(DM[j, a] - DM[j, 7 - a]) / 2 for a in range(4)] for j in range(4)]


def combine(coefs, items):
    total = None
    for c, x in zip(coefs, items):
        term = x * np.float32(c)
        total = term if total is None else total + term
    return total


def along_second(plane):
    even = [plane[a] + plane[7 - a] for a in range(4)]
    odd = [plane[a] - plane[7 - a] for a in range(4)]
    out = [None] * 8
    for j in range(4):
        e = combine(SUM_PART[j], even)
        o = combine(DIF_PART[j], odd)
        out[j] = o + e
        out[7 - j] = o - e
    return out


def along_third(x, rot):
    total = x * rot[0]
    for r in range(1, 8):
        total = total + pltpu.roll(x, r, 0) * rot[r]
    return total


def gather_lanes(x, idx):
    return jnp.take_along_axis(x, idx, axis=1, mode="promise_in_bounds")


def third_tables():
    lane = lax.broadcasted_iota(jnp.int32, (SUB, LANES), 1)
    k = lax.broadcasted_iota(jnp.int32, (SUB, LANES), 0)
    z = lane % EZ
    back = jnp.where(z == 0, lane + (EZ - 1), lane - 1)
    ahead = jnp.where(z == EZ - 1, lane - (EZ - 1), lane + 1)
    return jnp.where(k == 0, back, ahead), k == 0, k == ORDER


def plane_sum(plane, tables, rows=EXT):
    idx, first, last = tables
    up = plane[7] + pltpu.roll(plane[0], LANES - EZ, 1)
    plane = [pltpu.roll(up, EZ, 1)] + list(plane[1:7]) + [up]
    out = []
    for v in plane[:rows]:
        x = jnp.where(first, pltpu.roll(v, 1, 0), jnp.where(last, pltpu.roll(v, 7, 0), 0.0))
        out.append(v + gather_lanes(x, idx))
    return out


def full(rows):
    return list(rows) + [pltpu.roll(rows[0], LANES - EZ, 1)]


def write(ref, lead, plane):
    for j, v in enumerate(plane):
        ref[lead + (j,)] = v


def read(ref, *lead, rows=EXT):
    return [ref[lead + (j,)] for j in range(rows)]


def brick_index(order_ref):
    order = jnp.broadcast_to(order_ref[...], (LANES, LANES))
    pos = lax.broadcasted_iota(jnp.int32, (LANES, LANES), 0)
    hot = jnp.where(order == pos, 1.0, 0.0).astype(jnp.bfloat16)
    slot = lax.broadcasted_iota(jnp.int32, (SUB, LANES), 1).astype(jnp.float32).astype(jnp.bfloat16)
    found = lax.dot_general(
        slot, hot, (((1,), (1,)), ((), ())), preferred_element_type=jnp.float32
    )
    return found.astype(jnp.int32)


def source_plane(parity, i):
    return jnp.where(parity == 1, ORDER - i, i)


def source_plane(parity, i):
    return jnp.where(parity == 1, ORDER - i, i)


def project(weight, scal, idx, tables):
    weight = [gather_lanes(v, idx) for v in weight]
    planes = [[gather_lanes(plane[j], idx) * weight[j] for j in range(8)] for plane in scal]
    return [plane_sum(plane, tables, ROWS) for plane in planes + [weight]]


def project_odd(order_ref, scal_ref, mass_ref, tr_ref, od_ref, idx_ref, slot_ref, far_ref,
                order_buf, near_buf, sems):
    parity = lax.axis_index("elem") % 2
    near, far = source_plane(parity, 0), source_plane(parity, ORDER)
    copies = [pltpu.make_async_copy(order_ref, order_buf, sems.at[0])]
    late = []
    for side, (plane, buf, group) in enumerate(((near, near_buf, copies), (far, far_ref, late))):
        sources = [scal_ref.at[0, plane], scal_ref.at[1, plane], mass_ref.at[plane]]
        sources += [tr_ref.at[r, plane] for r in range(3)]
        for r, source in enumerate(sources):
            group.append(pltpu.make_async_copy(source, buf.at[r], sems.at[1 + 6 * side + r]))
    for copy in copies + late:
        copy.start()
    tables = third_tables()
    copies[0].wait()
    idx = brick_index(order_buf)
    idx_ref[...] = idx
    slot_ref[...] = jnp.broadcast_to(order_buf[...], (SUB, LANES))
    for copy in copies[1:]:
        copy.wait()
    send_projection(near_buf, idx, tables, signs_of(parity), od_ref)
    for copy in late:
        copy.wait()


def signs_of(parity):
    first = jnp.where(parity == 1, time_step, -time_step).astype(jnp.float32)
    return first, np.float32(-time_step), np.float32(-time_step)


def send_projection(planes_ref, idx, tables, signs, out_ref):
    planes = project(read(planes_ref, 2), [read(planes_ref, m) for m in range(2)], idx, tables)
    planes.extend(
        [gather_lanes(v, idx) * signs[r] for v in read(planes_ref, 3 + r)] for r in range(3))
    write(out_ref, (), sum(planes, []))


def project_even(idx_ref, far_ref, ev_ref):
    signs = signs_of(lax.axis_index("elem") % 2)
    send_projection(far_ref, idx_ref[...], third_tables(), signs, ev_ref)


def prepare(idx_ref, scal_ref, mass_ref, tr_ref,
            gi_ref, q_ref, ri_ref, rt_ref, ti_ref, st_ref):
    parity = lax.axis_index("elem") % 2
    idx = idx_ref[...]
    tables = third_tables()
    signs = signs_of(parity)

    def load(i):
        src = source_plane(parity, i)
        planes = [read(scal_ref, m, src) for m in range(2)] + [read(mass_ref, src)]
        return planes + [read(tr_ref, r, src) for r in range(3)]

    faces = [read(tr_ref, 0, source_plane(parity, face * ORDER)) for face in range(2)]
    ahead = load(1)
    for face in range(2):
        first = [gather_lanes(v, idx) * signs[0] for v in faces[face]]
        write(st_ref, (face,), plane_sum(first, tables, ROWS))
    sums = [[None, None], [None, None]]
    for i in range(6):
        raw = [[gather_lanes(v, idx) for v in plane] for plane in ahead]
        weight = raw[2]
        first = plane_sum([v * signs[0] for v in raw[3]], tables)
        inverse = [1.0 / v for v in plane_sum(weight, tables)]
        rest = [[v * signs[r] for v in raw[3 + r]] for r in (1, 2)]
        planes = []
        for m in range(2):
            plane = plane_sum([raw[m][j] * weight[j] for j in range(8)], tables)
            planes.append([plane[j] * inverse[j] for j in range(8)])
        if i < 5:
            ahead = load(i + 2)
        for r in range(2):
            write(ti_ref, (i, r), rest[r])
        write(ri_ref, (i,), inverse)
        write(rt_ref, (i,), [first[j] * inverse[j] for j in range(8)])
        for m in range(2):
            write(gi_ref, (m, i), planes[m])
            for face in range(2):
                terms = [v * np.float32(DM[face * ORDER, i + 1]) for v in planes[m][:ROWS]]
                old = sums[face][m]
                sums[face][m] = [x + y for x, y in zip(old, terms)] if old else terms
    for face in range(2):
        for m in range(2):
            write(q_ref, (face, m), sums[face][m])


def rotations():
    k = lax.broadcasted_iota(jnp.int32, (SUB, LANES), 0)
    out = []
    for r in range(8):
        value = jnp.full((SUB, LANES), np.float32(DM[7, (7 - r) % 8]))
        for row in range(7):
            value = jnp.where(k == row, np.float32(DM[row, (row - r) % 8]), value)
        out.append(value)
    return out


def in_plane(plane, second_t, third_t, rot):
    second = along_second(plane)
    return [second_t[j] * second[j] + third_t[j] * along_third(plane[j], rot) for j in range(8)]


def inner_open(gi_ref, ri_ref, rt_ref, ti_ref, rot, wp_ref):
    tables = third_tables()
    for m in range(2):
        for j in range(8):
            rows = [gi_ref[m, a, j] for a in range(6)]
            even = [rows[a] + rows[5 - a] for a in range(3)]
            odd = [rows[a] - rows[5 - a] for a in range(3)]
            for i in range(3):
                e = combine([(DM[i + 1, a + 1] + DM[i + 1, 6 - a]) / 2 for a in range(3)], even)
                o = combine([(DM[i + 1, a + 1] - DM[i + 1, 6 - a]) / 2 for a in range(3)], odd)
                wp_ref[m, i, j] = (o + e) * rt_ref[i, j]
                wp_ref[m, 5 - i, j] = (o - e) * rt_ref[5 - i, j]
    for i in range(6):
        for m in range(2):
            plane = in_plane(read(gi_ref, m, i), read(ti_ref, i, 0), read(ti_ref, i, 1), rot)
            plane = plane_sum(plane, tables)
            write(wp_ref, (m, i), [wp_ref[m, i, j] + ri_ref[i, j] * plane[j] for j in range(8)])


def inner_close(p0_ref, p7_ref, wp_ref, rt_ref, scale, put, q_ref=None):
    for m in range(2):
        p0, p7 = full(read(p0_ref, m, rows=ROWS)), full(read(p7_ref, m, rows=ROWS))
        sums = [[], []]
        for i in range(6):
            near, far = np.float32(scale * DM[i + 1, 0]), np.float32(scale * DM[i + 1, ORDER])
            kept = put(m, i, [
                wp_ref[m, i, j] * np.float32(scale) + rt_ref[i, j] * (p0[j] * near + p7[j] * far)
                for j in range(8)
            ])
            for face in range(2):
                terms = [v * np.float32(DM[face * ORDER, i + 1]) for v in kept[:ROWS]]
                sums[face] = [x + y for x, y in zip(sums[face], terms)] if i else terms
        if q_ref is not None:
            for face in range(2):
                write(q_ref, (face, m), sums[face])


def own_terms(p_ref, a_ref, rf_ref, face, rot, tables, e_ref):
    second_t, third_t = read(a_ref, 0), read(a_ref, 1)
    for m in range(2):
        p = full(read(p_ref, m, rows=ROWS))
        plane = plane_sum(in_plane(p, second_t, third_t, rot), tables, ROWS)
        write(e_ref, (m,), [
            rf_ref[j] * (plane[j] + a_ref[2, j] * (p[j] * np.float32(DM[face * ORDER, face * ORDER])))
            for j in range(ROWS)
        ])


def both_sides(own, got, tables, a_ref):
    total = [[own[r][j] + got[r][j] for j in range(8)] for r in range(3)]
    write(a_ref, (0,), total[1])
    write(a_ref, (1,), total[2])
    write(a_ref, (2,), plane_sum(total[0], tables, ROWS))


def transports(ref, start):
    return [[ref[start + 8 * r + j] for j in range(8)] for r in range(3)]


def make_field_face(face):
    far = np.float32(DM[ORDER - face * ORDER, face * ORDER])

    def field_face(own_ref, got_ref, q_ref, st_ref, p_ref, rf_ref, send_ref):
        inverse = [1.0 / (own_ref[14 + j] + got_ref[14 + j]) for j in range(ROWS)]
        p = [
            [(own_ref[ROWS * m + j] + got_ref[ROWS * m + j]) * inverse[j] for j in range(ROWS)]
            for m in range(2)
        ]
        sent = [
            [st_ref[1 - face, j] * (q_ref[1 - face, m, j] + p[m][j] * far) for j in range(ROWS)]
            for m in range(2)
        ]
        write(send_ref, (), sent[0] + sent[1])
        for m in range(2):
            write(p_ref, (m,), p[m])
        write(rf_ref, (), inverse)

    return field_face


def make_stage_face(face, scale, total, raw):
    far = np.float32(DM[ORDER - face * ORDER, face * ORDER])
    scale = np.float32(scale)

    def stage_face(own_ref, got_ref, e_ref, acc_ref, q_ref, rt_ref, rf_ref, p_ref, send_ref):
        p = []
        for m in range(2):
            value = [own_ref[ROWS * m + j] + got_ref[ROWS * m + j] for j in range(ROWS)]
            if raw:
                value = [value[j] * rf_ref[j] for j in range(ROWS)]
            value = [(value[j] + e_ref[m, j]) * scale for j in range(ROWS)]
            if total:
                value = [value[j] + acc_ref[face, m, j] for j in range(ROWS)]
            p.append(value)
        sent = [
            [rt_ref[1 - face, j] * (q_ref[1 - face, m, j] + p[m][j] * far) for j in range(ROWS)]
            for m in range(2)
        ]
        write(send_ref, (), sent[0] + sent[1])
        for m in range(2):
            write(p_ref, (m,), p[m])

    return stage_face


def make_first_inner(scale, opening, start):
    def first_inner(*refs):
        p0_ref, p7_ref, gi_ref, rt_ref, r7_ref = refs[:5]
        tables = third_tables()
        rot = rotations()
        if start:
            od_ref, rod_ref, ev_ref, rev_ref, st_ref, r0_ref, ri_ref, ti_ref = refs[5:13]
            gn_ref, an_ref, q_ref, e7_ref, a0_ref, a7_ref, rs_ref, wp_ref = refs[13:]
            inner_open(gi_ref, ri_ref, rt_ref, ti_ref, rot, wp_ref)
            for own, got, out in ((od_ref, rod_ref, a0_ref), (ev_ref, rev_ref, a7_ref)):
                both_sides(transports(own, 3 * ROWS), transports(got, 3 * ROWS), tables, out)
            write(rs_ref, (0,), [st_ref[0, j] * r0_ref[j] for j in range(ROWS)])
            write(rs_ref, (1,), [st_ref[1, j] * r7_ref[j] for j in range(ROWS)])
        else:
            acci_ref, wp_ref, a7_ref = refs[5:8]
            gn_ref, an_ref, q_ref, e7_ref = refs[8:]
        own_terms(p7_ref, a7_ref, r7_ref, 1, rot, tables, e7_ref)

        def put(m, i, value):
            base = gi_ref if opening else acci_ref
            write(gn_ref, (m, i), value)
            write(an_ref, (m, i), [base[m, i, j] + value[j] for j in range(8)])
            return value

        inner_close(p0_ref, p7_ref, wp_ref, rt_ref, scale, put, q_ref)

    return first_inner


def between(m7_ref, gi_ref, a7_ref, r7_ref, ri_ref, rt_ref, ti_ref, p0_ref, a0_ref, r0_ref,
            wp_ref, e7_ref, e0_ref):
    rot = rotations()
    tables = third_tables()
    own_terms(p0_ref, a0_ref, r0_ref, 0, rot, tables, e0_ref)
    own_terms(m7_ref, a7_ref, r7_ref, 1, rot, tables, e7_ref)
    inner_open(gi_ref, ri_ref, rt_ref, ti_ref, rot, wp_ref)


def face_totals(now, before, accf_ref, afn_ref, opening):
    for face in range(2):
        for m in range(2):
            for j in range(ROWS):
                value = now[face][m, j] + before[face][m, j]
                afn_ref[face, m, j] = value if opening else value + accf_ref[face, m, j]


def make_second_inner(scale, opening, closing):
    def second_inner(m0_ref, m7_ref, p0_ref, p7_ref, accf_ref, acci_ref, wp_ref, ri_ref, rt_ref,
                     ti_ref, a0_ref, r0_ref, gn_ref, q_ref, an_ref, afn_ref, wn_ref, e0_ref):
        rot = rotations()

        def put(m, i, value):
            total = [acci_ref[m, i, j] + value[j] for j in range(8)]
            kept = total if closing else value
            write(gn_ref, (m, i), kept)
            if not closing:
                write(an_ref, (m, i), total)
            return kept

        inner_close(m0_ref, m7_ref, wp_ref, rt_ref, scale, put, q_ref)
        own_terms(m0_ref, a0_ref, r0_ref, 0, rot, third_tables(), e0_ref)
        face_totals((m0_ref, m7_ref), (p0_ref, p7_ref), accf_ref, afn_ref, opening)
        inner_open(gn_ref, ri_ref, rt_ref, ti_ref, rot, wn_ref)

    return second_inner


def make_last_inner(scale):
    def last_inner(slot_ref, m0_ref, m7_ref, p0_ref, p7_ref, accf_ref, acci_ref, wp_ref, rt_ref,
                   a0_ref, r0_ref, out_ref, afn_ref, e0_ref, buf, sems):
        parity = lax.axis_index("elem") % 2
        idx = slot_ref[...]

        def put(m, i, value):
            total = [acci_ref[m, i, j] + value[j] for j in range(8)]
            dst = source_plane(parity, i + 1) - 1
            write(buf, (m, dst), [gather_lanes(v, idx) for v in total])
            return total

        inner_close(m0_ref, m7_ref, wp_ref, rt_ref, scale, put)
        copies = [
            pltpu.make_async_copy(buf.at[m], out_ref.at[m, pl.ds(1, 6)], sems.at[m])
            for m in range(2)
        ]
        for copy in copies:
            copy.start()
        own_terms(m0_ref, a0_ref, r0_ref, 0, rotations(), third_tables(), e0_ref)
        face_totals((m0_ref, m7_ref), (p0_ref, p7_ref), accf_ref, afn_ref, False)
        for copy in copies:
            copy.wait()

    return last_inner


def final_face(face, scale, slot_ref, own_ref, got_ref, e_ref, accf_ref, m):
    idx = slot_ref[...]
    rows = [
        (own_ref[ROWS * m + j] + got_ref[ROWS * m + j] + e_ref[m, j]) * np.float32(scale)
        + accf_ref[face, m, j]
        for j in range(ROWS)
    ]
    return [gather_lanes(v, idx) for v in full(rows)]


def make_finish_near(face, scale):
    def finish_near(slot_ref, own_ref, got_ref, e_ref, accf_ref, face_ref):
        for m in range(2):
            write(face_ref, (m,), final_face(face, scale, slot_ref, own_ref, got_ref, e_ref, accf_ref, m))

    return finish_near


def make_finish_far(face, scale):
    def finish_far(slot_ref, own_ref, got_ref, e_ref, accf_ref, near_ref, part_ref,
                   out_ref, buf, sems):
        dst = source_plane(lax.axis_index("elem") % 2, face * ORDER)
        copies = []
        for m in range(2):
            copies.append(
                pltpu.make_async_copy(near_ref.at[m], out_ref.at[m, ORDER - dst], sems.at[1, m])
            )
            copies[-1].start()
        for m in range(2):
            write(buf, (m,), final_face(face, scale, slot_ref, own_ref, got_ref, e_ref, accf_ref, m))
            copies.append(pltpu.make_async_copy(buf.at[m], out_ref.at[m, dst], sems.at[0, m]))
            copies[-1].start()
        for copy in copies:
            copy.wait()

    return finish_far


VM = pl.BlockSpec(memory_space=pltpu.VMEM)
HB = pl.BlockSpec(memory_space=pltpu.HBM)


def call(kernel, outs, args, name, cost, hbm=(), hbm_out=(), scratch=(), alias={}):
    specs = [HB if n in hbm else VM for n in range(len(args))]
    out_specs = [HB if n in hbm_out else VM for n in range(len(outs))]
    shapes = [jax.ShapeDtypeStruct(s, jnp.int32 if s == (SUB, LANES) else jnp.float32) for s in outs]
    single = len(outs) == 1
    return pl.pallas_call(
        kernel,
        out_shape=shapes[0] if single else shapes,
        in_specs=specs,
        out_specs=out_specs[0] if single else out_specs,
        scratch_shapes=list(scratch),
        input_output_aliases=alias,
        name=name,
        compiler_params=pltpu.CompilerParams(vmem_limit_bytes=8 << 20),
        cost_estimate=pl.CostEstimate(
            flops=cost * 1000000, bytes_accessed=1 << 10, transcendentals=0
        ),
    )(*args)


def per_device(scalars, transport, mass, element_order):
    count = lax.axis_size("elem")
    even_pairs = [(i, i ^ 1) for i in range(count)]
    odd_pairs = [(i, (i + 1) % count if i % 2 else (i - 1) % count) for i in range(count)]
    swap_od = lambda x: lax.ppermute(x, "elem", odd_pairs)
    swap_ev = lambda x: lax.ppermute(x, "elem", even_pairs)
    members = scalars.shape[0]
    grid = (EXT, EXT, SUB, LANES)
    scal = scalars.reshape((members,) + grid)
    tr = transport.reshape((3,) + grid)
    mas = mass.reshape(grid)
    tile, part = (EXT, SUB, LANES), (ROWS, SUB, LANES)
    inner, face, faces = (2, 6) + tile, (2,) + part, (2, 2) + part
    sent, geometry = (2 * ROWS, SUB, LANES), (3,) + tile
    f32 = jnp.float32

    stay = lambda x: pltpu.with_memory_space_constraint(x, pltpu.HBM)
    bundle = (3 * ROWS + 24, SUB, LANES)
    od, idx, slots, far = call(
        project_odd, [bundle, (SUB, LANES), (SUB, LANES), (6,) + tile],
        (stay(element_order), stay(scal), stay(mas), stay(tr)), "project", 1, hbm=(0, 1, 2, 3),
        scratch=[pltpu.VMEM((1, LANES), jnp.int32), pltpu.VMEM((6,) + tile, f32),
                 pltpu.SemaphoreType.DMA((13,))])
    rod = swap_od(od)
    ev = call(project_even, [bundle], (idx, far), "project", 1)
    rev = swap_ev(ev)
    gi, q, ri, rt, ti, st = call(
        prepare, [inner, faces, (6,) + tile, (6,) + tile, (6, 2) + tile, (2,) + part],
        (idx, scal, mas, tr), "prepare", 1)
    p0, r0, cev = call(make_field_face(0), [face, part, sent], (od, rod, q, st), "odd", 3000)
    p7, r7, cod = call(make_field_face(1), [face, part, sent], (ev, rev, q, st), "even", 1)
    acci, accf, wp = gi, q, gi
    pairs = SUBSTEPS * STAGES // 2
    for n in range(pairs):
        s = 2 * n % STAGES + 1
        opening, closing, early = s == 1, s + 1 == STAGES, n == 0
        got_ev, got_od = swap_ev(cev), swap_od(cod)
        extra = (od, rod, ev, rev, st, r0, ri, ti) if early else (acci, wp, a7)
        res = call(
            make_first_inner(1.0 / s, opening, early),
            [inner, inner, faces, face] + ([geometry, geometry, (2,) + part] if early else []),
            (p0, p7, gi, rt, r7) + extra, "first", 1000,
            scratch=[pltpu.VMEM(inner, f32)] if early else [])
        gm, acci, q, e7 = res[:4]
        if early:
            a0, a7, rs = res[4:]
        m7, cod2 = call(
            make_stage_face(1, 1.0 / s, False, early), [face, sent],
            (cev, got_ev, e7, accf, q, rs, r7), "ahead", 1)
        got_od2 = swap_od(cod2)
        wp, e7, e0 = call(
            between, [inner, face, face], (m7, gm, a7, r7, ri, rt, ti, p0, a0, r0), "between", 2000)
        m0, cev2 = call(
            make_stage_face(0, 1.0 / s, False, early), [face, sent],
            (cod, got_od, e0, accf, q, rs, r0), "behind", 1)
        got_ev2 = swap_ev(cev2)
        scale = 1.0 / (s + 1)
        if n < pairs - 1:
            gi, q, acci, accf, wp, e0 = call(
                make_second_inner(scale, opening, closing),
                [inner, faces, inner, faces, inner, face],
                (m0, m7, p0, p7, accf, acci, wp, ri, rt, ti, a0, r0), "second", 3000)
            p0, cev = call(
                make_stage_face(0, scale, closing, False), [face, sent],
                (cod2, got_od2, e0, accf, q, rs, r0), "odd", 3000)
            p7, cod = call(
                make_stage_face(1, scale, closing, False), [face, sent],
                (cev2, got_ev2, e7, accf, q, rs, r7), "even", 1)
        else:
            out, accf, e0 = call(
                make_last_inner(scale), [(members,) + grid, faces, face],
                (slots, m0, m7, p0, p7, accf, acci, wp, rt, a0, r0), "last", 3000,
                hbm_out=(0,), scratch=[pltpu.VMEM(inner, f32), pltpu.SemaphoreType.DMA((2,))])
            near = call(
                make_finish_near(0, scale), [(2,) + tile],
                (slots, cod2, got_od2, e0, accf), "finish", 3000)
            out = call(
                make_finish_far(1, scale), [(members,) + grid],
                (slots, cev2, got_ev2, e7, accf, near, out), "finish", 1,
                hbm=(6,), hbm_out=(0,), alias={6: 0},
                scratch=[pltpu.VMEM((2,) + tile, f32), pltpu.SemaphoreType.DMA((2, 2))])
    return out.reshape(scalars.shape)


def solution(mesh):
    in_specs = (P("ens", None, "elem"), P(None, None, "elem"), P(None, "elem"), P("elem", None))
    out_specs = P("ens", None, "elem")
    return jax.shard_map(
        per_device, mesh=mesh, in_specs=in_specs, out_specs=out_specs, check_vma=False
    )
```

```python
import jax
import jax.numpy as jnp
import numpy as np
from jax import lax
from jax.experimental import pallas as pl
from jax.experimental.pallas import tpu as pltpu
from jax.sharding import PartitionSpec as P

ORDER = 7
EXT = ORDER + 1
SUBSTEPS = 2
STAGES = 4
EY = 8
EZ = 16
LANES = EY * EZ
SUB = 8
ROWS = 7

time_step = 0.015


def legendre_table(points, degree):
    table = np.zeros((points.shape[0], degree + 1))
    table[:, 0] = 1.0
    table[:, 1] = points
    for level in range(2, degree + 1):
        table[:, level] = (
            (2 * level - 1) * points * table[:, level - 1] - (level - 1) * table[:, level - 2]
        ) / level
    return table


def gll_derivative(degree):
    extent = degree + 1
    points = np.cos(np.pi * np.arange(extent) / degree)
    for sweep in range(60):
        table = legendre_table(points, degree)
        points = points - (points * table[:, degree] - table[:, degree - 1]) / (
            extent * table[:, degree]
        )
    points = points[::-1].copy()
    values = legendre_table(points, degree)[:, degree]
    matrix = np.zeros((extent, extent))
    for target in range(extent):
        for source in range(extent):
            if target != source:
                matrix[target, source] = values[target] / (
                    values[source] * (points[target] - points[source])
                )
    matrix[0, 0] = -degree * (degree + 1) / 4.0
    matrix[extent - 1, extent - 1] = degree * (degree + 1) / 4.0
    return matrix


DM = gll_derivative(ORDER)
SUM_PART = [[(DM[j, a] + DM[j, 7 - a]) / 2 for a in range(4)] for j in range(4)]
DIF_PART = [[(DM[j, a] - DM[j, 7 - a]) / 2 for a in range(4)] for j in range(4)]


def combine(coefs, items):
    total = None
    for c, x in zip(coefs, items):
        term = x * np.float32(c)
        total = term if total is None else total + term
    return total


def along_second(plane):
    even = [plane[a] + plane[7 - a] for a in range(4)]
    odd = [plane[a] - plane[7 - a] for a in range(4)]
    out = [None] * 8
    for j in range(4):
        e = combine(SUM_PART[j], even)
        o = combine(DIF_PART[j], odd)
        out[j] = o + e
        out[7 - j] = o - e
    return out


def along_third(x, rot):
    total = x * rot[0]
    for r in range(1, 8):
        total = total + pltpu.roll(x, r, 0) * rot[r]
    return total


def gather_lanes(x, idx):
    return jnp.take_along_axis(x, idx, axis=1, mode="promise_in_bounds")


def third_tables():
    lane = lax.broadcasted_iota(jnp.int32, (SUB, LANES), 1)
    k = lax.broadcasted_iota(jnp.int32, (SUB, LANES), 0)
    z = lane % EZ
    back = jnp.where(z == 0, lane + (EZ - 1), lane - 1)
    ahead = jnp.where(z == EZ - 1, lane - (EZ - 1), lane + 1)
    return jnp.where(k == 0, back, ahead), k == 0, k == ORDER


def plane_sum(plane, tables, rows=EXT):
    idx, first, last = tables
    up = plane[7] + pltpu.roll(plane[0], LANES - EZ, 1)
    plane = [pltpu.roll(up, EZ, 1)] + list(plane[1:7]) + [up]
    out = []
    for v in plane[:rows]:
        x = jnp.where(first, pltpu.roll(v, 1, 0), jnp.where(last, pltpu.roll(v, 7, 0), 0.0))
        out.append(v + gather_lanes(x, idx))
    return out


def full(rows):
    return list(rows) + [pltpu.roll(rows[0], LANES - EZ, 1)]


def write(ref, lead, plane):
    for j, v in enumerate(plane):
        ref[lead + (j,)] = v


def read(ref, *lead, rows=EXT):
    return [ref[lead + (j,)] for j in range(rows)]


def brick_index(order_ref):
    order = jnp.broadcast_to(order_ref[...], (LANES, LANES))
    pos = lax.broadcasted_iota(jnp.int32, (LANES, LANES), 0)
    hot = jnp.where(order == pos, 1.0, 0.0).astype(jnp.bfloat16)
    slot = lax.broadcasted_iota(jnp.int32, (SUB, LANES), 1).astype(jnp.float32).astype(jnp.bfloat16)
    found = lax.dot_general(
        slot, hot, (((1,), (1,)), ((), ())), preferred_element_type=jnp.float32
    )
    return found.astype(jnp.int32)


def source_plane(parity, i):
    return jnp.where(parity == 1, ORDER - i, i)


def source_plane(parity, i):
    return jnp.where(parity == 1, ORDER - i, i)


def project(weight, scal, idx, tables):
    weight = [gather_lanes(v, idx) for v in weight]
    planes = [[gather_lanes(plane[j], idx) * weight[j] for j in range(8)] for plane in scal]
    return [plane_sum(plane, tables, ROWS) for plane in planes + [weight]]


def project_odd(order_ref, scal_ref, mass_ref, tr_ref, od_ref, idx_ref, slot_ref, raw_ref,
                order_buf, near_buf, sems):
    parity = lax.axis_index("elem") % 2
    near, far = source_plane(parity, 0), source_plane(parity, ORDER)
    copies = [pltpu.make_async_copy(order_ref, order_buf, sems.at[0])]
    for r, source in enumerate((scal_ref.at[0, near], scal_ref.at[1, near], mass_ref.at[near])):
        copies.append(pltpu.make_async_copy(source, near_buf.at[r], sems.at[1 + r]))
    sources = [scal_ref.at[0, far], scal_ref.at[1, far], mass_ref.at[far]]
    sources += [tr_ref.at[r, far] for r in range(3)] + [tr_ref.at[r, near] for r in range(3)]
    late = [
        pltpu.make_async_copy(source, raw_ref.at[r], sems.at[4 + r])
        for r, source in enumerate(sources)
    ]
    for copy in copies + late:
        copy.start()
    tables = third_tables()
    copies[0].wait()
    idx = brick_index(order_buf)
    idx_ref[...] = idx
    slot_ref[...] = jnp.broadcast_to(order_buf[...], (SUB, LANES))
    for copy in copies[1:]:
        copy.wait()
    planes = project(read(near_buf, 2), [read(near_buf, m) for m in range(2)], idx, tables)
    write(od_ref, (), sum(planes, []))
    for copy in late:
        copy.wait()


def signs_of(parity):
    first = jnp.where(parity == 1, time_step, -time_step).astype(jnp.float32)
    return first, np.float32(-time_step), np.float32(-time_step)


def project_even(idx_ref, raw_ref, ev_ref, tf_ref):
    idx = idx_ref[...]
    signs = signs_of(lax.axis_index("elem") % 2)
    planes = project(read(raw_ref, 2), [read(raw_ref, m) for m in range(2)], idx, third_tables())
    turned = [[gather_lanes(v, idx) * signs[r % 3] for v in read(raw_ref, 3 + r)] for r in range(6)]
    write(ev_ref, (), sum(planes + turned[:3], []))
    write(tf_ref, (), sum(turned[3:], []))


def prepare(idx_ref, scal_ref, mass_ref, tr_ref,
            gi_ref, q_ref, ri_ref, rt_ref, ti_ref, st_ref):
    parity = lax.axis_index("elem") % 2
    idx = idx_ref[...]
    tables = third_tables()
    signs = signs_of(parity)

    def load(i):
        src = source_plane(parity, i)
        planes = [read(scal_ref, m, src) for m in range(2)] + [read(mass_ref, src)]
        return planes + [read(tr_ref, r, src) for r in range(3)]

    faces = [read(tr_ref, 0, source_plane(parity, face * ORDER)) for face in range(2)]
    ahead = load(1)
    for face in range(2):
        first = [gather_lanes(v, idx) * signs[0] for v in faces[face]]
        write(st_ref, (face,), plane_sum(first, tables, ROWS))
    sums = [[None, None], [None, None]]
    for i in range(6):
        raw = [[gather_lanes(v, idx) for v in plane] for plane in ahead]
        weight = raw[2]
        first = plane_sum([v * signs[0] for v in raw[3]], tables)
        inverse = [1.0 / v for v in plane_sum(weight, tables)]
        rest = [[v * signs[r] for v in raw[3 + r]] for r in (1, 2)]
        planes = []
        for m in range(2):
            plane = plane_sum([raw[m][j] * weight[j] for j in range(8)], tables)
            planes.append([plane[j] * inverse[j] for j in range(8)])
        if i < 5:
            ahead = load(i + 2)
        for r in range(2):
            write(ti_ref, (i, r), rest[r])
        write(ri_ref, (i,), inverse)
        write(rt_ref, (i,), [first[j] * inverse[j] for j in range(8)])
        for m in range(2):
            write(gi_ref, (m, i), planes[m])
            for face in range(2):
                terms = [v * np.float32(DM[face * ORDER, i + 1]) for v in planes[m][:ROWS]]
                old = sums[face][m]
                sums[face][m] = [x + y for x, y in zip(old, terms)] if old else terms
    for face in range(2):
        for m in range(2):
            write(q_ref, (face, m), sums[face][m])


def rotations():
    k = lax.broadcasted_iota(jnp.int32, (SUB, LANES), 0)
    out = []
    for r in range(8):
        value = jnp.full((SUB, LANES), np.float32(DM[7, (7 - r) % 8]))
        for row in range(7):
            value = jnp.where(k == row, np.float32(DM[row, (row - r) % 8]), value)
        out.append(value)
    return out


def in_plane(plane, second_t, third_t, rot):
    second = along_second(plane)
    return [second_t[j] * second[j] + third_t[j] * along_third(plane[j], rot) for j in range(8)]


def inner_open(gi_ref, ri_ref, rt_ref, ti_ref, rot, wp_ref):
    tables = third_tables()
    for m in range(2):
        for j in range(8):
            rows = [gi_ref[m, a, j] for a in range(6)]
            even = [rows[a] + rows[5 - a] for a in range(3)]
            odd = [rows[a] - rows[5 - a] for a in range(3)]
            for i in range(3):
                e = combine([(DM[i + 1, a + 1] + DM[i + 1, 6 - a]) / 2 for a in range(3)], even)
                o = combine([(DM[i + 1, a + 1] - DM[i + 1, 6 - a]) / 2 for a in range(3)], odd)
                wp_ref[m, i, j] = (o + e) * rt_ref[i, j]
                wp_ref[m, 5 - i, j] = (o - e) * rt_ref[5 - i, j]
    for i in range(6):
        for m in range(2):
            plane = in_plane(read(gi_ref, m, i), read(ti_ref, i, 0), read(ti_ref, i, 1), rot)
            plane = plane_sum(plane, tables)
            write(wp_ref, (m, i), [wp_ref[m, i, j] + ri_ref[i, j] * plane[j] for j in range(8)])


def inner_close(p0_ref, p7_ref, wp_ref, rt_ref, scale, put, q_ref=None):
    for m in range(2):
        p0, p7 = full(read(p0_ref, m, rows=ROWS)), full(read(p7_ref, m, rows=ROWS))
        sums = [[], []]
        for i in range(6):
            near, far = np.float32(scale * DM[i + 1, 0]), np.float32(scale * DM[i + 1, ORDER])
            kept = put(m, i, [
                wp_ref[m, i, j] * np.float32(scale) + rt_ref[i, j] * (p0[j] * near + p7[j] * far)
                for j in range(8)
            ])
            for face in range(2):
                terms = [v * np.float32(DM[face * ORDER, i + 1]) for v in kept[:ROWS]]
                sums[face] = [x + y for x, y in zip(sums[face], terms)] if i else terms
        if q_ref is not None:
            for face in range(2):
                write(q_ref, (face, m), sums[face])


def own_terms(p_ref, a_ref, rf_ref, face, rot, tables, e_ref):
    second_t, third_t = read(a_ref, 0), read(a_ref, 1)
    for m in range(2):
        p = full(read(p_ref, m, rows=ROWS))
        plane = plane_sum(in_plane(p, second_t, third_t, rot), tables, ROWS)
        write(e_ref, (m,), [
            rf_ref[j] * (plane[j] + a_ref[2, j] * (p[j] * np.float32(DM[face * ORDER, face * ORDER])))
            for j in range(ROWS)
        ])


def both_sides(own, got, tables, a_ref):
    total = [[own[r][j] + got[r][j] for j in range(8)] for r in range(3)]
    write(a_ref, (0,), total[1])
    write(a_ref, (1,), total[2])
    write(a_ref, (2,), plane_sum(total[0], tables, ROWS))


def transports(ref, start):
    return [[ref[start + 8 * r + j] for j in range(8)] for r in range(3)]


def make_field_face(face):
    far = np.float32(DM[ORDER - face * ORDER, face * ORDER])

    def field_face(own_ref, got_ref, q_ref, st_ref, p_ref, rf_ref, send_ref):
        inverse = [1.0 / (own_ref[14 + j] + got_ref[14 + j]) for j in range(ROWS)]
        p = [
            [(own_ref[ROWS * m + j] + got_ref[ROWS * m + j]) * inverse[j] for j in range(ROWS)]
            for m in range(2)
        ]
        sent = [
            [st_ref[1 - face, j] * (q_ref[1 - face, m, j] + p[m][j] * far) for j in range(ROWS)]
            for m in range(2)
        ]
        write(send_ref, (), sent[0] + sent[1])
        for m in range(2):
            write(p_ref, (m,), p[m])
        write(rf_ref, (), inverse)

    return field_face


def make_stage_face(face, scale, total, raw):
    far = np.float32(DM[ORDER - face * ORDER, face * ORDER])
    scale = np.float32(scale)

    def stage_face(own_ref, got_ref, e_ref, acc_ref, q_ref, rt_ref, rf_ref, p_ref, send_ref):
        p = []
        for m in range(2):
            value = [own_ref[ROWS * m + j] + got_ref[ROWS * m + j] for j in range(ROWS)]
            if raw:
                value = [value[j] * rf_ref[j] for j in range(ROWS)]
            value = [(value[j] + e_ref[m, j]) * scale for j in range(ROWS)]
            if total:
                value = [value[j] + acc_ref[face, m, j] for j in range(ROWS)]
            p.append(value)
        sent = [
            [rt_ref[1 - face, j] * (q_ref[1 - face, m, j] + p[m][j] * far) for j in range(ROWS)]
            for m in range(2)
        ]
        write(send_ref, (), sent[0] + sent[1])
        for m in range(2):
            write(p_ref, (m,), p[m])

    return stage_face


def make_first_inner(scale, opening, start):
    def first_inner(*refs):
        p0_ref, p7_ref, gi_ref, rt_ref, r7_ref = refs[:5]
        tables = third_tables()
        rot = rotations()
        if start:
            tf_ref, rtf_ref, ev_ref, rev_ref, st_ref, r0_ref, ri_ref, ti_ref = refs[5:13]
            gn_ref, an_ref, q_ref, e7_ref, a0_ref, a7_ref, rs_ref, wp_ref = refs[13:]
            inner_open(gi_ref, ri_ref, rt_ref, ti_ref, rot, wp_ref)
            both_sides(transports(tf_ref, 0), transports(rtf_ref, 0), tables, a0_ref)
            both_sides(
                transports(ev_ref, 3 * ROWS), transports(rev_ref, 3 * ROWS), tables, a7_ref)
            write(rs_ref, (0,), [st_ref[0, j] * r0_ref[j] for j in range(ROWS)])
            write(rs_ref, (1,), [st_ref[1, j] * r7_ref[j] for j in range(ROWS)])
        else:
            acci_ref, wp_ref, a7_ref = refs[5:8]
            gn_ref, an_ref, q_ref, e7_ref = refs[8:]
        own_terms(p7_ref, a7_ref, r7_ref, 1, rot, tables, e7_ref)

        def put(m, i, value):
            base = gi_ref if opening else acci_ref
            write(gn_ref, (m, i), value)
            write(an_ref, (m, i), [base[m, i, j] + value[j] for j in range(8)])
            return value

        inner_close(p0_ref, p7_ref, wp_ref, rt_ref, scale, put, q_ref)

    return first_inner


def between(m7_ref, gi_ref, a7_ref, r7_ref, ri_ref, rt_ref, ti_ref, p0_ref, a0_ref, r0_ref,
            wp_ref, e7_ref, e0_ref):
    rot = rotations()
    tables = third_tables()
    own_terms(p0_ref, a0_ref, r0_ref, 0, rot, tables, e0_ref)
    own_terms(m7_ref, a7_ref, r7_ref, 1, rot, tables, e7_ref)
    inner_open(gi_ref, ri_ref, rt_ref, ti_ref, rot, wp_ref)


def face_totals(now, before, accf_ref, afn_ref, opening):
    for face in range(2):
        for m in range(2):
            for j in range(ROWS):
                value = now[face][m, j] + before[face][m, j]
                afn_ref[face, m, j] = value if opening else value + accf_ref[face, m, j]


def make_second_inner(scale, opening, closing):
    def second_inner(m0_ref, m7_ref, p0_ref, p7_ref, accf_ref, acci_ref, wp_ref, ri_ref, rt_ref,
                     ti_ref, a0_ref, r0_ref, gn_ref, q_ref, an_ref, afn_ref, wn_ref, e0_ref):
        rot = rotations()

        def put(m, i, value):
            total = [acci_ref[m, i, j] + value[j] for j in range(8)]
            kept = total if closing else value
            write(gn_ref, (m, i), kept)
            if not closing:
                write(an_ref, (m, i), total)
            return kept

        inner_close(m0_ref, m7_ref, wp_ref, rt_ref, scale, put, q_ref)
        own_terms(m0_ref, a0_ref, r0_ref, 0, rot, third_tables(), e0_ref)
        face_totals((m0_ref, m7_ref), (p0_ref, p7_ref), accf_ref, afn_ref, opening)
        inner_open(gn_ref, ri_ref, rt_ref, ti_ref, rot, wn_ref)

    return second_inner


def make_last_inner(scale):
    def last_inner(slot_ref, m0_ref, m7_ref, p0_ref, p7_ref, accf_ref, acci_ref, wp_ref, rt_ref,
                   a0_ref, r0_ref, out_ref, afn_ref, e0_ref, buf, sems):
        parity = lax.axis_index("elem") % 2
        idx = slot_ref[...]

        def put(m, i, value):
            total = [acci_ref[m, i, j] + value[j] for j in range(8)]
            dst = source_plane(parity, i + 1) - 1
            write(buf, (m, dst), [gather_lanes(v, idx) for v in total])
            return total

        inner_close(m0_ref, m7_ref, wp_ref, rt_ref, scale, put)
        copies = [
            pltpu.make_async_copy(buf.at[m], out_ref.at[m, pl.ds(1, 6)], sems.at[m])
            for m in range(2)
        ]
        for copy in copies:
            copy.start()
        own_terms(m0_ref, a0_ref, r0_ref, 0, rotations(), third_tables(), e0_ref)
        face_totals((m0_ref, m7_ref), (p0_ref, p7_ref), accf_ref, afn_ref, False)
        for copy in copies:
            copy.wait()

    return last_inner


def final_face(face, scale, slot_ref, own_ref, got_ref, e_ref, accf_ref, m):
    idx = slot_ref[...]
    rows = [
        (own_ref[ROWS * m + j] + got_ref[ROWS * m + j] + e_ref[m, j]) * np.float32(scale)
        + accf_ref[face, m, j]
        for j in range(ROWS)
    ]
    return [gather_lanes(v, idx) for v in full(rows)]


def make_finish_near(face, scale):
    def finish_near(slot_ref, own_ref, got_ref, e_ref, accf_ref, face_ref):
        for m in range(2):
            write(face_ref, (m,), final_face(face, scale, slot_ref, own_ref, got_ref, e_ref, accf_ref, m))

    return finish_near


def make_finish_far(face, scale):
    def finish_far(slot_ref, own_ref, got_ref, e_ref, accf_ref, near_ref, part_ref,
                   out_ref, buf, sems):
        dst = source_plane(lax.axis_index("elem") % 2, face * ORDER)
        copies = []
        for m in range(2):
            copies.append(
                pltpu.make_async_copy(near_ref.at[m], out_ref.at[m, ORDER - dst], sems.at[1, m])
            )
            copies[-1].start()
        for m in range(2):
            write(buf, (m,), final_face(face, scale, slot_ref, own_ref, got_ref, e_ref, accf_ref, m))
            copies.append(pltpu.make_async_copy(buf.at[m], out_ref.at[m, dst], sems.at[0, m]))
            copies[-1].start()
        for copy in copies:
            copy.wait()

    return finish_far


VM = pl.BlockSpec(memory_space=pltpu.VMEM)
HB = pl.BlockSpec(memory_space=pltpu.HBM)


def call(kernel, outs, args, name, cost, hbm=(), hbm_out=(), scratch=(), alias={}):
    specs = [HB if n in hbm else VM for n in range(len(args))]
    out_specs = [HB if n in hbm_out else VM for n in range(len(outs))]
    shapes = [jax.ShapeDtypeStruct(s, jnp.int32 if s == (SUB, LANES) else jnp.float32) for s in outs]
    single = len(outs) == 1
    return pl.pallas_call(
        kernel,
        out_shape=shapes[0] if single else shapes,
        in_specs=specs,
        out_specs=out_specs[0] if single else out_specs,
        scratch_shapes=list(scratch),
        input_output_aliases=alias,
        name=name,
        compiler_params=pltpu.CompilerParams(vmem_limit_bytes=8 << 20),
        cost_estimate=pl.CostEstimate(
            flops=cost * 1000000, bytes_accessed=1 << 10, transcendentals=0
        ),
    )(*args)


def per_device(scalars, transport, mass, element_order):
    count = lax.axis_size("elem")
    even_pairs = [(i, i ^ 1) for i in range(count)]
    odd_pairs = [(i, (i + 1) % count if i % 2 else (i - 1) % count) for i in range(count)]
    swap_od = lambda x: lax.ppermute(x, "elem", odd_pairs)
    swap_ev = lambda x: lax.ppermute(x, "elem", even_pairs)
    members = scalars.shape[0]
    grid = (EXT, EXT, SUB, LANES)
    scal = scalars.reshape((members,) + grid)
    tr = transport.reshape((3,) + grid)
    mas = mass.reshape(grid)
    tile, part = (EXT, SUB, LANES), (ROWS, SUB, LANES)
    inner, face, faces = (2, 6) + tile, (2,) + part, (2, 2) + part
    sent, geometry = (2 * ROWS, SUB, LANES), (3,) + tile
    f32 = jnp.float32

    stay = lambda x: pltpu.with_memory_space_constraint(x, pltpu.HBM)
    bundle = (3 * ROWS + 24, SUB, LANES)
    od, idx, slots, raw = call(
        project_odd, [(3 * ROWS, SUB, LANES), (SUB, LANES), (SUB, LANES), (9,) + tile],
        (stay(element_order), stay(scal), stay(mas), stay(tr)), "project", 1, hbm=(0, 1, 2, 3),
        scratch=[pltpu.VMEM((1, LANES), jnp.int32), pltpu.VMEM((3,) + tile, f32),
                 pltpu.SemaphoreType.DMA((13,))])
    rod = swap_od(od)
    ev, tf = call(project_even, [bundle, (24, SUB, LANES)], (idx, raw), "project", 1)
    rev, rtf = swap_ev(ev), swap_od(tf)
    gi, q, ri, rt, ti, st = call(
        prepare, [inner, faces, (6,) + tile, (6,) + tile, (6, 2) + tile, (2,) + part],
        (idx, scal, mas, tr), "prepare", 1)
    p0, r0, cev = call(make_field_face(0), [face, part, sent], (od, rod, q, st), "odd", 3000)
    p7, r7, cod = call(make_field_face(1), [face, part, sent], (ev, rev, q, st), "even", 1)
    acci, accf, wp = gi, q, gi
    pairs = SUBSTEPS * STAGES // 2
    for n in range(pairs):
        s = 2 * n % STAGES + 1
        opening, closing, early = s == 1, s + 1 == STAGES, n == 0
        got_ev, got_od = swap_ev(cev), swap_od(cod)
        extra = (tf, rtf, ev, rev, st, r0, ri, ti) if early else (acci, wp, a7)
        res = call(
            make_first_inner(1.0 / s, opening, early),
            [inner, inner, faces, face] + ([geometry, geometry, (2,) + part] if early else []),
            (p0, p7, gi, rt, r7) + extra, "first", 1000,
            scratch=[pltpu.VMEM(inner, f32)] if early else [])
        gm, acci, q, e7 = res[:4]
        if early:
            a0, a7, rs = res[4:]
        m7, cod2 = call(
            make_stage_face(1, 1.0 / s, False, early), [face, sent],
            (cev, got_ev, e7, accf, q, rs, r7), "ahead", 1)
        got_od2 = swap_od(cod2)
        wp, e7, e0 = call(
            between, [inner, face, face], (m7, gm, a7, r7, ri, rt, ti, p0, a0, r0), "between", 2000)
        m0, cev2 = call(
            make_stage_face(0, 1.0 / s, False, early), [face, sent],
            (cod, got_od, e0, accf, q, rs, r0), "behind", 1)
        got_ev2 = swap_ev(cev2)
        scale = 1.0 / (s + 1)
        if n < pairs - 1:
            gi, q, acci, accf, wp, e0 = call(
                make_second_inner(scale, opening, closing),
                [inner, faces, inner, faces, inner, face],
                (m0, m7, p0, p7, accf, acci, wp, ri, rt, ti, a0, r0), "second", 3000)
            p0, cev = call(
                make_stage_face(0, scale, closing, False), [face, sent],
                (cod2, got_od2, e0, accf, q, rs, r0), "odd", 3000)
            p7, cod = call(
                make_stage_face(1, scale, closing, False), [face, sent],
                (cev2, got_ev2, e7, accf, q, rs, r7), "even", 1)
        else:
            out, accf, e0 = call(
                make_last_inner(scale), [(members,) + grid, faces, face],
                (slots, m0, m7, p0, p7, accf, acci, wp, rt, a0, r0), "last", 3000,
                hbm_out=(0,), scratch=[pltpu.VMEM(inner, f32), pltpu.SemaphoreType.DMA((2,))])
            near = call(
                make_finish_near(0, scale), [(2,) + tile],
                (slots, cod2, got_od2, e0, accf), "finish", 3000)
            out = call(
                make_finish_far(1, scale), [(members,) + grid],
                (slots, cev2, got_ev2, e7, accf, near, out), "finish", 1,
                hbm=(6,), hbm_out=(0,), alias={6: 0},
                scratch=[pltpu.VMEM((2,) + tile, f32), pltpu.SemaphoreType.DMA((2, 2))])
    return out.reshape(scalars.shape)


def solution(mesh):
    in_specs = (P("ens", None, "elem"), P(None, None, "elem"), P(None, "elem"), P("elem", None))
    out_specs = P("ens", None, "elem")
    return jax.shard_map(
        per_device, mesh=mesh, in_specs=in_specs, out_specs=out_specs, check_vma=False
    )
```

```python
import jax
import jax.numpy as jnp
import numpy as np
from jax import lax
from jax.experimental import pallas as pl
from jax.experimental.pallas import tpu as pltpu
from jax.sharding import PartitionSpec as P

ORDER = 7
EXT = ORDER + 1
SUBSTEPS = 2
STAGES = 4
EY = 8
EZ = 16
LANES = EY * EZ
SUB = 8
ROWS = 7

time_step = 0.015


def legendre_table(points, degree):
    table = np.zeros((points.shape[0], degree + 1))
    table[:, 0] = 1.0
    table[:, 1] = points
    for level in range(2, degree + 1):
        table[:, level] = (
            (2 * level - 1) * points * table[:, level - 1] - (level - 1) * table[:, level - 2]
        ) / level
    return table


def gll_derivative(degree):
    extent = degree + 1
    points = np.cos(np.pi * np.arange(extent) / degree)
    for sweep in range(60):
        table = legendre_table(points, degree)
        points = points - (points * table[:, degree] - table[:, degree - 1]) / (
            extent * table[:, degree]
        )
    points = points[::-1].copy()
    values = legendre_table(points, degree)[:, degree]
    matrix = np.zeros((extent, extent))
    for target in range(extent):
        for source in range(extent):
            if target != source:
                matrix[target, source] = values[target] / (
                    values[source] * (points[target] - points[source])
                )
    matrix[0, 0] = -degree * (degree + 1) / 4.0
    matrix[extent - 1, extent - 1] = degree * (degree + 1) / 4.0
    return matrix


DM = gll_derivative(ORDER)
SUM_PART = [[(DM[j, a] + DM[j, 7 - a]) / 2 for a in range(4)] for j in range(4)]
DIF_PART = [[(DM[j, a] - DM[j, 7 - a]) / 2 for a in range(4)] for j in range(4)]


def combine(coefs, items):
    total = None
    for c, x in zip(coefs, items):
        term = x * np.float32(c)
        total = term if total is None else total + term
    return total


def along_second(plane):
    even = [plane[a] + plane[7 - a] for a in range(4)]
    odd = [plane[a] - plane[7 - a] for a in range(4)]
    out = [None] * 8
    for j in range(4):
        e = combine(SUM_PART[j], even)
        o = combine(DIF_PART[j], odd)
        out[j] = o + e
        out[7 - j] = o - e
    return out


def along_third(x, rot):
    total = x * rot[0]
    for r in range(1, 8):
        total = total + pltpu.roll(x, r, 0) * rot[r]
    return total


def gather_lanes(x, idx):
    return jnp.take_along_axis(x, idx, axis=1, mode="promise_in_bounds")


def third_tables():
    lane = lax.broadcasted_iota(jnp.int32, (SUB, LANES), 1)
    k = lax.broadcasted_iota(jnp.int32, (SUB, LANES), 0)
    z = lane % EZ
    back = jnp.where(z == 0, lane + (EZ - 1), lane - 1)
    ahead = jnp.where(z == EZ - 1, lane - (EZ - 1), lane + 1)
    return jnp.where(k == 0, back, ahead), k == 0, k == ORDER


def plane_sum(plane, tables, rows=EXT):
    idx, first, last = tables
    up = plane[7] + pltpu.roll(plane[0], LANES - EZ, 1)
    plane = [pltpu.roll(up, EZ, 1)] + list(plane[1:7]) + [up]
    out = []
    for v in plane[:rows]:
        x = jnp.where(first, pltpu.roll(v, 1, 0), jnp.where(last, pltpu.roll(v, 7, 0), 0.0))
        out.append(v + gather_lanes(x, idx))
    return out


def full(rows):
    return list(rows) + [pltpu.roll(rows[0], LANES - EZ, 1)]


def write(ref, lead, plane):
    for j, v in enumerate(plane):
        ref[lead + (j,)] = v


def read(ref, *lead, rows=EXT):
    return [ref[lead + (j,)] for j in range(rows)]


def brick_index(order_ref):
    order = jnp.broadcast_to(order_ref[...], (LANES, LANES))
    pos = lax.broadcasted_iota(jnp.int32, (LANES, LANES), 0)
    hot = jnp.where(order == pos, 1.0, 0.0).astype(jnp.bfloat16)
    slot = lax.broadcasted_iota(jnp.int32, (SUB, LANES), 1).astype(jnp.float32).astype(jnp.bfloat16)
    found = lax.dot_general(
        slot, hot, (((1,), (1,)), ((), ())), preferred_element_type=jnp.float32
    )
    return found.astype(jnp.int32)


def source_plane(parity, i):
    return jnp.where(parity == 1, ORDER - i, i)


def source_plane(parity, i):
    return jnp.where(parity == 1, ORDER - i, i)


def project(weight, scal, idx, tables):
    weight = [gather_lanes(v, idx) for v in weight]
    planes = [[gather_lanes(plane[j], idx) * weight[j] for j in range(8)] for plane in scal]
    return [plane_sum(plane, tables, ROWS) for plane in planes + [weight]]


def project_odd(order_ref, scal_ref, mass_ref, tr_ref, od_ref, idx_ref, slot_ref, raw_ref,
                order_buf, near_buf, sems):
    parity = lax.axis_index("elem") % 2
    near, far = source_plane(parity, 0), source_plane(parity, ORDER)
    copies = [
        pltpu.make_async_copy(order_ref, order_buf, sems.at[0]),
        pltpu.make_async_copy(mass_ref.at[near], near_buf.at[2], sems.at[1]),
        pltpu.make_async_copy(scal_ref.at[:, near], near_buf.at[pl.ds(0, 2)], sems.at[2]),
    ]
    late = [
        pltpu.make_async_copy(scal_ref.at[:, far], raw_ref.at[pl.ds(0, 2)], sems.at[3]),
        pltpu.make_async_copy(mass_ref.at[far], raw_ref.at[2], sems.at[4]),
        pltpu.make_async_copy(tr_ref.at[:, far], raw_ref.at[pl.ds(3, 3)], sems.at[5]),
        pltpu.make_async_copy(tr_ref.at[:, near], raw_ref.at[pl.ds(6, 3)], sems.at[6]),
    ]
    for copy in copies + late:
        copy.start()
    tables = third_tables()
    copies[0].wait()
    idx = brick_index(order_buf)
    idx_ref[...] = idx
    slot_ref[...] = jnp.broadcast_to(order_buf[...], (SUB, LANES))
    for copy in copies[1:]:
        copy.wait()
    planes = project(read(near_buf, 2), [read(near_buf, m) for m in range(2)], idx, tables)
    write(od_ref, (), sum(planes, []))
    for copy in late:
        copy.wait()


def signs_of(parity):
    first = jnp.where(parity == 1, time_step, -time_step).astype(jnp.float32)
    return first, np.float32(-time_step), np.float32(-time_step)


def project_even(idx_ref, raw_ref, ev_ref, tf_ref):
    idx = idx_ref[...]
    signs = signs_of(lax.axis_index("elem") % 2)
    planes = project(read(raw_ref, 2), [read(raw_ref, m) for m in range(2)], idx, third_tables())
    turned = [[gather_lanes(v, idx) * signs[r % 3] for v in read(raw_ref, 3 + r)] for r in range(6)]
    write(ev_ref, (), sum(planes + turned[:3], []))
    write(tf_ref, (), sum(turned[3:], []))


def prepare(idx_ref, scal_ref, mass_ref, tr_ref,
            gi_ref, q_ref, ri_ref, rt_ref, ti_ref, st_ref):
    parity = lax.axis_index("elem") % 2
    idx = idx_ref[...]
    tables = third_tables()
    signs = signs_of(parity)

    def load(i):
        src = source_plane(parity, i)
        planes = [read(scal_ref, m, src) for m in range(2)] + [read(mass_ref, src)]
        return planes + [read(tr_ref, r, src) for r in range(3)]

    faces = [read(tr_ref, 0, source_plane(parity, face * ORDER)) for face in range(2)]
    ahead = load(1)
    for face in range(2):
        first = [gather_lanes(v, idx) * signs[0] for v in faces[face]]
        write(st_ref, (face,), plane_sum(first, tables, ROWS))
    sums = [[None, None], [None, None]]
    for i in range(6):
        raw = [[gather_lanes(v, idx) for v in plane] for plane in ahead]
        weight = raw[2]
        first = plane_sum([v * signs[0] for v in raw[3]], tables)
        inverse = [1.0 / v for v in plane_sum(weight, tables)]
        rest = [[v * signs[r] for v in raw[3 + r]] for r in (1, 2)]
        planes = []
        for m in range(2):
            plane = plane_sum([raw[m][j] * weight[j] for j in range(8)], tables)
            planes.append([plane[j] * inverse[j] for j in range(8)])
        if i < 5:
            ahead = load(i + 2)
        for r in range(2):
            write(ti_ref, (i, r), rest[r])
        write(ri_ref, (i,), inverse)
        write(rt_ref, (i,), [first[j] * inverse[j] for j in range(8)])
        for m in range(2):
            write(gi_ref, (m, i), planes[m])
            for face in range(2):
                terms = [v * np.float32(DM[face * ORDER, i + 1]) for v in planes[m][:ROWS]]
                old = sums[face][m]
                sums[face][m] = [x + y for x, y in zip(old, terms)] if old else terms
    for face in range(2):
        for m in range(2):
            write(q_ref, (face, m), sums[face][m])


def rotations():
    k = lax.broadcasted_iota(jnp.int32, (SUB, LANES), 0)
    out = []
    for r in range(8):
        value = jnp.full((SUB, LANES), np.float32(DM[7, (7 - r) % 8]))
        for row in range(7):
            value = jnp.where(k == row, np.float32(DM[row, (row - r) % 8]), value)
        out.append(value)
    return out


def in_plane(plane, second_t, third_t, rot):
    second = along_second(plane)
    return [second_t[j] * second[j] + third_t[j] * along_third(plane[j], rot) for j in range(8)]


def inner_open(gi_ref, ri_ref, rt_ref, ti_ref, rot, wp_ref):
    tables = third_tables()
    for m in range(2):
        for j in range(8):
            rows = [gi_ref[m, a, j] for a in range(6)]
            even = [rows[a] + rows[5 - a] for a in range(3)]
            odd = [rows[a] - rows[5 - a] for a in range(3)]
            for i in range(3):
                e = combine([(DM[i + 1, a + 1] + DM[i + 1, 6 - a]) / 2 for a in range(3)], even)
                o = combine([(DM[i + 1, a + 1] - DM[i + 1, 6 - a]) / 2 for a in range(3)], odd)
                wp_ref[m, i, j] = (o + e) * rt_ref[i, j]
                wp_ref[m, 5 - i, j] = (o - e) * rt_ref[5 - i, j]
    for i in range(6):
        for m in range(2):
            plane = in_plane(read(gi_ref, m, i), read(ti_ref, i, 0), read(ti_ref, i, 1), rot)
            plane = plane_sum(plane, tables)
            write(wp_ref, (m, i), [wp_ref[m, i, j] + ri_ref[i, j] * plane[j] for j in range(8)])


def inner_close(p0_ref, p7_ref, wp_ref, rt_ref, scale, put, q_ref=None):
    for m in range(2):
        p0, p7 = full(read(p0_ref, m, rows=ROWS)), full(read(p7_ref, m, rows=ROWS))
        sums = [[], []]
        for i in range(6):
            near, far = np.float32(scale * DM[i + 1, 0]), np.float32(scale * DM[i + 1, ORDER])
            kept = put(m, i, [
                wp_ref[m, i, j] * np.float32(scale) + rt_ref[i, j] * (p0[j] * near + p7[j] * far)
                for j in range(8)
            ])
            for face in range(2):
                terms = [v * np.float32(DM[face * ORDER, i + 1]) for v in kept[:ROWS]]
                sums[face] = [x + y for x, y in zip(sums[face], terms)] if i else terms
        if q_ref is not None:
            for face in range(2):
                write(q_ref, (face, m), sums[face])


def own_terms(p_ref, a_ref, rf_ref, face, rot, tables, e_ref):
    second_t, third_t = read(a_ref, 0), read(a_ref, 1)
    for m in range(2):
        p = full(read(p_ref, m, rows=ROWS))
        plane = plane_sum(in_plane(p, second_t, third_t, rot), tables, ROWS)
        write(e_ref, (m,), [
            rf_ref[j] * (plane[j] + a_ref[2, j] * (p[j] * np.float32(DM[face * ORDER, face * ORDER])))
            for j in range(ROWS)
        ])


def both_sides(own, got, tables, a_ref):
    total = [[own[r][j] + got[r][j] for j in range(8)] for r in range(3)]
    write(a_ref, (0,), total[1])
    write(a_ref, (1,), total[2])
    write(a_ref, (2,), plane_sum(total[0], tables, ROWS))


def transports(ref, start):
    return [[ref[start + 8 * r + j] for j in range(8)] for r in range(3)]


def make_field_face(face):
    far = np.float32(DM[ORDER - face * ORDER, face * ORDER])

    def field_face(own_ref, got_ref, q_ref, st_ref, p_ref, rf_ref, send_ref):
        inverse = [1.0 / (own_ref[14 + j] + got_ref[14 + j]) for j in range(ROWS)]
        p = [
            [(own_ref[ROWS * m + j] + got_ref[ROWS * m + j]) * inverse[j] for j in range(ROWS)]
            for m in range(2)
        ]
        sent = [
            [st_ref[1 - face, j] * (q_ref[1 - face, m, j] + p[m][j] * far) for j in range(ROWS)]
            for m in range(2)
        ]
        write(send_ref, (), sent[0] + sent[1])
        for m in range(2):
            write(p_ref, (m,), p[m])
        write(rf_ref, (), inverse)

    return field_face


def make_stage_face(face, scale, total, raw):
    far = np.float32(DM[ORDER - face * ORDER, face * ORDER])
    scale = np.float32(scale)

    def stage_face(own_ref, got_ref, e_ref, acc_ref, q_ref, rt_ref, rf_ref, p_ref, send_ref):
        p = []
        for m in range(2):
            value = [own_ref[ROWS * m + j] + got_ref[ROWS * m + j] for j in range(ROWS)]
            if raw:
                value = [value[j] * rf_ref[j] for j in range(ROWS)]
            value = [(value[j] + e_ref[m, j]) * scale for j in range(ROWS)]
            if total:
                value = [value[j] + acc_ref[face, m, j] for j in range(ROWS)]
            p.append(value)
        sent = [
            [rt_ref[1 - face, j] * (q_ref[1 - face, m, j] + p[m][j] * far) for j in range(ROWS)]
            for m in range(2)
        ]
        write(send_ref, (), sent[0] + sent[1])
        for m in range(2):
            write(p_ref, (m,), p[m])

    return stage_face


def make_first_inner(scale, opening, start):
    def first_inner(*refs):
        p0_ref, p7_ref, gi_ref, rt_ref, r7_ref = refs[:5]
        tables = third_tables()
        rot = rotations()
        if start:
            tf_ref, rtf_ref, ev_ref, rev_ref, st_ref, r0_ref, wp_ref = refs[5:12]
            gn_ref, an_ref, q_ref, e7_ref, a0_ref, a7_ref, rs_ref = refs[12:]
            both_sides(transports(tf_ref, 0), transports(rtf_ref, 0), tables, a0_ref)
            both_sides(
                transports(ev_ref, 3 * ROWS), transports(rev_ref, 3 * ROWS), tables, a7_ref)
            write(rs_ref, (0,), [st_ref[0, j] * r0_ref[j] for j in range(ROWS)])
            write(rs_ref, (1,), [st_ref[1, j] * r7_ref[j] for j in range(ROWS)])
        else:
            acci_ref, wp_ref, a7_ref = refs[5:8]
            gn_ref, an_ref, q_ref, e7_ref = refs[8:]
        own_terms(p7_ref, a7_ref, r7_ref, 1, rot, tables, e7_ref)

        def put(m, i, value):
            base = gi_ref if opening else acci_ref
            write(gn_ref, (m, i), value)
            write(an_ref, (m, i), [base[m, i, j] + value[j] for j in range(8)])
            return value

        inner_close(p0_ref, p7_ref, wp_ref, rt_ref, scale, put, q_ref)

    return first_inner


def between(m7_ref, gi_ref, a7_ref, r7_ref, ri_ref, rt_ref, ti_ref, p0_ref, a0_ref, r0_ref,
            wp_ref, e7_ref, e0_ref):
    rot = rotations()
    tables = third_tables()
    own_terms(p0_ref, a0_ref, r0_ref, 0, rot, tables, e0_ref)
    own_terms(m7_ref, a7_ref, r7_ref, 1, rot, tables, e7_ref)
    inner_open(gi_ref, ri_ref, rt_ref, ti_ref, rot, wp_ref)


def face_totals(now, before, accf_ref, afn_ref, opening):
    for face in range(2):
        for m in range(2):
            for j in range(ROWS):
                value = now[face][m, j] + before[face][m, j]
                afn_ref[face, m, j] = value if opening else value + accf_ref[face, m, j]


def make_second_inner(scale, opening, closing):
    def second_inner(m0_ref, m7_ref, p0_ref, p7_ref, accf_ref, acci_ref, wp_ref, ri_ref, rt_ref,
                     ti_ref, a0_ref, r0_ref, gn_ref, q_ref, an_ref, afn_ref, wn_ref, e0_ref):
        rot = rotations()

        def put(m, i, value):
            total = [acci_ref[m, i, j] + value[j] for j in range(8)]
            kept = total if closing else value
            write(gn_ref, (m, i), kept)
            if not closing:
                write(an_ref, (m, i), total)
            return kept

        inner_close(m0_ref, m7_ref, wp_ref, rt_ref, scale, put, q_ref)
        own_terms(m0_ref, a0_ref, r0_ref, 0, rot, third_tables(), e0_ref)
        face_totals((m0_ref, m7_ref), (p0_ref, p7_ref), accf_ref, afn_ref, opening)
        inner_open(gn_ref, ri_ref, rt_ref, ti_ref, rot, wn_ref)

    return second_inner


def make_last_inner(scale):
    def last_inner(slot_ref, m0_ref, m7_ref, p0_ref, p7_ref, accf_ref, acci_ref, wp_ref, rt_ref,
                   a0_ref, r0_ref, out_ref, afn_ref, e0_ref, buf, sems):
        parity = lax.axis_index("elem") % 2
        idx = slot_ref[...]

        def put(m, i, value):
            total = [acci_ref[m, i, j] + value[j] for j in range(8)]
            dst = source_plane(parity, i + 1) - 1
            write(buf, (m, dst), [gather_lanes(v, idx) for v in total])
            return total

        inner_close(m0_ref, m7_ref, wp_ref, rt_ref, scale, put)
        copies = [
            pltpu.make_async_copy(buf.at[m], out_ref.at[m, pl.ds(1, 6)], sems.at[m])
            for m in range(2)
        ]
        for copy in copies:
            copy.start()
        own_terms(m0_ref, a0_ref, r0_ref, 0, rotations(), third_tables(), e0_ref)
        face_totals((m0_ref, m7_ref), (p0_ref, p7_ref), accf_ref, afn_ref, False)
        for copy in copies:
            copy.wait()

    return last_inner


def final_face(face, scale, slot_ref, own_ref, got_ref, e_ref, accf_ref, m):
    idx = slot_ref[...]
    rows = [
        (own_ref[ROWS * m + j] + got_ref[ROWS * m + j] + e_ref[m, j]) * np.float32(scale)
        + accf_ref[face, m, j]
        for j in range(ROWS)
    ]
    return [gather_lanes(v, idx) for v in full(rows)]


def make_finish_near(face, scale):
    def finish_near(slot_ref, own_ref, got_ref, e_ref, accf_ref, face_ref):
        for m in range(2):
            write(face_ref, (m,), final_face(face, scale, slot_ref, own_ref, got_ref, e_ref, accf_ref, m))

    return finish_near


def make_finish_far(face, scale):
    def finish_far(slot_ref, own_ref, got_ref, e_ref, accf_ref, near_ref, part_ref,
                   out_ref, buf, sems):
        dst = source_plane(lax.axis_index("elem") % 2, face * ORDER)
        copies = []
        for m in range(2):
            copies.append(
                pltpu.make_async_copy(near_ref.at[m], out_ref.at[m, ORDER - dst], sems.at[1, m])
            )
            copies[-1].start()
        for m in range(2):
            write(buf, (m,), final_face(face, scale, slot_ref, own_ref, got_ref, e_ref, accf_ref, m))
            copies.append(pltpu.make_async_copy(buf.at[m], out_ref.at[m, dst], sems.at[0, m]))
            copies[-1].start()
        for copy in copies:
            copy.wait()

    return finish_far


VM = pl.BlockSpec(memory_space=pltpu.VMEM)
HB = pl.BlockSpec(memory_space=pltpu.HBM)


def call(kernel, outs, args, name, cost, hbm=(), hbm_out=(), scratch=(), alias={}):
    specs = [HB if n in hbm else VM for n in range(len(args))]
    out_specs = [HB if n in hbm_out else VM for n in range(len(outs))]
    shapes = [jax.ShapeDtypeStruct(s, jnp.int32 if s == (SUB, LANES) else jnp.float32) for s in outs]
    single = len(outs) == 1
    return pl.pallas_call(
        kernel,
        out_shape=shapes[0] if single else shapes,
        in_specs=specs,
        out_specs=out_specs[0] if single else out_specs,
        scratch_shapes=list(scratch),
        input_output_aliases=alias,
        name=name,
        compiler_params=pltpu.CompilerParams(vmem_limit_bytes=8 << 20),
        cost_estimate=pl.CostEstimate(
            flops=cost * 1000000, bytes_accessed=1 << 10, transcendentals=0
        ),
    )(*args)


def per_device(scalars, transport, mass, element_order):
    count = lax.axis_size("elem")
    even_pairs = [(i, i ^ 1) for i in range(count)]
    odd_pairs = [(i, (i + 1) % count if i % 2 else (i - 1) % count) for i in range(count)]
    swap_od = lambda x: lax.ppermute(x, "elem", odd_pairs)
    swap_ev = lambda x: lax.ppermute(x, "elem", even_pairs)
    members = scalars.shape[0]
    grid = (EXT, EXT, SUB, LANES)
    scal = scalars.reshape((members,) + grid)
    tr = transport.reshape((3,) + grid)
    mas = mass.reshape(grid)
    tile, part = (EXT, SUB, LANES), (ROWS, SUB, LANES)
    inner, face, faces = (2, 6) + tile, (2,) + part, (2, 2) + part
    sent, geometry = (2 * ROWS, SUB, LANES), (3,) + tile
    f32 = jnp.float32

    stay = lambda x: pltpu.with_memory_space_constraint(x, pltpu.HBM)
    bundle = (3 * ROWS + 24, SUB, LANES)
    od, idx, slots, raw = call(
        project_odd, [(3 * ROWS, SUB, LANES), (SUB, LANES), (SUB, LANES), (9,) + tile],
        (stay(element_order), stay(scal), stay(mas), stay(tr)), "project", 1, hbm=(0, 1, 2, 3),
        scratch=[pltpu.VMEM((1, LANES), jnp.int32), pltpu.VMEM((3,) + tile, f32),
                 pltpu.SemaphoreType.DMA((7,))])
    rod = swap_od(od)
    ev, tf = call(project_even, [bundle, (24, SUB, LANES)], (idx, raw), "project", 1)
    rev, rtf = swap_ev(ev), swap_od(tf)
    gi, q, ri, rt, ti, st = call(
        prepare, [inner, faces, (6,) + tile, (6,) + tile, (6, 2) + tile, (2,) + part],
        (idx, scal, mas, tr), "prepare", 1)
    p0, r0, cev = call(make_field_face(0), [face, part, sent], (od, rod, q, st), "odd", 3000)

    def opening_terms(gi_ref, ri_ref, rt_ref, ti_ref, after_ref, wp_ref):
        inner_open(gi_ref, ri_ref, rt_ref, ti_ref, rotations(), wp_ref)

    wp = call(opening_terms, [inner], (gi, ri, rt, ti, r0), "terms", 1)
    p7, r7, cod = call(make_field_face(1), [face, part, sent], (ev, rev, q, st), "even", 1)
    acci, accf = gi, q
    pairs = SUBSTEPS * STAGES // 2
    for n in range(pairs):
        s = 2 * n % STAGES + 1
        opening, closing, early = s == 1, s + 1 == STAGES, n == 0
        got_ev, got_od = swap_ev(cev), swap_od(cod)
        extra = (tf, rtf, ev, rev, st, r0, wp) if early else (acci, wp, a7)
        res = call(
            make_first_inner(1.0 / s, opening, early),
            [inner, inner, faces, face] + ([geometry, geometry, (2,) + part] if early else []),
            (p0, p7, gi, rt, r7) + extra, "first", 1000)
        gm, acci, q, e7 = res[:4]
        if early:
            a0, a7, rs = res[4:]
        m7, cod2 = call(
            make_stage_face(1, 1.0 / s, False, early), [face, sent],
            (cev, got_ev, e7, accf, q, rs, r7), "ahead", 1)
        got_od2 = swap_od(cod2)
        wp, e7, e0 = call(
            between, [inner, face, face], (m7, gm, a7, r7, ri, rt, ti, p0, a0, r0), "between", 2000)
        m0, cev2 = call(
            make_stage_face(0, 1.0 / s, False, early), [face, sent],
            (cod, got_od, e0, accf, q, rs, r0), "behind", 1)
        got_ev2 = swap_ev(cev2)
        scale = 1.0 / (s + 1)
        if n < pairs - 1:
            gi, q, acci, accf, wp, e0 = call(
                make_second_inner(scale, opening, closing),
                [inner, faces, inner, faces, inner, face],
                (m0, m7, p0, p7, accf, acci, wp, ri, rt, ti, a0, r0), "second", 3000)
            p0, cev = call(
                make_stage_face(0, scale, closing, False), [face, sent],
                (cod2, got_od2, e0, accf, q, rs, r0), "odd", 3000)
            p7, cod = call(
                make_stage_face(1, scale, closing, False), [face, sent],
                (cev2, got_ev2, e7, accf, q, rs, r7), "even", 1)
        else:
            out, accf, e0 = call(
                make_last_inner(scale), [(members,) + grid, faces, face],
                (slots, m0, m7, p0, p7, accf, acci, wp, rt, a0, r0), "last", 3000,
                hbm_out=(0,), scratch=[pltpu.VMEM(inner, f32), pltpu.SemaphoreType.DMA((2,))])
            near = call(
                make_finish_near(0, scale), [(2,) + tile],
                (slots, cod2, got_od2, e0, accf), "finish", 3000)
            out = call(
                make_finish_far(1, scale), [(members,) + grid],
                (slots, cev2, got_ev2, e7, accf, near, out), "finish", 1,
                hbm=(6,), hbm_out=(0,), alias={6: 0},
                scratch=[pltpu.VMEM((2,) + tile, f32), pltpu.SemaphoreType.DMA((2, 2))])
    return out.reshape(scalars.shape)


def solution(mesh):
    in_specs = (P("ens", None, "elem"), P(None, None, "elem"), P(None, "elem"), P("elem", None))
    out_specs = P("ens", None, "elem")
    return jax.shard_map(
        per_device, mesh=mesh, in_specs=in_specs, out_specs=out_specs, check_vma=False
    )
```

```python
import jax
import jax.numpy as jnp
import numpy as np
from jax import lax
from jax.experimental import pallas as pl
from jax.experimental.pallas import tpu as pltpu
from jax.sharding import PartitionSpec as P

ORDER = 7
EXT = ORDER + 1
SUBSTEPS = 2
STAGES = 4
EY = 8
EZ = 16
LANES = EY * EZ
SUB = 8
ROWS = 7

time_step = 0.015


def legendre_table(points, degree):
    table = np.zeros((points.shape[0], degree + 1))
    table[:, 0] = 1.0
    table[:, 1] = points
    for level in range(2, degree + 1):
        table[:, level] = (
            (2 * level - 1) * points * table[:, level - 1] - (level - 1) * table[:, level - 2]
        ) / level
    return table


def gll_derivative(degree):
    extent = degree + 1
    points = np.cos(np.pi * np.arange(extent) / degree)
    for sweep in range(60):
        table = legendre_table(points, degree)
        points = points - (points * table[:, degree] - table[:, degree - 1]) / (
            extent * table[:, degree]
        )
    points = points[::-1].copy()
    values = legendre_table(points, degree)[:, degree]
    matrix = np.zeros((extent, extent))
    for target in range(extent):
        for source in range(extent):
            if target != source:
                matrix[target, source] = values[target] / (
                    values[source] * (points[target] - points[source])
                )
    matrix[0, 0] = -degree * (degree + 1) / 4.0
    matrix[extent - 1, extent - 1] = degree * (degree + 1) / 4.0
    return matrix


DM = gll_derivative(ORDER)
SUM_PART = [[(DM[j, a] + DM[j, 7 - a]) / 2 for a in range(4)] for j in range(4)]
DIF_PART = [[(DM[j, a] - DM[j, 7 - a]) / 2 for a in range(4)] for j in range(4)]


def combine(coefs, items):
    total = None
    for c, x in zip(coefs, items):
        term = x * np.float32(c)
        total = term if total is None else total + term
    return total


def along_second(plane):
    even = [plane[a] + plane[7 - a] for a in range(4)]
    odd = [plane[a] - plane[7 - a] for a in range(4)]
    out = [None] * 8
    for j in range(4):
        e = combine(SUM_PART[j], even)
        o = combine(DIF_PART[j], odd)
        out[j] = o + e
        out[7 - j] = o - e
    return out


def along_third(x, rot):
    total = x * rot[0]
    for r in range(1, 8):
        total = total + pltpu.roll(x, r, 0) * rot[r]
    return total


def gather_lanes(x, idx):
    return jnp.take_along_axis(x, idx, axis=1, mode="promise_in_bounds")


def third_tables():
    lane = lax.broadcasted_iota(jnp.int32, (SUB, LANES), 1)
    k = lax.broadcasted_iota(jnp.int32, (SUB, LANES), 0)
    z = lane % EZ
    back = jnp.where(z == 0, lane + (EZ - 1), lane - 1)
    ahead = jnp.where(z == EZ - 1, lane - (EZ - 1), lane + 1)
    return jnp.where(k == 0, back, ahead), k == 0, k == ORDER


def plane_sum(plane, tables, rows=EXT):
    idx, first, last = tables
    up = plane[7] + pltpu.roll(plane[0], LANES - EZ, 1)
    plane = [pltpu.roll(up, EZ, 1)] + list(plane[1:7]) + [up]
    out = []
    for v in plane[:rows]:
        x = jnp.where(first, pltpu.roll(v, 1, 0), jnp.where(last, pltpu.roll(v, 7, 0), 0.0))
        out.append(v + gather_lanes(x, idx))
    return out


def full(rows):
    return list(rows) + [pltpu.roll(rows[0], LANES - EZ, 1)]


def write(ref, lead, plane):
    for j, v in enumerate(plane):
        ref[lead + (j,)] = v


def read(ref, *lead, rows=EXT):
    return [ref[lead + (j,)] for j in range(rows)]


def brick_index(order_ref):
    order = jnp.broadcast_to(order_ref[...], (LANES, LANES))
    pos = lax.broadcasted_iota(jnp.int32, (LANES, LANES), 0)
    hot = jnp.where(order == pos, 1.0, 0.0).astype(jnp.bfloat16)
    slot = lax.broadcasted_iota(jnp.int32, (SUB, LANES), 1).astype(jnp.float32).astype(jnp.bfloat16)
    found = lax.dot_general(
        slot, hot, (((1,), (1,)), ((), ())), preferred_element_type=jnp.float32
    )
    return found.astype(jnp.int32)


def source_plane(parity, i):
    return jnp.where(parity == 1, ORDER - i, i)


def source_plane(parity, i):
    return jnp.where(parity == 1, ORDER - i, i)


def project(weight, scal, idx, tables):
    weight = [gather_lanes(v, idx) for v in weight]
    planes = [[gather_lanes(plane[j], idx) * weight[j] for j in range(8)] for plane in scal]
    return [plane_sum(plane, tables, ROWS) for plane in planes + [weight]]


def project_odd(order_ref, scal_ref, mass_ref, tr_ref, od_ref, idx_ref, slot_ref, raw_ref,
                order_buf, near_buf, sems):
    parity = lax.axis_index("elem") % 2
    near, far = source_plane(parity, 0), source_plane(parity, ORDER)
    copies = [pltpu.make_async_copy(order_ref, order_buf, sems.at[0])]
    for r, source in enumerate((scal_ref.at[0, near], scal_ref.at[1, near], mass_ref.at[near])):
        copies.append(pltpu.make_async_copy(source, near_buf.at[r], sems.at[1 + r]))
    sources = [scal_ref.at[0, far], scal_ref.at[1, far], mass_ref.at[far]]
    sources += [tr_ref.at[r, far] for r in range(3)] + [tr_ref.at[r, near] for r in range(3)]
    late = [
        pltpu.make_async_copy(source, raw_ref.at[r], sems.at[4 + r])
        for r, source in enumerate(sources)
    ]
    for copy in copies + late:
        copy.start()
    tables = third_tables()
    copies[0].wait()
    idx = brick_index(order_buf)
    idx_ref[...] = idx
    slot_ref[...] = jnp.broadcast_to(order_buf[...], (SUB, LANES))
    for copy in copies[1:]:
        copy.wait()
    planes = project(read(near_buf, 2), [read(near_buf, m) for m in range(2)], idx, tables)
    write(od_ref, (), sum(planes, []))
    for copy in late:
        copy.wait()


def signs_of(parity):
    first = jnp.where(parity == 1, time_step, -time_step).astype(jnp.float32)
    return first, np.float32(-time_step), np.float32(-time_step)


def project_even(idx_ref, raw_ref, ev_ref, te_ref, to_ref):
    idx = idx_ref[...]
    signs = signs_of(lax.axis_index("elem") % 2)
    planes = project(read(raw_ref, 2), [read(raw_ref, m) for m in range(2)], idx, third_tables())
    turned = [[gather_lanes(v, idx) * signs[r % 3] for v in read(raw_ref, 3 + r)] for r in range(6)]
    write(ev_ref, (), sum(planes, []))
    write(te_ref, (), sum(turned[:3], []))
    write(to_ref, (), sum(turned[3:], []))


def prepare(idx_ref, scal_ref, mass_ref, tr_ref,
            gi_ref, q_ref, ri_ref, rt_ref, ti_ref, st_ref):
    parity = lax.axis_index("elem") % 2
    idx = idx_ref[...]
    tables = third_tables()
    signs = signs_of(parity)

    def load(i):
        src = source_plane(parity, i)
        planes = [read(scal_ref, m, src) for m in range(2)] + [read(mass_ref, src)]
        return planes + [read(tr_ref, r, src) for r in range(3)]

    faces = [read(tr_ref, 0, source_plane(parity, face * ORDER)) for face in range(2)]
    ahead = load(1)
    for face in range(2):
        first = [gather_lanes(v, idx) * signs[0] for v in faces[face]]
        write(st_ref, (face,), plane_sum(first, tables, ROWS))
    sums = [[None, None], [None, None]]
    for i in range(6):
        raw = [[gather_lanes(v, idx) for v in plane] for plane in ahead]
        weight = raw[2]
        first = plane_sum([v * signs[0] for v in raw[3]], tables)
        inverse = [1.0 / v for v in plane_sum(weight, tables)]
        rest = [[v * signs[r] for v in raw[3 + r]] for r in (1, 2)]
        planes = []
        for m in range(2):
            plane = plane_sum([raw[m][j] * weight[j] for j in range(8)], tables)
            planes.append([plane[j] * inverse[j] for j in range(8)])
        if i < 5:
            ahead = load(i + 2)
        for r in range(2):
            write(ti_ref, (i, r), rest[r])
        write(ri_ref, (i,), inverse)
        write(rt_ref, (i,), [first[j] * inverse[j] for j in range(8)])
        for m in range(2):
            write(gi_ref, (m, i), planes[m])
            for face in range(2):
                terms = [v * np.float32(DM[face * ORDER, i + 1]) for v in planes[m][:ROWS]]
                old = sums[face][m]
                sums[face][m] = [x + y for x, y in zip(old, terms)] if old else terms
    for face in range(2):
        for m in range(2):
            write(q_ref, (face, m), sums[face][m])


def rotations():
    k = lax.broadcasted_iota(jnp.int32, (SUB, LANES), 0)
    out = []
    for r in range(8):
        value = jnp.full((SUB, LANES), np.float32(DM[7, (7 - r) % 8]))
        for row in range(7):
            value = jnp.where(k == row, np.float32(DM[row, (row - r) % 8]), value)
        out.append(value)
    return out


def in_plane(plane, second_t, third_t, rot):
    second = along_second(plane)
    return [second_t[j] * second[j] + third_t[j] * along_third(plane[j], rot) for j in range(8)]


def inner_open(gi_ref, ri_ref, rt_ref, ti_ref, rot, wp_ref):
    tables = third_tables()
    for m in range(2):
        for j in range(8):
            rows = [gi_ref[m, a, j] for a in range(6)]
            even = [rows[a] + rows[5 - a] for a in range(3)]
            odd = [rows[a] - rows[5 - a] for a in range(3)]
            for i in range(3):
                e = combine([(DM[i + 1, a + 1] + DM[i + 1, 6 - a]) / 2 for a in range(3)], even)
                o = combine([(DM[i + 1, a + 1] - DM[i + 1, 6 - a]) / 2 for a in range(3)], odd)
                wp_ref[m, i, j] = (o + e) * rt_ref[i, j]
                wp_ref[m, 5 - i, j] = (o - e) * rt_ref[5 - i, j]
    for i in range(6):
        for m in range(2):
            plane = in_plane(read(gi_ref, m, i), read(ti_ref, i, 0), read(ti_ref, i, 1), rot)
            plane = plane_sum(plane, tables)
            write(wp_ref, (m, i), [wp_ref[m, i, j] + ri_ref[i, j] * plane[j] for j in range(8)])


def inner_close(p0_ref, p7_ref, wp_ref, rt_ref, scale, put, q_ref=None):
    for m in range(2):
        p0, p7 = full(read(p0_ref, m, rows=ROWS)), full(read(p7_ref, m, rows=ROWS))
        sums = [[], []]
        for i in range(6):
            near, far = np.float32(scale * DM[i + 1, 0]), np.float32(scale * DM[i + 1, ORDER])
            kept = put(m, i, [
                wp_ref[m, i, j] * np.float32(scale) + rt_ref[i, j] * (p0[j] * near + p7[j] * far)
                for j in range(8)
            ])
            for face in range(2):
                terms = [v * np.float32(DM[face * ORDER, i + 1]) for v in kept[:ROWS]]
                sums[face] = [x + y for x, y in zip(sums[face], terms)] if i else terms
        if q_ref is not None:
            for face in range(2):
                write(q_ref, (face, m), sums[face])


def own_terms(p_ref, a_ref, rf_ref, face, rot, tables, e_ref):
    second_t, third_t = read(a_ref, 0), read(a_ref, 1)
    for m in range(2):
        p = full(read(p_ref, m, rows=ROWS))
        plane = plane_sum(in_plane(p, second_t, third_t, rot), tables, ROWS)
        write(e_ref, (m,), [
            rf_ref[j] * (plane[j] + a_ref[2, j] * (p[j] * np.float32(DM[face * ORDER, face * ORDER])))
            for j in range(ROWS)
        ])


def both_sides(own_ref, got_ref, passed_ref, tables, a_ref):
    total = [
        [own_ref[8 * r + j] + (got_ref[8 * r + j] + passed_ref[8 * r + j]) for j in range(8)]
        for r in range(3)
    ]
    write(a_ref, (0,), total[1])
    write(a_ref, (1,), total[2])
    write(a_ref, (2,), plane_sum(total[0], tables, ROWS))


def make_field_face(face):
    far = np.float32(DM[ORDER - face * ORDER, face * ORDER])

    def field_face(own_ref, got_ref, q_ref, st_ref, p_ref, rf_ref, send_ref):
        inverse = [1.0 / (own_ref[14 + j] + got_ref[14 + j]) for j in range(ROWS)]
        p = [
            [(own_ref[ROWS * m + j] + got_ref[ROWS * m + j]) * inverse[j] for j in range(ROWS)]
            for m in range(2)
        ]
        sent = [
            [st_ref[1 - face, j] * (q_ref[1 - face, m, j] + p[m][j] * far) for j in range(ROWS)]
            for m in range(2)
        ]
        write(send_ref, (), sent[0] + sent[1])
        for m in range(2):
            write(p_ref, (m,), p[m])
        write(rf_ref, (), inverse)

    return field_face


def make_stage_face(face, scale, total, raw):
    far = np.float32(DM[ORDER - face * ORDER, face * ORDER])
    scale = np.float32(scale)

    def stage_face(own_ref, got_ref, e_ref, acc_ref, q_ref, rt_ref, rf_ref, p_ref, send_ref):
        p = []
        for m in range(2):
            value = [own_ref[ROWS * m + j] + got_ref[ROWS * m + j] for j in range(ROWS)]
            if raw:
                value = [value[j] * rf_ref[j] for j in range(ROWS)]
            value = [(value[j] + e_ref[m, j]) * scale for j in range(ROWS)]
            if total:
                value = [value[j] + acc_ref[face, m, j] for j in range(ROWS)]
            p.append(value)
        sent = [
            [rt_ref[1 - face, j] * (q_ref[1 - face, m, j] + p[m][j] * far) for j in range(ROWS)]
            for m in range(2)
        ]
        write(send_ref, (), sent[0] + sent[1])
        for m in range(2):
            write(p_ref, (m,), p[m])

    return stage_face


def make_first_inner(scale, opening, start):
    def first_inner(*refs):
        p0_ref, p7_ref, gi_ref, rt_ref, r7_ref = refs[:5]
        tables = third_tables()
        rot = rotations()
        if start:
            own_ref, got_ref, passed_ref, st_ref, r0_ref, ri_ref, ti_ref = refs[5:12]
            gn_ref, an_ref, q_ref, e7_ref, a7_ref, rs_ref, wp_ref = refs[12:]
            inner_open(gi_ref, ri_ref, rt_ref, ti_ref, rot, wp_ref)
            both_sides(own_ref, got_ref, passed_ref, tables, a7_ref)
            write(rs_ref, (0,), [st_ref[0, j] * r0_ref[j] for j in range(ROWS)])
            write(rs_ref, (1,), [st_ref[1, j] * r7_ref[j] for j in range(ROWS)])
        else:
            acci_ref, wp_ref, a7_ref = refs[5:8]
            gn_ref, an_ref, q_ref, e7_ref = refs[8:]
        own_terms(p7_ref, a7_ref, r7_ref, 1, rot, tables, e7_ref)

        def put(m, i, value):
            base = gi_ref if opening else acci_ref
            write(gn_ref, (m, i), value)
            write(an_ref, (m, i), [base[m, i, j] + value[j] for j in range(8)])
            return value

        inner_close(p0_ref, p7_ref, wp_ref, rt_ref, scale, put, q_ref)

    return first_inner


def make_between(start):
    def between(*refs):
        m7_ref, gi_ref, a7_ref, r7_ref, ri_ref, rt_ref, ti_ref, p0_ref, r0_ref = refs[:9]
        rot = rotations()
        tables = third_tables()
        if start:
            own_ref, got_ref, passed_ref, wp_ref, e7_ref, e0_ref, a0_ref = refs[9:]
            both_sides(own_ref, got_ref, passed_ref, tables, a0_ref)
        else:
            a0_ref, wp_ref, e7_ref, e0_ref = refs[9:]
        own_terms(p0_ref, a0_ref, r0_ref, 0, rot, tables, e0_ref)
        own_terms(m7_ref, a7_ref, r7_ref, 1, rot, tables, e7_ref)
        inner_open(gi_ref, ri_ref, rt_ref, ti_ref, rot, wp_ref)

    return between


def face_totals(now, before, accf_ref, afn_ref, opening):
    for face in range(2):
        for m in range(2):
            for j in range(ROWS):
                value = now[face][m, j] + before[face][m, j]
                afn_ref[face, m, j] = value if opening else value + accf_ref[face, m, j]


def make_second_inner(scale, opening, closing):
    def second_inner(m0_ref, m7_ref, p0_ref, p7_ref, accf_ref, acci_ref, wp_ref, ri_ref, rt_ref,
                     ti_ref, a0_ref, r0_ref, gn_ref, q_ref, an_ref, afn_ref, wn_ref, e0_ref):
        rot = rotations()

        def put(m, i, value):
            total = [acci_ref[m, i, j] + value[j] for j in range(8)]
            kept = total if closing else value
            write(gn_ref, (m, i), kept)
            if not closing:
                write(an_ref, (m, i), total)
            return kept

        inner_close(m0_ref, m7_ref, wp_ref, rt_ref, scale, put, q_ref)
        own_terms(m0_ref, a0_ref, r0_ref, 0, rot, third_tables(), e0_ref)
        face_totals((m0_ref, m7_ref), (p0_ref, p7_ref), accf_ref, afn_ref, opening)
        inner_open(gn_ref, ri_ref, rt_ref, ti_ref, rot, wn_ref)

    return second_inner


def make_last_inner(scale):
    def last_inner(slot_ref, m0_ref, m7_ref, p0_ref, p7_ref, accf_ref, acci_ref, wp_ref, rt_ref,
                   a0_ref, r0_ref, out_ref, afn_ref, e0_ref, buf, sems):
        parity = lax.axis_index("elem") % 2
        idx = slot_ref[...]

        def put(m, i, value):
            total = [acci_ref[m, i, j] + value[j] for j in range(8)]
            dst = source_plane(parity, i + 1) - 1
            write(buf, (m, dst), [gather_lanes(v, idx) for v in total])
            return total

        inner_close(m0_ref, m7_ref, wp_ref, rt_ref, scale, put)
        copies = [
            pltpu.make_async_copy(buf.at[m], out_ref.at[m, pl.ds(1, 6)], sems.at[m])
            for m in range(2)
        ]
        for copy in copies:
            copy.start()
        own_terms(m0_ref, a0_ref, r0_ref, 0, rotations(), third_tables(), e0_ref)
        face_totals((m0_ref, m7_ref), (p0_ref, p7_ref), accf_ref, afn_ref, False)
        for copy in copies:
            copy.wait()

    return last_inner


def final_face(face, scale, slot_ref, own_ref, got_ref, e_ref, accf_ref, m):
    idx = slot_ref[...]
    rows = [
        (own_ref[ROWS * m + j] + got_ref[ROWS * m + j] + e_ref[m, j]) * np.float32(scale)
        + accf_ref[face, m, j]
        for j in range(ROWS)
    ]
    return [gather_lanes(v, idx) for v in full(rows)]


def make_finish_near(face, scale):
    def finish_near(slot_ref, own_ref, got_ref, e_ref, accf_ref, face_ref):
        for m in range(2):
            write(face_ref, (m,), final_face(face, scale, slot_ref, own_ref, got_ref, e_ref, accf_ref, m))

    return finish_near


def make_finish_far(face, scale):
    def finish_far(slot_ref, own_ref, got_ref, e_ref, accf_ref, near_ref, part_ref,
                   out_ref, buf, sems):
        dst = source_plane(lax.axis_index("elem") % 2, face * ORDER)
        copies = []
        for m in range(2):
            copies.append(
                pltpu.make_async_copy(near_ref.at[m], out_ref.at[m, ORDER - dst], sems.at[1, m])
            )
            copies[-1].start()
        for m in range(2):
            write(buf, (m,), final_face(face, scale, slot_ref, own_ref, got_ref, e_ref, accf_ref, m))
            copies.append(pltpu.make_async_copy(buf.at[m], out_ref.at[m, dst], sems.at[0, m]))
            copies[-1].start()
        for copy in copies:
            copy.wait()

    return finish_far


VM = pl.BlockSpec(memory_space=pltpu.VMEM)
HB = pl.BlockSpec(memory_space=pltpu.HBM)


def call(kernel, outs, args, name, cost, hbm=(), hbm_out=(), scratch=(), alias={}):
    specs = [HB if n in hbm else VM for n in range(len(args))]
    out_specs = [HB if n in hbm_out else VM for n in range(len(outs))]
    shapes = [jax.ShapeDtypeStruct(s, jnp.int32 if s == (SUB, LANES) else jnp.float32) for s in outs]
    single = len(outs) == 1
    return pl.pallas_call(
        kernel,
        out_shape=shapes[0] if single else shapes,
        in_specs=specs,
        out_specs=out_specs[0] if single else out_specs,
        scratch_shapes=list(scratch),
        input_output_aliases=alias,
        name=name,
        compiler_params=pltpu.CompilerParams(vmem_limit_bytes=8 << 20),
        cost_estimate=pl.CostEstimate(
            flops=cost * 1000000, bytes_accessed=1 << 10, transcendentals=0
        ),
    )(*args)


def per_device(scalars, transport, mass, element_order):
    count = lax.axis_size("elem")
    even_pairs = [(i, i ^ 1) for i in range(count)]
    odd_pairs = [(i, (i + 1) % count if i % 2 else (i - 1) % count) for i in range(count)]
    swap_od = lambda x: lax.ppermute(x, "elem", odd_pairs)
    swap_ev = lambda x: lax.ppermute(x, "elem", even_pairs)
    parts = lax.axis_size("ens")
    second_core = lambda pairs: [
        (e * count + a, e * count + b) for e in range(1, parts, 2) for a, b in pairs
    ]
    hand_over = lambda x: lax.ppermute(x, "ens", [(e, e - 1) for e in range(1, parts, 2)])
    members = scalars.shape[0]
    grid = (EXT, EXT, SUB, LANES)
    scal = scalars.reshape((members,) + grid)
    tr = transport.reshape((3,) + grid)
    mas = mass.reshape(grid)
    tile, part = (EXT, SUB, LANES), (ROWS, SUB, LANES)
    inner, face, faces = (2, 6) + tile, (2,) + part, (2, 2) + part
    sent, geometry = (2 * ROWS, SUB, LANES), (3,) + tile
    f32 = jnp.float32

    stay = lambda x: pltpu.with_memory_space_constraint(x, pltpu.HBM)
    bundle = (24, SUB, LANES)
    od, idx, slots, raw = call(
        project_odd, [(3 * ROWS, SUB, LANES), (SUB, LANES), (SUB, LANES), (9,) + tile],
        (stay(element_order), stay(scal), stay(mas), stay(tr)), "project", 1, hbm=(0, 1, 2, 3),
        scratch=[pltpu.VMEM((1, LANES), jnp.int32), pltpu.VMEM((3,) + tile, f32),
                 pltpu.SemaphoreType.DMA((13,))])
    rod = swap_od(od)
    ev, te, to = call(
        project_even, [(3 * ROWS, SUB, LANES), bundle, bundle], (idx, raw), "project", 1)
    rev = swap_ev(ev)
    got_te = lax.ppermute(te, ("ens", "elem"), second_core(even_pairs))
    got_to = lax.ppermute(to, ("ens", "elem"), second_core(odd_pairs))
    passed_te, passed_to = hand_over(got_te), hand_over(got_to)
    gi, q, ri, rt, ti, st = call(
        prepare, [inner, faces, (6,) + tile, (6,) + tile, (6, 2) + tile, (2,) + part],
        (idx, scal, mas, tr), "prepare", 1)
    p0, r0, cev = call(make_field_face(0), [face, part, sent], (od, rod, q, st), "odd", 3000)
    p7, r7, cod = call(make_field_face(1), [face, part, sent], (ev, rev, q, st), "even", 1)
    acci, accf, wp = gi, q, gi
    pairs = SUBSTEPS * STAGES // 2
    for n in range(pairs):
        s = 2 * n % STAGES + 1
        opening, closing, early = s == 1, s + 1 == STAGES, n == 0
        got_ev, got_od = swap_ev(cev), swap_od(cod)
        extra = (te, got_te, passed_te, st, r0, ri, ti) if early else (acci, wp, a7)
        res = call(
            make_first_inner(1.0 / s, opening, early),
            [inner, inner, faces, face] + ([geometry, (2,) + part] if early else []),
            (p0, p7, gi, rt, r7) + extra, "first", 1000,
            scratch=[pltpu.VMEM(inner, f32)] if early else [])
        gm, acci, q, e7 = res[:4]
        if early:
            a7, rs = res[4:]
        m7, cod2 = call(
            make_stage_face(1, 1.0 / s, False, early), [face, sent],
            (cev, got_ev, e7, accf, q, rs, r7), "ahead", 1)
        got_od2 = swap_od(cod2)
        res = call(
            make_between(early), [inner, face, face] + ([geometry] if early else []),
            (m7, gm, a7, r7, ri, rt, ti, p0, r0)
            + ((to, got_to, passed_to) if early else (a0,)), "between", 2000)
        wp, e7, e0 = res[:3]
        if early:
            a0 = res[3]
        m0, cev2 = call(
            make_stage_face(0, 1.0 / s, False, early), [face, sent],
            (cod, got_od, e0, accf, q, rs, r0), "behind", 1)
        got_ev2 = swap_ev(cev2)
        scale = 1.0 / (s + 1)
        if n < pairs - 1:
            gi, q, acci, accf, wp, e0 = call(
                make_second_inner(scale, opening, closing),
                [inner, faces, inner, faces, inner, face],
                (m0, m7, p0, p7, accf, acci, wp, ri, rt, ti, a0, r0), "second", 3000)
            p0, cev = call(
                make_stage_face(0, scale, closing, False), [face, sent],
                (cod2, got_od2, e0, accf, q, rs, r0), "odd", 3000)
            p7, cod = call(
                make_stage_face(1, scale, closing, False), [face, sent],
                (cev2, got_ev2, e7, accf, q, rs, r7), "even", 1)
        else:
            out, accf, e0 = call(
                make_last_inner(scale), [(members,) + grid, faces, face],
                (slots, m0, m7, p0, p7, accf, acci, wp, rt, a0, r0), "last", 3000,
                hbm_out=(0,), scratch=[pltpu.VMEM(inner, f32), pltpu.SemaphoreType.DMA((2,))])
            near = call(
                make_finish_near(0, scale), [(2,) + tile],
                (slots, cod2, got_od2, e0, accf), "finish", 3000)
            out = call(
                make_finish_far(1, scale), [(members,) + grid],
                (slots, cev2, got_ev2, e7, accf, near, out), "finish", 1,
                hbm=(6,), hbm_out=(0,), alias={6: 0},
                scratch=[pltpu.VMEM((2,) + tile, f32), pltpu.SemaphoreType.DMA((2, 2))])
    return out.reshape(scalars.shape)


def solution(mesh):
    in_specs = (P("ens", None, "elem"), P(None, None, "elem"), P(None, "elem"), P("elem", None))
    out_specs = P("ens", None, "elem")
    return jax.shard_map(
        per_device, mesh=mesh, in_specs=in_specs, out_specs=out_specs, check_vma=False
    )
```

```python
import jax
import jax.numpy as jnp
import numpy as np
from jax import lax
from jax.experimental import pallas as pl
from jax.experimental.pallas import tpu as pltpu
from jax.sharding import PartitionSpec as P

ORDER = 7
EXT = ORDER + 1
SUBSTEPS = 2
STAGES = 4
EY = 8
EZ = 16
LANES = EY * EZ
SUB = 8
ROWS = 7

time_step = 0.015


def legendre_table(points, degree):
    table = np.zeros((points.shape[0], degree + 1))
    table[:, 0] = 1.0
    table[:, 1] = points
    for level in range(2, degree + 1):
        table[:, level] = (
            (2 * level - 1) * points * table[:, level - 1] - (level - 1) * table[:, level - 2]
        ) / level
    return table


def gll_derivative(degree):
    extent = degree + 1
    points = np.cos(np.pi * np.arange(extent) / degree)
    for sweep in range(60):
        table = legendre_table(points, degree)
        points = points - (points * table[:, degree] - table[:, degree - 1]) / (
            extent * table[:, degree]
        )
    points = points[::-1].copy()
    values = legendre_table(points, degree)[:, degree]
    matrix = np.zeros((extent, extent))
    for target in range(extent):
        for source in range(extent):
            if target != source:
                matrix[target, source] = values[target] / (
                    values[source] * (points[target] - points[source])
                )
    matrix[0, 0] = -degree * (degree + 1) / 4.0
    matrix[extent - 1, extent - 1] = degree * (degree + 1) / 4.0
    return matrix


DM = gll_derivative(ORDER)
SUM_PART = [[(DM[j, a] + DM[j, 7 - a]) / 2 for a in range(4)] for j in range(4)]
DIF_PART = [[(DM[j, a] - DM[j, 7 - a]) / 2 for a in range(4)] for j in range(4)]


def combine(coefs, items):
    total = None
    for c, x in zip(coefs, items):
        term = x * np.float32(c)
        total = term if total is None else total + term
    return total


def along_second(plane):
    even = [plane[a] + plane[7 - a] for a in range(4)]
    odd = [plane[a] - plane[7 - a] for a in range(4)]
    out = [None] * 8
    for j in range(4):
        e = combine(SUM_PART[j], even)
        o = combine(DIF_PART[j], odd)
        out[j] = o + e
        out[7 - j] = o - e
    return out


def along_third(x, rot):
    total = x * rot[0]
    for r in range(1, 8):
        total = total + pltpu.roll(x, r, 0) * rot[r]
    return total


def gather_lanes(x, idx):
    return jnp.take_along_axis(x, idx, axis=1, mode="promise_in_bounds")


def third_tables():
    lane = lax.broadcasted_iota(jnp.int32, (SUB, LANES), 1)
    k = lax.broadcasted_iota(jnp.int32, (SUB, LANES), 0)
    z = lane % EZ
    back = jnp.where(z == 0, lane + (EZ - 1), lane - 1)
    ahead = jnp.where(z == EZ - 1, lane - (EZ - 1), lane + 1)
    return jnp.where(k == 0, back, ahead), k == 0, k == ORDER


def plane_sum(plane, tables, rows=EXT):
    idx, first, last = tables
    up = plane[7] + pltpu.roll(plane[0], LANES - EZ, 1)
    plane = [pltpu.roll(up, EZ, 1)] + list(plane[1:7]) + [up]
    out = []
    for v in plane[:rows]:
        x = jnp.where(first, pltpu.roll(v, 1, 0), jnp.where(last, pltpu.roll(v, 7, 0), 0.0))
        out.append(v + gather_lanes(x, idx))
    return out


def full(rows):
    return list(rows) + [pltpu.roll(rows[0], LANES - EZ, 1)]


def write(ref, lead, plane):
    for j, v in enumerate(plane):
        ref[lead + (j,)] = v


def read(ref, *lead, rows=EXT):
    return [ref[lead + (j,)] for j in range(rows)]


def brick_index(order_ref):
    order = jnp.broadcast_to(order_ref[...], (LANES, LANES))
    pos = lax.broadcasted_iota(jnp.int32, (LANES, LANES), 0)
    hot = jnp.where(order == pos, 1.0, 0.0).astype(jnp.bfloat16)
    slot = lax.broadcasted_iota(jnp.int32, (SUB, LANES), 1).astype(jnp.float32).astype(jnp.bfloat16)
    found = lax.dot_general(
        slot, hot, (((1,), (1,)), ((), ())), preferred_element_type=jnp.float32
    )
    return found.astype(jnp.int32)


def source_plane(parity, i):
    return jnp.where(parity == 1, ORDER - i, i)


def source_plane(parity, i):
    return jnp.where(parity == 1, ORDER - i, i)


def project(weight, scal, idx, tables):
    weight = [gather_lanes(v, idx) for v in weight]
    planes = [[gather_lanes(plane[j], idx) * weight[j] for j in range(8)] for plane in scal]
    return [plane_sum(plane, tables, ROWS) for plane in planes + [weight]]


def project_odd(order_ref, scal_ref, mass_ref, tr_ref, od_ref, idx_ref, slot_ref, raw_ref,
                order_buf, near_buf, sems):
    parity = lax.axis_index("elem") % 2
    near, far = source_plane(parity, 0), source_plane(parity, ORDER)
    copies = [pltpu.make_async_copy(order_ref, order_buf, sems.at[0])]
    for r, source in enumerate((scal_ref.at[0, near], scal_ref.at[1, near], mass_ref.at[near])):
        copies.append(pltpu.make_async_copy(source, near_buf.at[r], sems.at[1 + r]))
    sources = [scal_ref.at[0, far], scal_ref.at[1, far], mass_ref.at[far]]
    sources += [tr_ref.at[r, far] for r in range(3)] + [tr_ref.at[r, near] for r in range(3)]
    late = [
        pltpu.make_async_copy(source, raw_ref.at[r], sems.at[4 + r])
        for r, source in enumerate(sources)
    ]
    for copy in copies + late:
        copy.start()
    tables = third_tables()
    copies[0].wait()
    idx = brick_index(order_buf)
    idx_ref[...] = idx
    slot_ref[...] = jnp.broadcast_to(order_buf[...], (SUB, LANES))
    for copy in copies[1:]:
        copy.wait()
    planes = project(read(near_buf, 2), [read(near_buf, m) for m in range(2)], idx, tables)
    write(od_ref, (), sum(planes, []))
    for copy in late:
        copy.wait()


def signs_of(parity):
    first = jnp.where(parity == 1, time_step, -time_step).astype(jnp.float32)
    return first, np.float32(-time_step), np.float32(-time_step)


def project_even(idx_ref, raw_ref, ev_ref, tf_ref):
    idx = idx_ref[...]
    signs = signs_of(lax.axis_index("elem") % 2)
    planes = project(read(raw_ref, 2), [read(raw_ref, m) for m in range(2)], idx, third_tables())
    turned = [[gather_lanes(v, idx) * signs[r % 3] for v in read(raw_ref, 3 + r)] for r in range(6)]
    write(ev_ref, (), sum(planes + turned[:3], []))
    write(tf_ref, (), sum(turned[3:], []))


def prepare(idx_ref, scal_ref, mass_ref, tr_ref,
            gi_ref, q_ref, ri_ref, rt_ref, ti_ref, st_ref):
    parity = lax.axis_index("elem") % 2
    idx = idx_ref[...]
    tables = third_tables()
    signs = signs_of(parity)

    def load(i):
        src = source_plane(parity, i)
        planes = [read(scal_ref, m, src) for m in range(2)] + [read(mass_ref, src)]
        return planes + [read(tr_ref, r, src) for r in range(3)]

    faces = [read(tr_ref, 0, source_plane(parity, face * ORDER)) for face in range(2)]
    ahead = load(1)
    for face in range(2):
        first = [gather_lanes(v, idx) * signs[0] for v in faces[face]]
        write(st_ref, (face,), plane_sum(first, tables, ROWS))
    sums = [[None, None], [None, None]]
    for i in range(6):
        raw = [[gather_lanes(v, idx) for v in plane] for plane in ahead]
        weight = raw[2]
        first = plane_sum([v * signs[0] for v in raw[3]], tables)
        inverse = [1.0 / v for v in plane_sum(weight, tables)]
        rest = [[v * signs[r] for v in raw[3 + r]] for r in (1, 2)]
        planes = []
        for m in range(2):
            plane = plane_sum([raw[m][j] * weight[j] for j in range(8)], tables)
            planes.append([plane[j] * inverse[j] for j in range(8)])
        if i < 5:
            ahead = load(i + 2)
        for r in range(2):
            write(ti_ref, (i, r), rest[r])
        write(ri_ref, (i,), inverse)
        write(rt_ref, (i,), [first[j] * inverse[j] for j in range(8)])
        for m in range(2):
            write(gi_ref, (m, i), planes[m])
            for face in range(2):
                terms = [v * np.float32(DM[face * ORDER, i + 1]) for v in planes[m][:ROWS]]
                old = sums[face][m]
                sums[face][m] = [x + y for x, y in zip(old, terms)] if old else terms
    for face in range(2):
        for m in range(2):
            write(q_ref, (face, m), sums[face][m])


def rotations():
    k = lax.broadcasted_iota(jnp.int32, (SUB, LANES), 0)
    out = []
    for r in range(8):
        value = jnp.full((SUB, LANES), np.float32(DM[7, (7 - r) % 8]))
        for row in range(7):
            value = jnp.where(k == row, np.float32(DM[row, (row - r) % 8]), value)
        out.append(value)
    return out


def in_plane(plane, second_t, third_t, rot):
    second = along_second(plane)
    return [second_t[j] * second[j] + third_t[j] * along_third(plane[j], rot) for j in range(8)]


def inner_open(gi_ref, ri_ref, rt_ref, ti_ref, rot, wp_ref):
    tables = third_tables()
    for m in range(2):
        for j in range(8):
            rows = [gi_ref[m, a, j] for a in range(6)]
            even = [rows[a] + rows[5 - a] for a in range(3)]
            odd = [rows[a] - rows[5 - a] for a in range(3)]
            for i in range(3):
                e = combine([(DM[i + 1, a + 1] + DM[i + 1, 6 - a]) / 2 for a in range(3)], even)
                o = combine([(DM[i + 1, a + 1] - DM[i + 1, 6 - a]) / 2 for a in range(3)], odd)
                wp_ref[m, i, j] = (o + e) * rt_ref[i, j]
                wp_ref[m, 5 - i, j] = (o - e) * rt_ref[5 - i, j]
    for i in range(6):
        for m in range(2):
            plane = in_plane(read(gi_ref, m, i), read(ti_ref, i, 0), read(ti_ref, i, 1), rot)
            plane = plane_sum(plane, tables)
            write(wp_ref, (m, i), [wp_ref[m, i, j] + ri_ref[i, j] * plane[j] for j in range(8)])


def inner_close(p0_ref, p7_ref, wp_ref, rt_ref, scale, put, q_ref=None):
    for m in range(2):
        p0, p7 = full(read(p0_ref, m, rows=ROWS)), full(read(p7_ref, m, rows=ROWS))
        sums = [[], []]
        for i in range(6):
            near, far = np.float32(scale * DM[i + 1, 0]), np.float32(scale * DM[i + 1, ORDER])
            kept = put(m, i, [
                wp_ref[m, i, j] * np.float32(scale) + rt_ref[i, j] * (p0[j] * near + p7[j] * far)
                for j in range(8)
            ])
            for face in range(2):
                terms = [v * np.float32(DM[face * ORDER, i + 1]) for v in kept[:ROWS]]
                sums[face] = [x + y for x, y in zip(sums[face], terms)] if i else terms
        if q_ref is not None:
            for face in range(2):
                write(q_ref, (face, m), sums[face])


def own_terms(p_ref, a_ref, rf_ref, face, rot, tables, e_ref):
    second_t, third_t = read(a_ref, 0), read(a_ref, 1)
    for m in range(2):
        p = full(read(p_ref, m, rows=ROWS))
        plane = plane_sum(in_plane(p, second_t, third_t, rot), tables, ROWS)
        write(e_ref, (m,), [
            rf_ref[j] * (plane[j] + a_ref[2, j] * (p[j] * np.float32(DM[face * ORDER, face * ORDER])))
            for j in range(ROWS)
        ])


def both_sides(own, got, tables, a_ref):
    total = [[own[r][j] + got[r][j] for j in range(8)] for r in range(3)]
    write(a_ref, (0,), total[1])
    write(a_ref, (1,), total[2])
    write(a_ref, (2,), plane_sum(total[0], tables, ROWS))


def transports(ref, start):
    return [[ref[start + 8 * r + j] for j in range(8)] for r in range(3)]


def make_field_face(face):
    far = np.float32(DM[ORDER - face * ORDER, face * ORDER])

    def field_face(own_ref, got_ref, q_ref, st_ref, p_ref, rf_ref, send_ref):
        inverse = [1.0 / (own_ref[14 + j] + got_ref[14 + j]) for j in range(ROWS)]
        p = [
            [(own_ref[ROWS * m + j] + got_ref[ROWS * m + j]) * inverse[j] for j in range(ROWS)]
            for m in range(2)
        ]
        sent = [
            [st_ref[1 - face, j] * (q_ref[1 - face, m, j] + p[m][j] * far) for j in range(ROWS)]
            for m in range(2)
        ]
        write(send_ref, (), sent[0] + sent[1])
        for m in range(2):
            write(p_ref, (m,), p[m])
        write(rf_ref, (), inverse)

    return field_face


def make_stage_face(face, scale, total, raw):
    far = np.float32(DM[ORDER - face * ORDER, face * ORDER])
    scale = np.float32(scale)

    def stage_face(own_ref, got_ref, e_ref, acc_ref, q_ref, rt_ref, rf_ref, p_ref, send_ref):
        p = []
        for m in range(2):
            value = [own_ref[ROWS * m + j] + got_ref[ROWS * m + j] for j in range(ROWS)]
            if raw:
                value = [value[j] * rf_ref[j] for j in range(ROWS)]
            value = [(value[j] + e_ref[m, j]) * scale for j in range(ROWS)]
            if total:
                value = [value[j] + acc_ref[face, m, j] for j in range(ROWS)]
            p.append(value)
        sent = [
            [rt_ref[1 - face, j] * (q_ref[1 - face, m, j] + p[m][j] * far) for j in range(ROWS)]
            for m in range(2)
        ]
        write(send_ref, (), sent[0] + sent[1])
        for m in range(2):
            write(p_ref, (m,), p[m])

    return stage_face


def make_first_inner(scale, opening, start):
    def first_inner(*refs):
        p0_ref, p7_ref, gi_ref, rt_ref, r7_ref = refs[:5]
        tables = third_tables()
        rot = rotations()
        if start:
            ev_ref, rev_ref, st_ref, r0_ref, ri_ref, ti_ref = refs[5:11]
            gn_ref, an_ref, q_ref, e7_ref, a7_ref, rs_ref, wp_ref = refs[11:]
            inner_open(gi_ref, ri_ref, rt_ref, ti_ref, rot, wp_ref)
            both_sides(
                transports(ev_ref, 3 * ROWS), transports(rev_ref, 3 * ROWS), tables, a7_ref)
            write(rs_ref, (0,), [st_ref[0, j] * r0_ref[j] for j in range(ROWS)])
            write(rs_ref, (1,), [st_ref[1, j] * r7_ref[j] for j in range(ROWS)])
        else:
            acci_ref, wp_ref, a7_ref = refs[5:8]
            gn_ref, an_ref, q_ref, e7_ref = refs[8:]
        own_terms(p7_ref, a7_ref, r7_ref, 1, rot, tables, e7_ref)

        def put(m, i, value):
            base = gi_ref if opening else acci_ref
            write(gn_ref, (m, i), value)
            write(an_ref, (m, i), [base[m, i, j] + value[j] for j in range(8)])
            return value

        inner_close(p0_ref, p7_ref, wp_ref, rt_ref, scale, put, q_ref)

    return first_inner


def make_between(start):
    def between(*refs):
        m7_ref, gi_ref, a7_ref, r7_ref, ri_ref, rt_ref, ti_ref, p0_ref, r0_ref = refs[:9]
        rot = rotations()
        tables = third_tables()
        if start:
            tf_ref, rtf_ref, wp_ref, e7_ref, e0_ref, a0_ref = refs[9:]
            both_sides(transports(tf_ref, 0), transports(rtf_ref, 0), tables, a0_ref)
        else:
            a0_ref, wp_ref, e7_ref, e0_ref = refs[9:]
        own_terms(p0_ref, a0_ref, r0_ref, 0, rot, tables, e0_ref)
        own_terms(m7_ref, a7_ref, r7_ref, 1, rot, tables, e7_ref)
        inner_open(gi_ref, ri_ref, rt_ref, ti_ref, rot, wp_ref)

    return between


def face_totals(now, before, accf_ref, afn_ref, opening):
    for face in range(2):
        for m in range(2):
            for j in range(ROWS):
                value = now[face][m, j] + before[face][m, j]
                afn_ref[face, m, j] = value if opening else value + accf_ref[face, m, j]


def make_second_inner(scale, opening, closing):
    def second_inner(m0_ref, m7_ref, p0_ref, p7_ref, accf_ref, acci_ref, wp_ref, ri_ref, rt_ref,
                     ti_ref, a0_ref, r0_ref, gn_ref, q_ref, an_ref, afn_ref, wn_ref, e0_ref):
        rot = rotations()

        def put(m, i, value):
            total = [acci_ref[m, i, j] + value[j] for j in range(8)]
            kept = total if closing else value
            write(gn_ref, (m, i), kept)
            if not closing:
                write(an_ref, (m, i), total)
            return kept

        inner_close(m0_ref, m7_ref, wp_ref, rt_ref, scale, put, q_ref)
        own_terms(m0_ref, a0_ref, r0_ref, 0, rot, third_tables(), e0_ref)
        face_totals((m0_ref, m7_ref), (p0_ref, p7_ref), accf_ref, afn_ref, opening)
        inner_open(gn_ref, ri_ref, rt_ref, ti_ref, rot, wn_ref)

    return second_inner


def make_last_inner(scale):
    def last_inner(slot_ref, m0_ref, m7_ref, p0_ref, p7_ref, accf_ref, acci_ref, wp_ref, rt_ref,
                   a0_ref, r0_ref, out_ref, afn_ref, e0_ref, buf, sems):
        parity = lax.axis_index("elem") % 2
        idx = slot_ref[...]

        def put(m, i, value):
            total = [acci_ref[m, i, j] + value[j] for j in range(8)]
            dst = source_plane(parity, i + 1) - 1
            write(buf, (m, dst), [gather_lanes(v, idx) for v in total])
            return total

        inner_close(m0_ref, m7_ref, wp_ref, rt_ref, scale, put)
        copies = [
            pltpu.make_async_copy(buf.at[m], out_ref.at[m, pl.ds(1, 6)], sems.at[m])
            for m in range(2)
        ]
        for copy in copies:
            copy.start()
        own_terms(m0_ref, a0_ref, r0_ref, 0, rotations(), third_tables(), e0_ref)
        face_totals((m0_ref, m7_ref), (p0_ref, p7_ref), accf_ref, afn_ref, False)
        for copy in copies:
            copy.wait()

    return last_inner


def final_face(face, scale, slot_ref, own_ref, got_ref, e_ref, accf_ref, m):
    idx = slot_ref[...]
    rows = [
        (own_ref[ROWS * m + j] + got_ref[ROWS * m + j] + e_ref[m, j]) * np.float32(scale)
        + accf_ref[face, m, j]
        for j in range(ROWS)
    ]
    return [gather_lanes(v, idx) for v in full(rows)]


def make_finish_near(face, scale):
    def finish_near(slot_ref, own_ref, got_ref, e_ref, accf_ref, face_ref):
        for m in range(2):
            write(face_ref, (m,), final_face(face, scale, slot_ref, own_ref, got_ref, e_ref, accf_ref, m))

    return finish_near


def make_finish_far(face, scale):
    def finish_far(slot_ref, own_ref, got_ref, e_ref, accf_ref, near_ref, part_ref,
                   out_ref, buf, sems):
        dst = source_plane(lax.axis_index("elem") % 2, face * ORDER)
        copies = []
        for m in range(2):
            write(buf, (m,), final_face(face, scale, slot_ref, own_ref, got_ref, e_ref, accf_ref, m))
            copies.append(pltpu.make_async_copy(buf.at[m], out_ref.at[m, dst], sems.at[0, m]))
            copies.append(
                pltpu.make_async_copy(near_ref.at[m], out_ref.at[m, ORDER - dst], sems.at[1, m])
            )
            copies[-2].start()
            copies[-1].start()
        for copy in copies:
            copy.wait()

    return finish_far


VM = pl.BlockSpec(memory_space=pltpu.VMEM)
HB = pl.BlockSpec(memory_space=pltpu.HBM)


def call(kernel, outs, args, name, cost, hbm=(), hbm_out=(), scratch=(), alias={}):
    specs = [HB if n in hbm else VM for n in range(len(args))]
    out_specs = [HB if n in hbm_out else VM for n in range(len(outs))]
    shapes = [jax.ShapeDtypeStruct(s, jnp.int32 if s == (SUB, LANES) else jnp.float32) for s in outs]
    single = len(outs) == 1
    return pl.pallas_call(
        kernel,
        out_shape=shapes[0] if single else shapes,
        in_specs=specs,
        out_specs=out_specs[0] if single else out_specs,
        scratch_shapes=list(scratch),
        input_output_aliases=alias,
        name=name,
        compiler_params=pltpu.CompilerParams(vmem_limit_bytes=8 << 20),
        cost_estimate=pl.CostEstimate(
            flops=cost * 1000000, bytes_accessed=1 << 10, transcendentals=0
        ),
    )(*args)


def per_device(scalars, transport, mass, element_order):
    count = lax.axis_size("elem")
    even_pairs = [(i, i ^ 1) for i in range(count)]
    odd_pairs = [(i, (i + 1) % count if i % 2 else (i - 1) % count) for i in range(count)]
    swap_od = lambda x: lax.ppermute(x, "elem", odd_pairs)
    swap_ev = lambda x: lax.ppermute(x, "elem", even_pairs)
    members = scalars.shape[0]
    grid = (EXT, EXT, SUB, LANES)
    scal = scalars.reshape((members,) + grid)
    tr = transport.reshape((3,) + grid)
    mas = mass.reshape(grid)
    tile, part = (EXT, SUB, LANES), (ROWS, SUB, LANES)
    inner, face, faces = (2, 6) + tile, (2,) + part, (2, 2) + part
    sent, geometry = (2 * ROWS, SUB, LANES), (3,) + tile
    f32 = jnp.float32

    stay = lambda x: pltpu.with_memory_space_constraint(x, pltpu.HBM)
    bundle = (3 * ROWS + 24, SUB, LANES)
    od, idx, slots, raw = call(
        project_odd, [(3 * ROWS, SUB, LANES), (SUB, LANES), (SUB, LANES), (9,) + tile],
        (stay(element_order), stay(scal), stay(mas), stay(tr)), "project", 1, hbm=(0, 1, 2, 3),
        scratch=[pltpu.VMEM((1, LANES), jnp.int32), pltpu.VMEM((3,) + tile, f32),
                 pltpu.SemaphoreType.DMA((13,))])
    rod = swap_od(od)
    ev, tf = call(project_even, [bundle, (24, SUB, LANES)], (idx, raw), "project", 1)
    rev, rtf = swap_ev(ev), swap_od(tf)
    gi, q, ri, rt, ti, st = call(
        prepare, [inner, faces, (6,) + tile, (6,) + tile, (6, 2) + tile, (2,) + part],
        (idx, scal, mas, tr), "prepare", 1)
    p0, r0, cev = call(make_field_face(0), [face, part, sent], (od, rod, q, st), "odd", 3000)
    p7, r7, cod = call(make_field_face(1), [face, part, sent], (ev, rev, q, st), "even", 1)
    acci, accf, wp = gi, q, gi
    pairs = SUBSTEPS * STAGES // 2
    for n in range(pairs):
        s = 2 * n % STAGES + 1
        opening, closing, early = s == 1, s + 1 == STAGES, n == 0
        got_ev, got_od = swap_ev(cev), swap_od(cod)
        extra = (ev, rev, st, r0, ri, ti) if early else (acci, wp, a7)
        res = call(
            make_first_inner(1.0 / s, opening, early),
            [inner, inner, faces, face] + ([geometry, (2,) + part] if early else []),
            (p0, p7, gi, rt, r7) + extra, "first", 1000,
            scratch=[pltpu.VMEM(inner, f32)] if early else [])
        gm, acci, q, e7 = res[:4]
        if early:
            a7, rs = res[4:]
        m7, cod2 = call(
            make_stage_face(1, 1.0 / s, False, early), [face, sent],
            (cev, got_ev, e7, accf, q, rs, r7), "ahead", 1)
        got_od2 = swap_od(cod2)
        res = call(
            make_between(early), [inner, face, face] + ([geometry] if early else []),
            (m7, gm, a7, r7, ri, rt, ti, p0, r0) + ((tf, rtf) if early else (a0,)), "between", 2000)
        wp, e7, e0 = res[:3]
        if early:
            a0 = res[3]
        m0, cev2 = call(
            make_stage_face(0, 1.0 / s, False, early), [face, sent],
            (cod, got_od, e0, accf, q, rs, r0), "behind", 1)
        got_ev2 = swap_ev(cev2)
        scale = 1.0 / (s + 1)
        if n < pairs - 1:
            gi, q, acci, accf, wp, e0 = call(
                make_second_inner(scale, opening, closing),
                [inner, faces, inner, faces, inner, face],
                (m0, m7, p0, p7, accf, acci, wp, ri, rt, ti, a0, r0), "second", 3000)
            p0, cev = call(
                make_stage_face(0, scale, closing, False), [face, sent],
                (cod2, got_od2, e0, accf, q, rs, r0), "odd", 3000)
            p7, cod = call(
                make_stage_face(1, scale, closing, False), [face, sent],
                (cev2, got_ev2, e7, accf, q, rs, r7), "even", 1)
        else:
            out, accf, e0 = call(
                make_last_inner(scale), [(members,) + grid, faces, face],
                (slots, m0, m7, p0, p7, accf, acci, wp, rt, a0, r0), "last", 3000,
                hbm_out=(0,), scratch=[pltpu.VMEM(inner, f32), pltpu.SemaphoreType.DMA((2,))])
            near = call(
                make_finish_near(0, scale), [(2,) + tile],
                (slots, cod2, got_od2, e0, accf), "finish", 3000)
            out = call(
                make_finish_far(1, scale), [(members,) + grid],
                (slots, cev2, got_ev2, e7, accf, near, out), "finish", 1,
                hbm=(6,), hbm_out=(0,), alias={6: 0},
                scratch=[pltpu.VMEM((2,) + tile, f32), pltpu.SemaphoreType.DMA((2, 2))])
    return out.reshape(scalars.shape)


def solution(mesh):
    in_specs = (P("ens", None, "elem"), P(None, None, "elem"), P(None, "elem"), P("elem", None))
    out_specs = P("ens", None, "elem")
    return jax.shard_map(
        per_device, mesh=mesh, in_specs=in_specs, out_specs=out_specs, check_vma=False
    )
```

```python
import jax
import jax.numpy as jnp
import numpy as np
from jax import lax
from jax.experimental import pallas as pl
from jax.experimental.pallas import tpu as pltpu
from jax.sharding import PartitionSpec as P

ORDER = 7
EXT = ORDER + 1
SUBSTEPS = 2
STAGES = 4
EY = 8
EZ = 16
LANES = EY * EZ
SUB = 8
ROWS = 7

time_step = 0.015


def legendre_table(points, degree):
    table = np.zeros((points.shape[0], degree + 1))
    table[:, 0] = 1.0
    table[:, 1] = points
    for level in range(2, degree + 1):
        table[:, level] = (
            (2 * level - 1) * points * table[:, level - 1] - (level - 1) * table[:, level - 2]
        ) / level
    return table


def gll_derivative(degree):
    extent = degree + 1
    points = np.cos(np.pi * np.arange(extent) / degree)
    for sweep in range(60):
        table = legendre_table(points, degree)
        points = points - (points * table[:, degree] - table[:, degree - 1]) / (
            extent * table[:, degree]
        )
    points = points[::-1].copy()
    values = legendre_table(points, degree)[:, degree]
    matrix = np.zeros((extent, extent))
    for target in range(extent):
        for source in range(extent):
            if target != source:
                matrix[target, source] = values[target] / (
                    values[source] * (points[target] - points[source])
                )
    matrix[0, 0] = -degree * (degree + 1) / 4.0
    matrix[extent - 1, extent - 1] = degree * (degree + 1) / 4.0
    return matrix


DM = gll_derivative(ORDER)
SUM_PART = [[(DM[j, a] + DM[j, 7 - a]) / 2 for a in range(4)] for j in range(4)]
DIF_PART = [[(DM[j, a] - DM[j, 7 - a]) / 2 for a in range(4)] for j in range(4)]


def combine(coefs, items):
    total = None
    for c, x in zip(coefs, items):
        term = x * np.float32(c)
        total = term if total is None else total + term
    return total


def along_second(plane):
    even = [plane[a] + plane[7 - a] for a in range(4)]
    odd = [plane[a] - plane[7 - a] for a in range(4)]
    out = [None] * 8
    for j in range(4):
        e = combine(SUM_PART[j], even)
        o = combine(DIF_PART[j], odd)
        out[j] = o + e
        out[7 - j] = o - e
    return out


def along_third(x, rot):
    total = x * rot[0]
    for r in range(1, 8):
        total = total + pltpu.roll(x, r, 0) * rot[r]
    return total


def gather_lanes(x, idx):
    return jnp.take_along_axis(x, idx, axis=1, mode="promise_in_bounds")


def third_tables():
    lane = lax.broadcasted_iota(jnp.int32, (SUB, LANES), 1)
    k = lax.broadcasted_iota(jnp.int32, (SUB, LANES), 0)
    z = lane % EZ
    back = jnp.where(z == 0, lane + (EZ - 1), lane - 1)
    ahead = jnp.where(z == EZ - 1, lane - (EZ - 1), lane + 1)
    return jnp.where(k == 0, back, ahead), k == 0, k == ORDER


def plane_sum(plane, tables, rows=EXT):
    idx, first, last = tables
    up = plane[7] + pltpu.roll(plane[0], LANES - EZ, 1)
    plane = [pltpu.roll(up, EZ, 1)] + list(plane[1:7]) + [up]
    out = []
    for v in plane[:rows]:
        x = jnp.where(first, pltpu.roll(v, 1, 0), jnp.where(last, pltpu.roll(v, 7, 0), 0.0))
        out.append(v + gather_lanes(x, idx))
    return out


def full(rows):
    return list(rows) + [pltpu.roll(rows[0], LANES - EZ, 1)]


def write(ref, lead, plane):
    for j, v in enumerate(plane):
        ref[lead + (j,)] = v


def read(ref, *lead, rows=EXT):
    return [ref[lead + (j,)] for j in range(rows)]


def brick_index(order_ref):
    order = jnp.broadcast_to(order_ref[...], (LANES, LANES))
    pos = lax.broadcasted_iota(jnp.int32, (LANES, LANES), 0)
    hot = jnp.where(order == pos, 1.0, 0.0).astype(jnp.bfloat16)
    slot = lax.broadcasted_iota(jnp.int32, (SUB, LANES), 1).astype(jnp.float32).astype(jnp.bfloat16)
    found = lax.dot_general(
        slot, hot, (((1,), (1,)), ((), ())), preferred_element_type=jnp.float32
    )
    return found.astype(jnp.int32)


def source_plane(parity, i):
    return jnp.where(parity == 1, ORDER - i, i)


def source_plane(parity, i):
    return jnp.where(parity == 1, ORDER - i, i)


def project(weight, scal, idx, tables):
    weight = [gather_lanes(v, idx) for v in weight]
    planes = [[gather_lanes(plane[j], idx) * weight[j] for j in range(8)] for plane in scal]
    return [plane_sum(plane, tables, ROWS) for plane in planes + [weight]]


def project_odd(order_ref, scal_ref, mass_ref, tr_ref, od_ref, idx_ref, slot_ref, raw_ref,
                order_buf, near_buf, sems):
    parity = lax.axis_index("elem") % 2
    near, far = source_plane(parity, 0), source_plane(parity, ORDER)
    copies = [pltpu.make_async_copy(order_ref, order_buf, sems.at[0])]
    for r, source in enumerate((scal_ref.at[0, near], scal_ref.at[1, near], mass_ref.at[near])):
        copies.append(pltpu.make_async_copy(source, near_buf.at[r], sems.at[1 + r]))
    sources = [scal_ref.at[0, far], scal_ref.at[1, far], mass_ref.at[far]]
    sources += [tr_ref.at[r, far] for r in range(3)] + [tr_ref.at[r, near] for r in range(3)]
    late = [
        pltpu.make_async_copy(source, raw_ref.at[r], sems.at[4 + r])
        for r, source in enumerate(sources)
    ]
    for copy in copies + late:
        copy.start()
    tables = third_tables()
    copies[0].wait()
    idx = brick_index(order_buf)
    idx_ref[...] = idx
    slot_ref[...] = jnp.broadcast_to(order_buf[...], (SUB, LANES))
    for copy in copies[1:]:
        copy.wait()
    planes = project(read(near_buf, 2), [read(near_buf, m) for m in range(2)], idx, tables)
    write(od_ref, (), sum(planes, []))
    for copy in late:
        copy.wait()


def signs_of(parity):
    first = jnp.where(parity == 1, time_step, -time_step).astype(jnp.float32)
    return first, np.float32(-time_step), np.float32(-time_step)


def project_even(idx_ref, raw_ref, ev_ref):
    idx = idx_ref[...]
    signs = signs_of(lax.axis_index("elem") % 2)
    planes = project(read(raw_ref, 2), [read(raw_ref, m) for m in range(2)], idx, third_tables())
    turned = [[gather_lanes(v, idx) * signs[r % 3] for v in read(raw_ref, 3 + r)] for r in range(3)]
    write(ev_ref, (), sum(planes + turned, []))


def prepare(idx_ref, scal_ref, mass_ref, tr_ref, raw_ref,
            gi_ref, q_ref, ri_ref, rt_ref, ti_ref, st_ref, tf_ref):
    parity = lax.axis_index("elem") % 2
    idx = idx_ref[...]
    tables = third_tables()
    signs = signs_of(parity)

    def load(i):
        src = source_plane(parity, i)
        planes = [read(scal_ref, m, src) for m in range(2)] + [read(mass_ref, src)]
        return planes + [read(tr_ref, r, src) for r in range(3)]

    for r in range(3):
        turned = [gather_lanes(v, idx) * signs[r] for v in read(raw_ref, 6 + r)]
        for j in range(8):
            tf_ref[8 * r + j] = turned[j]
    faces = [read(tr_ref, 0, source_plane(parity, face * ORDER)) for face in range(2)]
    ahead = load(1)
    for face in range(2):
        first = [gather_lanes(v, idx) * signs[0] for v in faces[face]]
        write(st_ref, (face,), plane_sum(first, tables, ROWS))
    sums = [[None, None], [None, None]]
    for i in range(6):
        raw = [[gather_lanes(v, idx) for v in plane] for plane in ahead]
        weight = raw[2]
        first = plane_sum([v * signs[0] for v in raw[3]], tables)
        inverse = [1.0 / v for v in plane_sum(weight, tables)]
        rest = [[v * signs[r] for v in raw[3 + r]] for r in (1, 2)]
        planes = []
        for m in range(2):
            plane = plane_sum([raw[m][j] * weight[j] for j in range(8)], tables)
            planes.append([plane[j] * inverse[j] for j in range(8)])
        if i < 5:
            ahead = load(i + 2)
        for r in range(2):
            write(ti_ref, (i, r), rest[r])
        write(ri_ref, (i,), inverse)
        write(rt_ref, (i,), [first[j] * inverse[j] for j in range(8)])
        for m in range(2):
            write(gi_ref, (m, i), planes[m])
            for face in range(2):
                terms = [v * np.float32(DM[face * ORDER, i + 1]) for v in planes[m][:ROWS]]
                old = sums[face][m]
                sums[face][m] = [x + y for x, y in zip(old, terms)] if old else terms
    for face in range(2):
        for m in range(2):
            write(q_ref, (face, m), sums[face][m])


def rotations():
    k = lax.broadcasted_iota(jnp.int32, (SUB, LANES), 0)
    out = []
    for r in range(8):
        value = jnp.full((SUB, LANES), np.float32(DM[7, (7 - r) % 8]))
        for row in range(7):
            value = jnp.where(k == row, np.float32(DM[row, (row - r) % 8]), value)
        out.append(value)
    return out


def in_plane(plane, second_t, third_t, rot):
    second = along_second(plane)
    return [second_t[j] * second[j] + third_t[j] * along_third(plane[j], rot) for j in range(8)]


def inner_open(gi_ref, ri_ref, rt_ref, ti_ref, rot, wp_ref):
    tables = third_tables()
    for m in range(2):
        for j in range(8):
            rows = [gi_ref[m, a, j] for a in range(6)]
            even = [rows[a] + rows[5 - a] for a in range(3)]
            odd = [rows[a] - rows[5 - a] for a in range(3)]
            for i in range(3):
                e = combine([(DM[i + 1, a + 1] + DM[i + 1, 6 - a]) / 2 for a in range(3)], even)
                o = combine([(DM[i + 1, a + 1] - DM[i + 1, 6 - a]) / 2 for a in range(3)], odd)
                wp_ref[m, i, j] = (o + e) * rt_ref[i, j]
                wp_ref[m, 5 - i, j] = (o - e) * rt_ref[5 - i, j]
    for i in range(6):
        for m in range(2):
            plane = in_plane(read(gi_ref, m, i), read(ti_ref, i, 0), read(ti_ref, i, 1), rot)
            plane = plane_sum(plane, tables)
            write(wp_ref, (m, i), [wp_ref[m, i, j] + ri_ref[i, j] * plane[j] for j in range(8)])


def inner_close(p0_ref, p7_ref, wp_ref, rt_ref, scale, put, q_ref=None):
    for m in range(2):
        p0, p7 = full(read(p0_ref, m, rows=ROWS)), full(read(p7_ref, m, rows=ROWS))
        sums = [[], []]
        for i in range(6):
            near, far = np.float32(scale * DM[i + 1, 0]), np.float32(scale * DM[i + 1, ORDER])
            kept = put(m, i, [
                wp_ref[m, i, j] * np.float32(scale) + rt_ref[i, j] * (p0[j] * near + p7[j] * far)
                for j in range(8)
            ])
            for face in range(2):
                terms = [v * np.float32(DM[face * ORDER, i + 1]) for v in kept[:ROWS]]
                sums[face] = [x + y for x, y in zip(sums[face], terms)] if i else terms
        if q_ref is not None:
            for face in range(2):
                write(q_ref, (face, m), sums[face])


def own_terms(p_ref, a_ref, rf_ref, face, rot, tables, e_ref):
    second_t, third_t = read(a_ref, 0), read(a_ref, 1)
    for m in range(2):
        p = full(read(p_ref, m, rows=ROWS))
        plane = plane_sum(in_plane(p, second_t, third_t, rot), tables, ROWS)
        write(e_ref, (m,), [
            rf_ref[j] * (plane[j] + a_ref[2, j] * (p[j] * np.float32(DM[face * ORDER, face * ORDER])))
            for j in range(ROWS)
        ])


def both_sides(own, got, tables, a_ref):
    total = [[own[r][j] + got[r][j] for j in range(8)] for r in range(3)]
    write(a_ref, (0,), total[1])
    write(a_ref, (1,), total[2])
    write(a_ref, (2,), plane_sum(total[0], tables, ROWS))


def transports(ref, start):
    return [[ref[start + 8 * r + j] for j in range(8)] for r in range(3)]


def make_field_face(face):
    far = np.float32(DM[ORDER - face * ORDER, face * ORDER])

    def field_face(own_ref, got_ref, q_ref, st_ref, p_ref, rf_ref, send_ref):
        inverse = [1.0 / (own_ref[14 + j] + got_ref[14 + j]) for j in range(ROWS)]
        p = [
            [(own_ref[ROWS * m + j] + got_ref[ROWS * m + j]) * inverse[j] for j in range(ROWS)]
            for m in range(2)
        ]
        sent = [
            [st_ref[1 - face, j] * (q_ref[1 - face, m, j] + p[m][j] * far) for j in range(ROWS)]
            for m in range(2)
        ]
        write(send_ref, (), sent[0] + sent[1])
        for m in range(2):
            write(p_ref, (m,), p[m])
        write(rf_ref, (), inverse)

    return field_face


def make_stage_face(face, scale, total, raw):
    far = np.float32(DM[ORDER - face * ORDER, face * ORDER])
    scale = np.float32(scale)

    def stage_face(own_ref, got_ref, e_ref, acc_ref, q_ref, rt_ref, rf_ref, p_ref, send_ref):
        p = []
        for m in range(2):
            value = [own_ref[ROWS * m + j] + got_ref[ROWS * m + j] for j in range(ROWS)]
            if raw:
                value = [value[j] * rf_ref[j] for j in range(ROWS)]
            value = [(value[j] + e_ref[m, j]) * scale for j in range(ROWS)]
            if total:
                value = [value[j] + acc_ref[face, m, j] for j in range(ROWS)]
            p.append(value)
        sent = [
            [rt_ref[1 - face, j] * (q_ref[1 - face, m, j] + p[m][j] * far) for j in range(ROWS)]
            for m in range(2)
        ]
        write(send_ref, (), sent[0] + sent[1])
        for m in range(2):
            write(p_ref, (m,), p[m])

    return stage_face


def make_first_inner(scale, opening, start):
    def first_inner(*refs):
        p0_ref, p7_ref, gi_ref, rt_ref, r7_ref = refs[:5]
        tables = third_tables()
        rot = rotations()
        if start:
            ev_ref, rev_ref, st_ref, r0_ref, ri_ref, ti_ref = refs[5:11]
            gn_ref, an_ref, q_ref, e7_ref, a7_ref, rs_ref, wp_ref = refs[11:]
            inner_open(gi_ref, ri_ref, rt_ref, ti_ref, rot, wp_ref)
            both_sides(
                transports(ev_ref, 3 * ROWS), transports(rev_ref, 3 * ROWS), tables, a7_ref)
            write(rs_ref, (0,), [st_ref[0, j] * r0_ref[j] for j in range(ROWS)])
            write(rs_ref, (1,), [st_ref[1, j] * r7_ref[j] for j in range(ROWS)])
        else:
            acci_ref, wp_ref, a7_ref = refs[5:8]
            gn_ref, an_ref, q_ref, e7_ref = refs[8:]
        own_terms(p7_ref, a7_ref, r7_ref, 1, rot, tables, e7_ref)

        def put(m, i, value):
            base = gi_ref if opening else acci_ref
            write(gn_ref, (m, i), value)
            write(an_ref, (m, i), [base[m, i, j] + value[j] for j in range(8)])
            return value

        inner_close(p0_ref, p7_ref, wp_ref, rt_ref, scale, put, q_ref)

    return first_inner


def make_between(start):
    def between(*refs):
        m7_ref, gi_ref, a7_ref, r7_ref, ri_ref, rt_ref, ti_ref, p0_ref, r0_ref = refs[:9]
        rot = rotations()
        tables = third_tables()
        if start:
            tf_ref, rtf_ref, wp_ref, e7_ref, e0_ref, a0_ref = refs[9:]
            both_sides(transports(tf_ref, 0), transports(rtf_ref, 0), tables, a0_ref)
        else:
            a0_ref, wp_ref, e7_ref, e0_ref = refs[9:]
        own_terms(p0_ref, a0_ref, r0_ref, 0, rot, tables, e0_ref)
        own_terms(m7_ref, a7_ref, r7_ref, 1, rot, tables, e7_ref)
        inner_open(gi_ref, ri_ref, rt_ref, ti_ref, rot, wp_ref)

    return between


def face_totals(now, before, accf_ref, afn_ref, opening):
    for face in range(2):
        for m in range(2):
            for j in range(ROWS):
                value = now[face][m, j] + before[face][m, j]
                afn_ref[face, m, j] = value if opening else value + accf_ref[face, m, j]


def make_second_inner(scale, opening, closing):
    def second_inner(m0_ref, m7_ref, p0_ref, p7_ref, accf_ref, acci_ref, wp_ref, ri_ref, rt_ref,
                     ti_ref, a0_ref, r0_ref, gn_ref, q_ref, an_ref, afn_ref, wn_ref, e0_ref):
        rot = rotations()

        def put(m, i, value):
            total = [acci_ref[m, i, j] + value[j] for j in range(8)]
            kept = total if closing else value
            write(gn_ref, (m, i), kept)
            if not closing:
                write(an_ref, (m, i), total)
            return kept

        inner_close(m0_ref, m7_ref, wp_ref, rt_ref, scale, put, q_ref)
        own_terms(m0_ref, a0_ref, r0_ref, 0, rot, third_tables(), e0_ref)
        face_totals((m0_ref, m7_ref), (p0_ref, p7_ref), accf_ref, afn_ref, opening)
        inner_open(gn_ref, ri_ref, rt_ref, ti_ref, rot, wn_ref)

    return second_inner


def make_last_inner(scale):
    def last_inner(slot_ref, m0_ref, m7_ref, p0_ref, p7_ref, accf_ref, acci_ref, wp_ref, rt_ref,
                   a0_ref, r0_ref, out_ref, afn_ref, e0_ref, buf, sems):
        parity = lax.axis_index("elem") % 2
        idx = slot_ref[...]

        def put(m, i, value):
            total = [acci_ref[m, i, j] + value[j] for j in range(8)]
            dst = source_plane(parity, i + 1) - 1
            write(buf, (m, dst), [gather_lanes(v, idx) for v in total])
            return total

        inner_close(m0_ref, m7_ref, wp_ref, rt_ref, scale, put)
        copies = [
            pltpu.make_async_copy(buf.at[m], out_ref.at[m, pl.ds(1, 6)], sems.at[m])
            for m in range(2)
        ]
        for copy in copies:
            copy.start()
        own_terms(m0_ref, a0_ref, r0_ref, 0, rotations(), third_tables(), e0_ref)
        face_totals((m0_ref, m7_ref), (p0_ref, p7_ref), accf_ref, afn_ref, False)
        for copy in copies:
            copy.wait()

    return last_inner


def final_face(face, scale, slot_ref, own_ref, got_ref, e_ref, accf_ref, m):
    idx = slot_ref[...]
    rows = [
        (own_ref[ROWS * m + j] + got_ref[ROWS * m + j] + e_ref[m, j]) * np.float32(scale)
        + accf_ref[face, m, j]
        for j in range(ROWS)
    ]
    return [gather_lanes(v, idx) for v in full(rows)]


def make_finish_near(face, scale):
    def finish_near(slot_ref, own_ref, got_ref, e_ref, accf_ref, face_ref):
        for m in range(2):
            write(face_ref, (m,), final_face(face, scale, slot_ref, own_ref, got_ref, e_ref, accf_ref, m))

    return finish_near


def make_finish_far(face, scale):
    def finish_far(slot_ref, own_ref, got_ref, e_ref, accf_ref, near_ref, part_ref,
                   out_ref, buf, sems):
        dst = source_plane(lax.axis_index("elem") % 2, face * ORDER)
        copies = []
        for m in range(2):
            write(buf, (m,), final_face(face, scale, slot_ref, own_ref, got_ref, e_ref, accf_ref, m))
            copies.append(pltpu.make_async_copy(buf.at[m], out_ref.at[m, dst], sems.at[0, m]))
            copies.append(
                pltpu.make_async_copy(near_ref.at[m], out_ref.at[m, ORDER - dst], sems.at[1, m])
            )
            copies[-2].start()
            copies[-1].start()
        for copy in copies:
            copy.wait()

    return finish_far


VM = pl.BlockSpec(memory_space=pltpu.VMEM)
HB = pl.BlockSpec(memory_space=pltpu.HBM)


def call(kernel, outs, args, name, cost, hbm=(), hbm_out=(), scratch=(), alias={}):
    specs = [HB if n in hbm else VM for n in range(len(args))]
    out_specs = [HB if n in hbm_out else VM for n in range(len(outs))]
    shapes = [jax.ShapeDtypeStruct(s, jnp.int32 if s == (SUB, LANES) else jnp.float32) for s in outs]
    single = len(outs) == 1
    return pl.pallas_call(
        kernel,
        out_shape=shapes[0] if single else shapes,
        in_specs=specs,
        out_specs=out_specs[0] if single else out_specs,
        scratch_shapes=list(scratch),
        input_output_aliases=alias,
        name=name,
        compiler_params=pltpu.CompilerParams(vmem_limit_bytes=8 << 20),
        cost_estimate=pl.CostEstimate(
            flops=cost * 1000000, bytes_accessed=1 << 10, transcendentals=0
        ),
    )(*args)


def per_device(scalars, transport, mass, element_order):
    count = lax.axis_size("elem")
    even_pairs = [(i, i ^ 1) for i in range(count)]
    odd_pairs = [(i, (i + 1) % count if i % 2 else (i - 1) % count) for i in range(count)]
    swap_od = lambda x: lax.ppermute(x, "elem", odd_pairs)
    swap_ev = lambda x: lax.ppermute(x, "elem", even_pairs)
    members = scalars.shape[0]
    grid = (EXT, EXT, SUB, LANES)
    scal = scalars.reshape((members,) + grid)
    tr = transport.reshape((3,) + grid)
    mas = mass.reshape(grid)
    tile, part = (EXT, SUB, LANES), (ROWS, SUB, LANES)
    inner, face, faces = (2, 6) + tile, (2,) + part, (2, 2) + part
    sent, geometry = (2 * ROWS, SUB, LANES), (3,) + tile
    f32 = jnp.float32

    stay = lambda x: pltpu.with_memory_space_constraint(x, pltpu.HBM)
    bundle = (3 * ROWS + 24, SUB, LANES)
    od, idx, slots, raw = call(
        project_odd, [(3 * ROWS, SUB, LANES), (SUB, LANES), (SUB, LANES), (9,) + tile],
        (stay(element_order), stay(scal), stay(mas), stay(tr)), "project", 1, hbm=(0, 1, 2, 3),
        scratch=[pltpu.VMEM((1, LANES), jnp.int32), pltpu.VMEM((3,) + tile, f32),
                 pltpu.SemaphoreType.DMA((13,))])
    rod = swap_od(od)
    ev = call(project_even, [bundle], (idx, raw), "project", 1)
    rev = swap_ev(ev)
    gi, q, ri, rt, ti, st, tf = call(
        prepare,
        [inner, faces, (6,) + tile, (6,) + tile, (6, 2) + tile, (2,) + part, (24, SUB, LANES)],
        (idx, scal, mas, tr, raw), "prepare", 1)
    rtf = swap_od(tf)
    p0, r0, cev = call(make_field_face(0), [face, part, sent], (od, rod, q, st), "odd", 3000)
    p7, r7, cod = call(make_field_face(1), [face, part, sent], (ev, rev, q, st), "even", 1)
    acci, accf, wp = gi, q, gi
    pairs = SUBSTEPS * STAGES // 2
    for n in range(pairs):
        s = 2 * n % STAGES + 1
        opening, closing, early = s == 1, s + 1 == STAGES, n == 0
        got_ev, got_od = swap_ev(cev), swap_od(cod)
        extra = (ev, rev, st, r0, ri, ti) if early else (acci, wp, a7)
        res = call(
            make_first_inner(1.0 / s, opening, early),
            [inner, inner, faces, face] + ([geometry, (2,) + part] if early else []),
            (p0, p7, gi, rt, r7) + extra, "first", 1000,
            scratch=[pltpu.VMEM(inner, f32)] if early else [])
        gm, acci, q, e7 = res[:4]
        if early:
            a7, rs = res[4:]
        m7, cod2 = call(
            make_stage_face(1, 1.0 / s, False, early), [face, sent],
            (cev, got_ev, e7, accf, q, rs, r7), "ahead", 1)
        got_od2 = swap_od(cod2)
        res = call(
            make_between(early), [inner, face, face] + ([geometry] if early else []),
            (m7, gm, a7, r7, ri, rt, ti, p0, r0) + ((tf, rtf) if early else (a0,)), "between", 2000)
        wp, e7, e0 = res[:3]
        if early:
            a0 = res[3]
        m0, cev2 = call(
            make_stage_face(0, 1.0 / s, False, early), [face, sent],
            (cod, got_od, e0, accf, q, rs, r0), "behind", 1)
        got_ev2 = swap_ev(cev2)
        scale = 1.0 / (s + 1)
        if n < pairs - 1:
            gi, q, acci, accf, wp, e0 = call(
                make_second_inner(scale, opening, closing),
                [inner, faces, inner, faces, inner, face],
                (m0, m7, p0, p7, accf, acci, wp, ri, rt, ti, a0, r0), "second", 3000)
            p0, cev = call(
                make_stage_face(0, scale, closing, False), [face, sent],
                (cod2, got_od2, e0, accf, q, rs, r0), "odd", 3000)
            p7, cod = call(
                make_stage_face(1, scale, closing, False), [face, sent],
                (cev2, got_ev2, e7, accf, q, rs, r7), "even", 1)
        else:
            out, accf, e0 = call(
                make_last_inner(scale), [(members,) + grid, faces, face],
                (slots, m0, m7, p0, p7, accf, acci, wp, rt, a0, r0), "last", 3000,
                hbm_out=(0,), scratch=[pltpu.VMEM(inner, f32), pltpu.SemaphoreType.DMA((2,))])
            near = call(
                make_finish_near(0, scale), [(2,) + tile],
                (slots, cod2, got_od2, e0, accf), "finish", 3000)
            out = call(
                make_finish_far(1, scale), [(members,) + grid],
                (slots, cev2, got_ev2, e7, accf, near, out), "finish", 1,
                hbm=(6,), hbm_out=(0,), alias={6: 0},
                scratch=[pltpu.VMEM((2,) + tile, f32), pltpu.SemaphoreType.DMA((2, 2))])
    return out.reshape(scalars.shape)


def solution(mesh):
    in_specs = (P("ens", None, "elem"), P(None, None, "elem"), P(None, "elem"), P("elem", None))
    out_specs = P("ens", None, "elem")
    return jax.shard_map(
        per_device, mesh=mesh, in_specs=in_specs, out_specs=out_specs, check_vma=False
    )
```

```python
import jax
import jax.numpy as jnp
import numpy as np
from jax import lax
from jax.experimental import pallas as pl
from jax.experimental.pallas import tpu as pltpu
from jax.sharding import PartitionSpec as P

ORDER = 7
EXT = ORDER + 1
SUBSTEPS = 2
STAGES = 4
EY = 8
EZ = 16
LANES = EY * EZ
SUB = 8
ROWS = 7

time_step = 0.015


def legendre_table(points, degree):
    table = np.zeros((points.shape[0], degree + 1))
    table[:, 0] = 1.0
    table[:, 1] = points
    for level in range(2, degree + 1):
        table[:, level] = (
            (2 * level - 1) * points * table[:, level - 1] - (level - 1) * table[:, level - 2]
        ) / level
    return table


def gll_derivative(degree):
    extent = degree + 1
    points = np.cos(np.pi * np.arange(extent) / degree)
    for sweep in range(60):
        table = legendre_table(points, degree)
        points = points - (points * table[:, degree] - table[:, degree - 1]) / (
            extent * table[:, degree]
        )
    points = points[::-1].copy()
    values = legendre_table(points, degree)[:, degree]
    matrix = np.zeros((extent, extent))
    for target in range(extent):
        for source in range(extent):
            if target != source:
                matrix[target, source] = values[target] / (
                    values[source] * (points[target] - points[source])
                )
    matrix[0, 0] = -degree * (degree + 1) / 4.0
    matrix[extent - 1, extent - 1] = degree * (degree + 1) / 4.0
    return matrix


DM = gll_derivative(ORDER)
SUM_PART = [[(DM[j, a] + DM[j, 7 - a]) / 2 for a in range(4)] for j in range(4)]
DIF_PART = [[(DM[j, a] - DM[j, 7 - a]) / 2 for a in range(4)] for j in range(4)]


def combine(coefs, items):
    total = None
    for c, x in zip(coefs, items):
        term = x * np.float32(c)
        total = term if total is None else total + term
    return total


def along_second(plane):
    even = [plane[a] + plane[7 - a] for a in range(4)]
    odd = [plane[a] - plane[7 - a] for a in range(4)]
    out = [None] * 8
    for j in range(4):
        e = combine(SUM_PART[j], even)
        o = combine(DIF_PART[j], odd)
        out[j] = o + e
        out[7 - j] = o - e
    return out


def along_third(x, rot):
    total = x * rot[0]
    for r in range(1, 8):
        total = total + pltpu.roll(x, r, 0) * rot[r]
    return total


def gather_lanes(x, idx):
    return jnp.take_along_axis(x, idx, axis=1, mode="promise_in_bounds")


def third_tables():
    lane = lax.broadcasted_iota(jnp.int32, (SUB, LANES), 1)
    k = lax.broadcasted_iota(jnp.int32, (SUB, LANES), 0)
    z = lane % EZ
    back = jnp.where(z == 0, lane + (EZ - 1), lane - 1)
    ahead = jnp.where(z == EZ - 1, lane - (EZ - 1), lane + 1)
    return jnp.where(k == 0, back, ahead), k == 0, k == ORDER


def plane_sum(plane, tables, rows=EXT):
    idx, first, last = tables
    up = plane[7] + pltpu.roll(plane[0], LANES - EZ, 1)
    plane = [pltpu.roll(up, EZ, 1)] + list(plane[1:7]) + [up]
    out = []
    for v in plane[:rows]:
        x = jnp.where(first, pltpu.roll(v, 1, 0), jnp.where(last, pltpu.roll(v, 7, 0), 0.0))
        out.append(v + gather_lanes(x, idx))
    return out


def full(rows):
    return list(rows) + [pltpu.roll(rows[0], LANES - EZ, 1)]


def write(ref, lead, plane):
    for j, v in enumerate(plane):
        ref[lead + (j,)] = v


def read(ref, *lead, rows=EXT):
    return [ref[lead + (j,)] for j in range(rows)]


def brick_index(order_ref):
    order = jnp.broadcast_to(order_ref[...], (LANES, LANES))
    pos = lax.broadcasted_iota(jnp.int32, (LANES, LANES), 0)
    hot = jnp.where(order == pos, 1.0, 0.0).astype(jnp.bfloat16)
    slot = lax.broadcasted_iota(jnp.int32, (SUB, LANES), 1).astype(jnp.float32).astype(jnp.bfloat16)
    found = lax.dot_general(
        slot, hot, (((1,), (1,)), ((), ())), preferred_element_type=jnp.float32
    )
    return found.astype(jnp.int32)


def source_plane(parity, i):
    return jnp.where(parity == 1, ORDER - i, i)


def source_plane(parity, i):
    return jnp.where(parity == 1, ORDER - i, i)


def project(weight, scal, idx, tables):
    weight = [gather_lanes(v, idx) for v in weight]
    planes = [[gather_lanes(plane[j], idx) * weight[j] for j in range(8)] for plane in scal]
    return [plane_sum(plane, tables, ROWS) for plane in planes + [weight]]


def project_odd(order_ref, scal_ref, mass_ref, tr_ref, od_ref, idx_ref, slot_ref, raw_ref,
                order_buf, near_buf, sems):
    parity = lax.axis_index("elem") % 2
    near, far = source_plane(parity, 0), source_plane(parity, ORDER)
    copies = [pltpu.make_async_copy(order_ref, order_buf, sems.at[0])]
    for r, source in enumerate((scal_ref.at[0, near], scal_ref.at[1, near], mass_ref.at[near])):
        copies.append(pltpu.make_async_copy(source, near_buf.at[r], sems.at[1 + r]))
    sources = [scal_ref.at[0, far], scal_ref.at[1, far], mass_ref.at[far]]
    sources += [tr_ref.at[r, far] for r in range(3)]
    late = [
        pltpu.make_async_copy(source, raw_ref.at[r], sems.at[4 + r])
        for r, source in enumerate(sources)
    ]
    for copy in copies + late:
        copy.start()
    tables = third_tables()
    copies[0].wait()
    idx = brick_index(order_buf)
    idx_ref[...] = idx
    slot_ref[...] = jnp.broadcast_to(order_buf[...], (SUB, LANES))
    for copy in copies[1:]:
        copy.wait()
    planes = project(read(near_buf, 2), [read(near_buf, m) for m in range(2)], idx, tables)
    write(od_ref, (), sum(planes, []))
    for copy in late:
        copy.wait()


def signs_of(parity):
    first = jnp.where(parity == 1, time_step, -time_step).astype(jnp.float32)
    return first, np.float32(-time_step), np.float32(-time_step)


def project_even(idx_ref, raw_ref, ev_ref):
    idx = idx_ref[...]
    signs = signs_of(lax.axis_index("elem") % 2)
    planes = project(read(raw_ref, 2), [read(raw_ref, m) for m in range(2)], idx, third_tables())
    turned = [[gather_lanes(v, idx) * signs[r % 3] for v in read(raw_ref, 3 + r)] for r in range(3)]
    write(ev_ref, (), sum(planes + turned, []))


def prepare(idx_ref, scal_ref, mass_ref, tr_ref,
            gi_ref, q_ref, ri_ref, rt_ref, ti_ref, st_ref, tf_ref):
    parity = lax.axis_index("elem") % 2
    idx = idx_ref[...]
    tables = third_tables()
    signs = signs_of(parity)

    def load(i):
        src = source_plane(parity, i)
        planes = [read(scal_ref, m, src) for m in range(2)] + [read(mass_ref, src)]
        return planes + [read(tr_ref, r, src) for r in range(3)]

    for r in range(3):
        turned = [gather_lanes(v, idx) * signs[r] for v in read(tr_ref, r, source_plane(parity, 0))]
        for j in range(8):
            tf_ref[8 * r + j] = turned[j]
    faces = [read(tr_ref, 0, source_plane(parity, face * ORDER)) for face in range(2)]
    ahead = load(1)
    for face in range(2):
        first = [gather_lanes(v, idx) * signs[0] for v in faces[face]]
        write(st_ref, (face,), plane_sum(first, tables, ROWS))
    sums = [[None, None], [None, None]]
    for i in range(6):
        raw = [[gather_lanes(v, idx) for v in plane] for plane in ahead]
        weight = raw[2]
        first = plane_sum([v * signs[0] for v in raw[3]], tables)
        inverse = [1.0 / v for v in plane_sum(weight, tables)]
        rest = [[v * signs[r] for v in raw[3 + r]] for r in (1, 2)]
        planes = []
        for m in range(2):
            plane = plane_sum([raw[m][j] * weight[j] for j in range(8)], tables)
            planes.append([plane[j] * inverse[j] for j in range(8)])
        if i < 5:
            ahead = load(i + 2)
        for r in range(2):
            write(ti_ref, (i, r), rest[r])
        write(ri_ref, (i,), inverse)
        write(rt_ref, (i,), [first[j] * inverse[j] for j in range(8)])
        for m in range(2):
            write(gi_ref, (m, i), planes[m])
            for face in range(2):
                terms = [v * np.float32(DM[face * ORDER, i + 1]) for v in planes[m][:ROWS]]
                old = sums[face][m]
                sums[face][m] = [x + y for x, y in zip(old, terms)] if old else terms
    for face in range(2):
        for m in range(2):
            write(q_ref, (face, m), sums[face][m])


def rotations():
    k = lax.broadcasted_iota(jnp.int32, (SUB, LANES), 0)
    out = []
    for r in range(8):
        value = jnp.full((SUB, LANES), np.float32(DM[7, (7 - r) % 8]))
        for row in range(7):
            value = jnp.where(k == row, np.float32(DM[row, (row - r) % 8]), value)
        out.append(value)
    return out


def in_plane(plane, second_t, third_t, rot):
    second = along_second(plane)
    return [second_t[j] * second[j] + third_t[j] * along_third(plane[j], rot) for j in range(8)]


def inner_open(gi_ref, ri_ref, rt_ref, ti_ref, rot, wp_ref):
    tables = third_tables()
    for m in range(2):
        for j in range(8):
            rows = [gi_ref[m, a, j] for a in range(6)]
            even = [rows[a] + rows[5 - a] for a in range(3)]
            odd = [rows[a] - rows[5 - a] for a in range(3)]
            for i in range(3):
                e = combine([(DM[i + 1, a + 1] + DM[i + 1, 6 - a]) / 2 for a in range(3)], even)
                o = combine([(DM[i + 1, a + 1] - DM[i + 1, 6 - a]) / 2 for a in range(3)], odd)
                wp_ref[m, i, j] = (o + e) * rt_ref[i, j]
                wp_ref[m, 5 - i, j] = (o - e) * rt_ref[5 - i, j]
    for i in range(6):
        for m in range(2):
            plane = in_plane(read(gi_ref, m, i), read(ti_ref, i, 0), read(ti_ref, i, 1), rot)
            plane = plane_sum(plane, tables)
            write(wp_ref, (m, i), [wp_ref[m, i, j] + ri_ref[i, j] * plane[j] for j in range(8)])


def inner_close(p0_ref, p7_ref, wp_ref, rt_ref, scale, put, q_ref=None):
    for m in range(2):
        p0, p7 = full(read(p0_ref, m, rows=ROWS)), full(read(p7_ref, m, rows=ROWS))
        sums = [[], []]
        for i in range(6):
            near, far = np.float32(scale * DM[i + 1, 0]), np.float32(scale * DM[i + 1, ORDER])
            kept = put(m, i, [
                wp_ref[m, i, j] * np.float32(scale) + rt_ref[i, j] * (p0[j] * near + p7[j] * far)
                for j in range(8)
            ])
            for face in range(2):
                terms = [v * np.float32(DM[face * ORDER, i + 1]) for v in kept[:ROWS]]
                sums[face] = [x + y for x, y in zip(sums[face], terms)] if i else terms
        if q_ref is not None:
            for face in range(2):
                write(q_ref, (face, m), sums[face])


def own_terms(p_ref, a_ref, rf_ref, face, rot, tables, e_ref):
    second_t, third_t = read(a_ref, 0), read(a_ref, 1)
    for m in range(2):
        p = full(read(p_ref, m, rows=ROWS))
        plane = plane_sum(in_plane(p, second_t, third_t, rot), tables, ROWS)
        write(e_ref, (m,), [
            rf_ref[j] * (plane[j] + a_ref[2, j] * (p[j] * np.float32(DM[face * ORDER, face * ORDER])))
            for j in range(ROWS)
        ])


def both_sides(own, got, tables, a_ref):
    total = [[own[r][j] + got[r][j] for j in range(8)] for r in range(3)]
    write(a_ref, (0,), total[1])
    write(a_ref, (1,), total[2])
    write(a_ref, (2,), plane_sum(total[0], tables, ROWS))


def transports(ref, start):
    return [[ref[start + 8 * r + j] for j in range(8)] for r in range(3)]


def make_field_face(face):
    far = np.float32(DM[ORDER - face * ORDER, face * ORDER])

    def field_face(own_ref, got_ref, q_ref, st_ref, p_ref, rf_ref, send_ref):
        inverse = [1.0 / (own_ref[14 + j] + got_ref[14 + j]) for j in range(ROWS)]
        p = [
            [(own_ref[ROWS * m + j] + got_ref[ROWS * m + j]) * inverse[j] for j in range(ROWS)]
            for m in range(2)
        ]
        sent = [
            [st_ref[1 - face, j] * (q_ref[1 - face, m, j] + p[m][j] * far) for j in range(ROWS)]
            for m in range(2)
        ]
        write(send_ref, (), sent[0] + sent[1])
        for m in range(2):
            write(p_ref, (m,), p[m])
        write(rf_ref, (), inverse)

    return field_face


def make_stage_face(face, scale, total, raw):
    far = np.float32(DM[ORDER - face * ORDER, face * ORDER])
    scale = np.float32(scale)

    def stage_face(own_ref, got_ref, e_ref, acc_ref, q_ref, rt_ref, rf_ref, p_ref, send_ref):
        p = []
        for m in range(2):
            value = [own_ref[ROWS * m + j] + got_ref[ROWS * m + j] for j in range(ROWS)]
            if raw:
                value = [value[j] * rf_ref[j] for j in range(ROWS)]
            value = [(value[j] + e_ref[m, j]) * scale for j in range(ROWS)]
            if total:
                value = [value[j] + acc_ref[face, m, j] for j in range(ROWS)]
            p.append(value)
        sent = [
            [rt_ref[1 - face, j] * (q_ref[1 - face, m, j] + p[m][j] * far) for j in range(ROWS)]
            for m in range(2)
        ]
        write(send_ref, (), sent[0] + sent[1])
        for m in range(2):
            write(p_ref, (m,), p[m])

    return stage_face


def make_first_inner(scale, opening, start):
    def first_inner(*refs):
        p0_ref, p7_ref, gi_ref, rt_ref, r7_ref = refs[:5]
        tables = third_tables()
        rot = rotations()
        if start:
            ev_ref, rev_ref, st_ref, r0_ref, ri_ref, ti_ref = refs[5:11]
            gn_ref, an_ref, q_ref, e7_ref, a7_ref, rs_ref, wp_ref = refs[11:]
            inner_open(gi_ref, ri_ref, rt_ref, ti_ref, rot, wp_ref)
            both_sides(
                transports(ev_ref, 3 * ROWS), transports(rev_ref, 3 * ROWS), tables, a7_ref)
            write(rs_ref, (0,), [st_ref[0, j] * r0_ref[j] for j in range(ROWS)])
            write(rs_ref, (1,), [st_ref[1, j] * r7_ref[j] for j in range(ROWS)])
        else:
            acci_ref, wp_ref, a7_ref = refs[5:8]
            gn_ref, an_ref, q_ref, e7_ref = refs[8:]
        own_terms(p7_ref, a7_ref, r7_ref, 1, rot, tables, e7_ref)

        def put(m, i, value):
            base = gi_ref if opening else acci_ref
            write(gn_ref, (m, i), value)
            write(an_ref, (m, i), [base[m, i, j] + value[j] for j in range(8)])
            return value

        inner_close(p0_ref, p7_ref, wp_ref, rt_ref, scale, put, q_ref)

    return first_inner


def make_between(start):
    def between(*refs):
        m7_ref, gi_ref, a7_ref, r7_ref, ri_ref, rt_ref, ti_ref, p0_ref, r0_ref = refs[:9]
        rot = rotations()
        tables = third_tables()
        if start:
            tf_ref, rtf_ref, wp_ref, e7_ref, e0_ref, a0_ref = refs[9:]
            both_sides(transports(tf_ref, 0), transports(rtf_ref, 0), tables, a0_ref)
        else:
            a0_ref, wp_ref, e7_ref, e0_ref = refs[9:]
        own_terms(p0_ref, a0_ref, r0_ref, 0, rot, tables, e0_ref)
        own_terms(m7_ref, a7_ref, r7_ref, 1, rot, tables, e7_ref)
        inner_open(gi_ref, ri_ref, rt_ref, ti_ref, rot, wp_ref)

    return between


def face_totals(now, before, accf_ref, afn_ref, opening):
    for face in range(2):
        for m in range(2):
            for j in range(ROWS):
                value = now[face][m, j] + before[face][m, j]
                afn_ref[face, m, j] = value if opening else value + accf_ref[face, m, j]


def make_second_inner(scale, opening, closing):
    def second_inner(m0_ref, m7_ref, p0_ref, p7_ref, accf_ref, acci_ref, wp_ref, ri_ref, rt_ref,
                     ti_ref, a0_ref, r0_ref, gn_ref, q_ref, an_ref, afn_ref, wn_ref, e0_ref):
        rot = rotations()

        def put(m, i, value):
            total = [acci_ref[m, i, j] + value[j] for j in range(8)]
            kept = total if closing else value
            write(gn_ref, (m, i), kept)
            if not closing:
                write(an_ref, (m, i), total)
            return kept

        inner_close(m0_ref, m7_ref, wp_ref, rt_ref, scale, put, q_ref)
        own_terms(m0_ref, a0_ref, r0_ref, 0, rot, third_tables(), e0_ref)
        face_totals((m0_ref, m7_ref), (p0_ref, p7_ref), accf_ref, afn_ref, opening)
        inner_open(gn_ref, ri_ref, rt_ref, ti_ref, rot, wn_ref)

    return second_inner


def make_last_inner(scale):
    def last_inner(slot_ref, m0_ref, m7_ref, p0_ref, p7_ref, accf_ref, acci_ref, wp_ref, rt_ref,
                   a0_ref, r0_ref, out_ref, afn_ref, e0_ref, buf, sems):
        parity = lax.axis_index("elem") % 2
        idx = slot_ref[...]

        def put(m, i, value):
            total = [acci_ref[m, i, j] + value[j] for j in range(8)]
            dst = source_plane(parity, i + 1) - 1
            write(buf, (m, dst), [gather_lanes(v, idx) for v in total])
            return total

        inner_close(m0_ref, m7_ref, wp_ref, rt_ref, scale, put)
        copies = [
            pltpu.make_async_copy(buf.at[m], out_ref.at[m, pl.ds(1, 6)], sems.at[m])
            for m in range(2)
        ]
        for copy in copies:
            copy.start()
        own_terms(m0_ref, a0_ref, r0_ref, 0, rotations(), third_tables(), e0_ref)
        face_totals((m0_ref, m7_ref), (p0_ref, p7_ref), accf_ref, afn_ref, False)
        for copy in copies:
            copy.wait()

    return last_inner


def final_face(face, scale, slot_ref, own_ref, got_ref, e_ref, accf_ref, m):
    idx = slot_ref[...]
    rows = [
        (own_ref[ROWS * m + j] + got_ref[ROWS * m + j] + e_ref[m, j]) * np.float32(scale)
        + accf_ref[face, m, j]
        for j in range(ROWS)
    ]
    return [gather_lanes(v, idx) for v in full(rows)]


def make_finish_near(face, scale):
    def finish_near(slot_ref, own_ref, got_ref, e_ref, accf_ref, face_ref):
        for m in range(2):
            write(face_ref, (m,), final_face(face, scale, slot_ref, own_ref, got_ref, e_ref, accf_ref, m))

    return finish_near


def make_finish_far(face, scale):
    def finish_far(slot_ref, own_ref, got_ref, e_ref, accf_ref, near_ref, part_ref,
                   out_ref, buf, sems):
        dst = source_plane(lax.axis_index("elem") % 2, face * ORDER)
        copies = []
        for m in range(2):
            write(buf, (m,), final_face(face, scale, slot_ref, own_ref, got_ref, e_ref, accf_ref, m))
            copies.append(pltpu.make_async_copy(buf.at[m], out_ref.at[m, dst], sems.at[0, m]))
            copies.append(
                pltpu.make_async_copy(near_ref.at[m], out_ref.at[m, ORDER - dst], sems.at[1, m])
            )
            copies[-2].start()
            copies[-1].start()
        for copy in copies:
            copy.wait()

    return finish_far


VM = pl.BlockSpec(memory_space=pltpu.VMEM)
HB = pl.BlockSpec(memory_space=pltpu.HBM)


def call(kernel, outs, args, name, cost, hbm=(), hbm_out=(), scratch=(), alias={}):
    specs = [HB if n in hbm else VM for n in range(len(args))]
    out_specs = [HB if n in hbm_out else VM for n in range(len(outs))]
    shapes = [jax.ShapeDtypeStruct(s, jnp.int32 if s == (SUB, LANES) else jnp.float32) for s in outs]
    single = len(outs) == 1
    return pl.pallas_call(
        kernel,
        out_shape=shapes[0] if single else shapes,
        in_specs=specs,
        out_specs=out_specs[0] if single else out_specs,
        scratch_shapes=list(scratch),
        input_output_aliases=alias,
        name=name,
        compiler_params=pltpu.CompilerParams(vmem_limit_bytes=8 << 20),
        cost_estimate=pl.CostEstimate(
            flops=cost * 1000000, bytes_accessed=1 << 10, transcendentals=0
        ),
    )(*args)


def per_device(scalars, transport, mass, element_order):
    count = lax.axis_size("elem")
    even_pairs = [(i, i ^ 1) for i in range(count)]
    odd_pairs = [(i, (i + 1) % count if i % 2 else (i - 1) % count) for i in range(count)]
    swap_od = lambda x: lax.ppermute(x, "elem", odd_pairs)
    swap_ev = lambda x: lax.ppermute(x, "elem", even_pairs)
    members = scalars.shape[0]
    grid = (EXT, EXT, SUB, LANES)
    scal = scalars.reshape((members,) + grid)
    tr = transport.reshape((3,) + grid)
    mas = mass.reshape(grid)
    tile, part = (EXT, SUB, LANES), (ROWS, SUB, LANES)
    inner, face, faces = (2, 6) + tile, (2,) + part, (2, 2) + part
    sent, geometry = (2 * ROWS, SUB, LANES), (3,) + tile
    f32 = jnp.float32

    stay = lambda x: pltpu.with_memory_space_constraint(x, pltpu.HBM)
    bundle = (3 * ROWS + 24, SUB, LANES)
    od, idx, slots, raw = call(
        project_odd, [(3 * ROWS, SUB, LANES), (SUB, LANES), (SUB, LANES), (6,) + tile],
        (stay(element_order), stay(scal), stay(mas), stay(tr)), "project", 1, hbm=(0, 1, 2, 3),
        scratch=[pltpu.VMEM((1, LANES), jnp.int32), pltpu.VMEM((3,) + tile, f32),
                 pltpu.SemaphoreType.DMA((10,))])
    rod = swap_od(od)
    ev = call(project_even, [bundle], (idx, raw), "project", 1)
    rev = swap_ev(ev)
    gi, q, ri, rt, ti, st, tf = call(
        prepare,
        [inner, faces, (6,) + tile, (6,) + tile, (6, 2) + tile, (2,) + part, (24, SUB, LANES)],
        (idx, scal, mas, tr), "prepare", 1)
    rtf = swap_od(tf)
    p0, r0, cev = call(make_field_face(0), [face, part, sent], (od, rod, q, st), "odd", 3000)
    p7, r7, cod = call(make_field_face(1), [face, part, sent], (ev, rev, q, st), "even", 1)
    acci, accf, wp = gi, q, gi
    pairs = SUBSTEPS * STAGES // 2
    for n in range(pairs):
        s = 2 * n % STAGES + 1
        opening, closing, early = s == 1, s + 1 == STAGES, n == 0
        got_ev, got_od = swap_ev(cev), swap_od(cod)
        extra = (ev, rev, st, r0, ri, ti) if early else (acci, wp, a7)
        res = call(
            make_first_inner(1.0 / s, opening, early),
            [inner, inner, faces, face] + ([geometry, (2,) + part] if early else []),
            (p0, p7, gi, rt, r7) + extra, "first", 1000,
            scratch=[pltpu.VMEM(inner, f32)] if early else [])
        gm, acci, q, e7 = res[:4]
        if early:
            a7, rs = res[4:]
        m7, cod2 = call(
            make_stage_face(1, 1.0 / s, False, early), [face, sent],
            (cev, got_ev, e7, accf, q, rs, r7), "ahead", 1)
        got_od2 = swap_od(cod2)
        res = call(
            make_between(early), [inner, face, face] + ([geometry] if early else []),
            (m7, gm, a7, r7, ri, rt, ti, p0, r0) + ((tf, rtf) if early else (a0,)), "between", 2000)
        wp, e7, e0 = res[:3]
        if early:
            a0 = res[3]
        m0, cev2 = call(
            make_stage_face(0, 1.0 / s, False, early), [face, sent],
            (cod, got_od, e0, accf, q, rs, r0), "behind", 1)
        got_ev2 = swap_ev(cev2)
        scale = 1.0 / (s + 1)
        if n < pairs - 1:
            gi, q, acci, accf, wp, e0 = call(
                make_second_inner(scale, opening, closing),
                [inner, faces, inner, faces, inner, face],
                (m0, m7, p0, p7, accf, acci, wp, ri, rt, ti, a0, r0), "second", 3000)
            p0, cev = call(
                make_stage_face(0, scale, closing, False), [face, sent],
                (cod2, got_od2, e0, accf, q, rs, r0), "odd", 3000)
            p7, cod = call(
                make_stage_face(1, scale, closing, False), [face, sent],
                (cev2, got_ev2, e7, accf, q, rs, r7), "even", 1)
        else:
            out, accf, e0 = call(
                make_last_inner(scale), [(members,) + grid, faces, face],
                (slots, m0, m7, p0, p7, accf, acci, wp, rt, a0, r0), "last", 3000,
                hbm_out=(0,), scratch=[pltpu.VMEM(inner, f32), pltpu.SemaphoreType.DMA((2,))])
            near = call(
                make_finish_near(0, scale), [(2,) + tile],
                (slots, cod2, got_od2, e0, accf), "finish", 3000)
            out = call(
                make_finish_far(1, scale), [(members,) + grid],
                (slots, cev2, got_ev2, e7, accf, near, out), "finish", 1,
                hbm=(6,), hbm_out=(0,), alias={6: 0},
                scratch=[pltpu.VMEM((2,) + tile, f32), pltpu.SemaphoreType.DMA((2, 2))])
    return out.reshape(scalars.shape)


def solution(mesh):
    in_specs = (P("ens", None, "elem"), P(None, None, "elem"), P(None, "elem"), P("elem", None))
    out_specs = P("ens", None, "elem")
    return jax.shard_map(
        per_device, mesh=mesh, in_specs=in_specs, out_specs=out_specs, check_vma=False
    )
```
